256 devices in a mesh: row: 2 (over core), col: 128 (over z, y, x).
Axes of the slice: x: 4, y: 4, z: 8, core: 2. Of those that a mesh axis runs over, the one named last changes fastest.
Arguments:
- image_tokens: bfloat16 [64, 4096, 256], P('row', 'col'), may hold values from -6 to 6
- w_in: bfloat16 [256, 768], replicated, may hold values from -0.375 to 0.375
- conv_kernel: bfloat16 [3, 3, 768], replicated, may hold values from -2 to 2
- conv_bias: float32 [768], replicated, may hold values from -3 to 3
- long_filter: bfloat16 [64, 256], replicated, may hold values from -0.75 to 0.75
- skip_gain: float32 [256], replicated, may hold values from 0.5 to 1.5
- w_out: bfloat16 [256, 256], replicated, may hold values from -0.375 to 0.375
Outputs:
- layer_out: bfloat16 [64, 4096, 256], P('row', 'col')
The draws below stay inside these ranges and needn't reach their ends.
All inputs are finite; a program needn't handle non-finite values.
Results may differ from the reference program's by a relative error of at most 0.014.
Values may be sent and summed in bfloat16 or wider, within the bound.
A program may use at most 64 MiB of HBM per device.

```python
import jax
import jax.numpy as jnp
from jax import lax

C = 256
H = 64
W = 4096
N_ROW = 2


def shard_levels(own_key, shape, pieces, low, top_value):
    factor_of = 1.0
    for dim, blocks in pieces:
        steps = jax.random.uniform(jax.random.fold_in(jax.random.fold_in(own_key, 6), dim), (blocks,), jnp.float32, low / len(pieces), top_value / len(pieces))
        factor_of = factor_of * jnp.repeat(jnp.exp(steps), shape[dim] // blocks).reshape((-1,) + (1,) * (len(shape) - 1 - dim))
    return factor_of


def gaussian(rng, extent, spread, bound, split=(), dtype=jnp.bfloat16):
    array = jax.random.normal(rng, extent, jnp.float32) * spread
    if len(split) > 0:
        array = shard_levels(rng, extent, split, -0.22, 0.18) * array
    return jnp.clip(array, min=-bound, max=bound).astype(dtype)


def setup_inputs(seed: int = 0) -> dict:
    key_of = jax.random.split(jax.random.key(seed), 8)
    return {
        "image_tokens": gaussian(key_of[0], (H, W, C), 1.0, 6.0, ((0, 2), (1, 128))),
        "w_in": gaussian(key_of[1], (C, 3 * C), C ** -0.5, 0.375),
        "conv_kernel": gaussian(key_of[2], (3, 3, 3 * C), 9 ** -0.5, 2.0),
        "conv_bias": gaussian(key_of[3], (3 * C,), 0.5, 3.0, (), jnp.float32),
        "long_filter": gaussian(key_of[4], (H, C), H ** -0.5, 0.75),
        "skip_gain": jnp.clip(jax.random.uniform(key_of[5], (C,), jnp.float32, 0.5, 1.5), 0.5, 1.5),
        "w_out": gaussian(key_of[6], (C, C), C ** -0.5, 0.375),
    }


def depthwise(field, kernel, bias):
    height = field.shape[0]
    span = field.shape[1]
    padded = jnp.pad(field, ((1, 1), (1, 1), (0, 0)))
    total = jnp.zeros(field.shape, jnp.float32) + bias.astype(jnp.float32)
    for row_off in range(3):
        for col_off in range(3):
            window = padded[row_off:row_off + height, col_off:col_off + span, :].astype(jnp.float32)
            total = total + window * kernel[row_off, col_off].astype(jnp.float32)
    return total.astype(jnp.bfloat16)


def reference(image_tokens, w_in, conv_kernel, conv_bias, long_filter, skip_gain, w_out):
    group = 32 if C % 32 == 0 else C
    count = C // group
    flat = image_tokens.reshape(H * W, C)
    w_groups = jnp.transpose(w_in.reshape(C, 3, count, group), (2, 0, 1, 3)).reshape(count, C, 3 * group)
    k_groups = jnp.transpose(conv_kernel.reshape(3, 3, 3, count, group), (3, 0, 1, 2, 4)).reshape(count, 3, 3, 3 * group)
    b_groups = jnp.transpose(conv_bias.reshape(3, count, group), (1, 0, 2)).reshape(count, 3 * group)
    f_groups = jnp.transpose(long_filter.reshape(H, count, group), (1, 0, 2))
    s_groups = skip_gain.reshape(count, group)

    def one_group(pack):
        weight, kernel, bias, filt, gain = pack
        proj = jnp.dot(flat, weight, preferred_element_type=jnp.float32).astype(jnp.bfloat16)
        proj = proj.reshape(H, W, 3 * group)
        mixed = depthwise(proj, kernel, bias)
        query = mixed[:, :, :group].astype(jnp.float32)
        key = mixed[:, :, group:2 * group].astype(jnp.float32)
        value = mixed[:, :, 2 * group:].astype(jnp.float32)
        product = (key * value).astype(jnp.bfloat16)
        prod_wide = product.astype(jnp.float32)
        spectrum = jnp.fft.rfft(prod_wide, n=2 * H, axis=0)
        response = jnp.fft.rfft(filt.astype(jnp.float32), n=2 * H, axis=0)
        longconv = jnp.fft.irfft(spectrum * response[:, None, :], n=2 * H, axis=0)[:H]
        return (query * (longconv + gain * prod_wide)).astype(jnp.bfloat16)

    gated = lax.map(one_group, (w_groups, k_groups, b_groups, f_groups, s_groups))
    gated = jnp.transpose(gated, (1, 2, 0, 3)).reshape(N_ROW, (H // N_ROW) * W, C)

    def project(block):
        return jnp.dot(block, w_out, preferred_element_type=jnp.float32).astype(jnp.bfloat16)

    return lax.map(project, gated).reshape(H, W, C)
```

```python
import functools

import jax
import jax.numpy as jnp
from jax import lax
from jax.experimental import pallas as pl
from jax.experimental.pallas import tpu as pltpu
from jax.sharding import PartitionSpec as P


def extended(block, sides, width):
    for axis, dim in sides:
        count = lax.axis_size(axis)
        forward = [(i, i + 1) for i in range(count - 1)]
        backward = [(target, source) for source, target in forward]
        low = lax.ppermute(
            lax.slice_in_dim(block, block.shape[dim] - width, None, axis=dim), axis, forward
        )
        high = lax.ppermute(lax.slice_in_dim(block, 0, width, axis=dim), axis, backward)
        block = jnp.concatenate([low, block, high], axis=dim)
    return block


def depthwise(padded, kernel, bias, height, span):
    total = jnp.zeros((height, span, padded.shape[2]), jnp.float32) + bias
    for row_off in range(3):
        for col_off in range(3):
            window = padded[row_off : row_off + height, col_off : col_off + span, :].astype(
                jnp.float32
            )
            total = total + window * kernel[row_off, col_off].astype(jnp.float32)
    return total.astype(jnp.bfloat16)


def longconv_kernel(rows, span, prev_ref, own_ref, q_ref, filt_ref, gain_ref, wout_ref, out_ref,
                    ext_ref, fb_ref, qf_ref, gated_ref):
    count = rows * span
    width = own_ref.shape[1]
    ext_ref[0:count, :] = prev_ref[...].astype(jnp.float32)
    ext_ref[count : 2 * count, :] = own_ref[...].astype(jnp.float32)
    qf_ref[...] = q_ref[...].astype(jnp.float32)
    for lag in range(2 * rows):
        fb_ref[lag] = jnp.broadcast_to(filt_ref[lag : lag + 1, :].astype(jnp.float32), (8, width))
    lane_groups = width // 128

    def chunk(i, carry):
        lanes = pl.ds(pl.multiple_of((i % lane_groups) * 128, 128), 128)
        w0 = pl.multiple_of((i // lane_groups) * 8, 8)
        acc = [None] * rows
        for src in range(2 * rows):
            x = ext_ref[pl.ds(src * span + w0, 8), lanes]
            for a in range(max(0, src - rows), rows):
                term = fb_ref[rows + a - src, :, lanes] * x
                acc[a] = term if acc[a] is None else acc[a] + term
        gain = jnp.broadcast_to(gain_ref[:, lanes], (8, 128))
        for a in range(rows):
            own = ext_ref[pl.ds(count + a * span + w0, 8), lanes]
            q = qf_ref[pl.ds(a * span + w0, 8), lanes]
            gated_ref[pl.ds(a * span + w0, 8), lanes] = q * (acc[a] + gain * own)
        return carry

    lax.fori_loop(0, (span // 8) * lane_groups, chunk, 0)
    out_ref[...] = jnp.dot(
        gated_ref[...].astype(jnp.bfloat16), wout_ref[...], preferred_element_type=jnp.float32
    ).astype(out_ref.dtype)


def on_device(image_tokens, w_in, conv_kernel, conv_bias, long_filter, skip_gain, w_out):
    row_count, col_count, width = image_tokens.shape
    tokens = extended(image_tokens, (("row", 0), ("col", 1)), 1)
    projected = jnp.dot(
        tokens.reshape(-1, width), w_in, preferred_element_type=jnp.float32
    ).astype(jnp.bfloat16)
    projected = projected.reshape(row_count + 2, col_count + 2, 3 * width)
    mixed = depthwise(projected, conv_kernel, conv_bias, row_count, col_count)
    query = mixed[:, :, :width]
    key = mixed[:, :, width : 2 * width].astype(jnp.float32)
    value = mixed[:, :, 2 * width :].astype(jnp.float32)
    product = (key * value).astype(jnp.bfloat16)
    count = lax.axis_size("row")
    prev = lax.ppermute(product, "row", [(i, i + 1) for i in range(count - 1)])
    flat = row_count * col_count
    vmem = pl.BlockSpec(memory_space=pltpu.VMEM)
    out = pl.pallas_call(
        functools.partial(longconv_kernel, row_count, col_count),
        out_shape=jax.ShapeDtypeStruct((flat, width), jnp.bfloat16),
        in_specs=[vmem] * 6,
        out_specs=vmem,
        scratch_shapes=[
            pltpu.VMEM((2 * flat, width), jnp.float32),
            pltpu.VMEM((2 * row_count, 8, width), jnp.float32),
            pltpu.VMEM((flat, width), jnp.float32),
            pltpu.VMEM((flat, width), jnp.float32),
        ],
    )(
        prev.reshape(flat, width),
        product.reshape(flat, width),
        query.reshape(flat, width),
        long_filter,
        skip_gain.reshape(1, width),
        w_out,
    )
    return out.reshape(row_count, col_count, width)


def solution(mesh):
    in_specs = (P("row", "col", None), P(), P(), P(), P(), P(), P())
    out_specs = P("row", "col", None)
    return jax.shard_map(
        on_device, mesh=mesh, in_specs=in_specs, out_specs=out_specs, check_vma=False
    )
```

```python
import functools

import jax
import jax.numpy as jnp
from jax import lax
from jax.experimental import pallas as pl
from jax.experimental.pallas import tpu as pltpu
from jax.sharding import PartitionSpec as P


def extended(block, sides, width):
    for axis, dim in sides:
        count = lax.axis_size(axis)
        forward = [(i, i + 1) for i in range(count - 1)]
        backward = [(target, source) for source, target in forward]
        low = lax.ppermute(
            lax.slice_in_dim(block, block.shape[dim] - width, None, axis=dim), axis, forward
        )
        high = lax.ppermute(lax.slice_in_dim(block, 0, width, axis=dim), axis, backward)
        block = jnp.concatenate([low, block, high], axis=dim)
    return block


def depthwise(padded, kernel, bias, height, span):
    total = jnp.zeros((height, span, padded.shape[2]), jnp.float32) + bias
    for row_off in range(3):
        for col_off in range(3):
            window = padded[row_off : row_off + height, col_off : col_off + span, :].astype(
                jnp.float32
            )
            total = total + window * kernel[row_off, col_off].astype(jnp.float32)
    return total.astype(jnp.bfloat16)


def longconv_kernel(rows, span, prev_ref, own_ref, q_ref, filt_ref, gain_ref, wout_ref, out_ref,
                    ext_ref, fb_ref, qf_ref, gated_ref):
    count = rows * span
    width = own_ref.shape[1]
    ext_ref[0:count, :] = prev_ref[...].astype(jnp.float32)
    ext_ref[count : 2 * count, :] = own_ref[...].astype(jnp.float32)
    qf_ref[...] = q_ref[...].astype(jnp.float32)
    for lag in range(2 * rows):
        fb_ref[lag] = jnp.broadcast_to(filt_ref[lag : lag + 1, :].astype(jnp.float32), (8, width))
    lane_groups = width // 128

    def chunk(i, carry):
        lanes = pl.ds(pl.multiple_of((i % lane_groups) * 128, 128), 128)
        w0 = pl.multiple_of((i // lane_groups) * 8, 8)
        acc = [None] * rows
        for src in range(2 * rows):
            x = ext_ref[pl.ds(src * span + w0, 8), lanes]
            for a in range(max(0, src - rows), rows):
                term = fb_ref[rows + a - src, :, lanes] * x
                acc[a] = term if acc[a] is None else acc[a] + term
        gain = jnp.broadcast_to(gain_ref[:, lanes], (8, 128))
        for a in range(rows):
            own = ext_ref[pl.ds(count + a * span + w0, 8), lanes]
            q = qf_ref[pl.ds(a * span + w0, 8), lanes]
            gated_ref[pl.ds(a * span + w0, 8), lanes] = q * (acc[a] + gain * own)
        return carry

    lax.fori_loop(0, (span // 8) * lane_groups, chunk, 0)
    out_ref[...] = jnp.dot(
        gated_ref[...].astype(jnp.bfloat16), wout_ref[...], preferred_element_type=jnp.float32
    ).astype(out_ref.dtype)


def front_kernel(rows, span, pitch, send_ref, x_ref, w_ref, k_ref, b_ref, q_out, p_out,
                 halo, pext, kb, bb, hp, send_sem, recv_sem):
    width = x_ref.shape[2]
    wide = w_ref.shape[1]
    r = lax.axis_index("row")
    c = lax.axis_index("col")
    ncol = lax.axis_size("col")
    partner = 1 - r
    mesh_id = pl.DeviceIdType.MESH

    halo[...] = jnp.zeros_like(halo)
    barrier = pltpu.get_barrier_semaphore()
    right = lax.rem(c + 1, ncol)
    left = lax.rem(c + ncol - 1, ncol)
    peers = ((partner, c), (r, right), (r, left), (partner, right), (partner, left))
    for dev in peers:
        pl.semaphore_signal(barrier, 1, device_id=dev, device_id_type=mesh_id)
    pl.semaphore_wait(barrier, len(peers))

    out = [
        pltpu.make_async_remote_copy(send_ref.at[slot], halo.at[slot], send_sem.at[slot],
                                     recv_sem.at[slot], device_id=dev, device_id_type=mesh_id)
        for slot, dev in enumerate(peers)
    ]
    send_when = (None, c < ncol - 1, c > 0, c < ncol - 1, c > 0)
    recv_when = (None, c > 0, c < ncol - 1, c > 0, c < ncol - 1)

    def guarded(cond, fn):
        if cond is None:
            fn()
        else:
            pl.when(cond)(fn)

    for cp, cond in zip(out, send_when):
        guarded(cond, cp.start)

    for i in range(9):
        kb[i] = jnp.broadcast_to(k_ref[i : i + 1, :].astype(jnp.float32), (span, wide))
    bb[...] = jnp.broadcast_to(b_ref[...], (span, wide))
    proj = jnp.dot(x_ref[...].reshape(rows * span, width), w_ref[...],
                   preferred_element_type=jnp.float32)
    proj = proj.astype(jnp.bfloat16).astype(jnp.float32)
    for i in range(rows):
        pext[pl.ds((1 + i) * pitch + 8, span), :] = proj[i * span : (i + 1) * span]
    other_row = r * (rows + 1)
    pext[pl.ds(pl.multiple_of(other_row * pitch, 8), pitch), :] = jnp.zeros((pitch, wide),
                                                                            jnp.float32)

    for cp, cond in zip(out, send_when):
        guarded(cond, cp.wait_send)
    for cp, cond in zip(out, recv_when):
        guarded(cond, cp.wait_recv)

    hp[...] = jnp.dot(halo[...].reshape(5 * span, width), w_ref[...],
                      preferred_element_type=jnp.float32).astype(jnp.bfloat16).astype(jnp.float32)
    halo_row = partner * (rows + 1)
    base = pl.multiple_of(halo_row * pitch, 8)
    pext[pl.ds(base + 8, span), :] = hp[0:span, :]
    pext[pl.ds(base + 7, 1), :] = hp[3 * span : 3 * span + 1, :]
    pext[pl.ds(base + 8 + span, 1), :] = hp[4 * span : 4 * span + 1, :]
    for i in range(rows):
        pext[pl.ds((1 + i) * pitch + 7, 1), :] = hp[pl.ds(span + i, 1), :]
        pext[pl.ds((1 + i) * pitch + 8 + span, 1), :] = hp[pl.ds(2 * span + i, 1), :]

    def row_body(i, carry):
        res = []
        for grp in range(3):
            lanes = pl.ds(grp * width, width)
            acc = bb[:, lanes]
            for a in range(3):
                window = pext[pl.ds(pl.multiple_of((i + a) * pitch, 8), pitch), lanes]
                for b in range(3):
                    acc = acc + window[7 + b : 7 + b + span] * kb[a * 3 + b, :, lanes]
            res.append(acc.astype(jnp.bfloat16))
        dst = pl.ds(pl.multiple_of(i * span, 16), span)
        q_out[dst, :] = res[0]
        p_out[dst, :] = (res[1].astype(jnp.float32) * res[2].astype(jnp.float32)).astype(
            jnp.bfloat16)
        return carry

    lax.fori_loop(0, rows, row_body, 0)


def on_device(image_tokens, w_in, conv_kernel, conv_bias, long_filter, skip_gain, w_out):
    row_count, col_count, width = image_tokens.shape
    pitch = 48
    flat = row_count * col_count
    wide = w_in.shape[1]
    vmem = pl.BlockSpec(memory_space=pltpu.VMEM)
    edge = lax.dynamic_index_in_dim(
        image_tokens, (1 - lax.axis_index("row")) * (row_count - 1), 0, keepdims=False)
    corner_shape = (col_count, width)
    send = jnp.stack([
        edge,
        image_tokens[:, col_count - 1],
        image_tokens[:, 0],
        jnp.broadcast_to(edge[col_count - 1], corner_shape),
        jnp.broadcast_to(edge[0], corner_shape),
    ])
    query, product = pl.pallas_call(
        functools.partial(front_kernel, row_count, col_count, pitch),
        out_shape=(
            jax.ShapeDtypeStruct((flat, width), jnp.bfloat16),
            jax.ShapeDtypeStruct((flat, width), jnp.bfloat16),
        ),
        in_specs=[vmem] * 5,
        out_specs=(vmem, vmem),
        scratch_shapes=[
            pltpu.VMEM((5, col_count, width), jnp.bfloat16),
            pltpu.VMEM(((row_count + 2) * pitch, wide), jnp.float32),
            pltpu.VMEM((9, col_count, wide), jnp.float32),
            pltpu.VMEM((col_count, wide), jnp.float32),
            pltpu.VMEM((5 * col_count, wide), jnp.float32),
            pltpu.SemaphoreType.DMA((5,)),
            pltpu.SemaphoreType.DMA((5,)),
        ],
        compiler_params=pltpu.CompilerParams(
            collective_id=0, has_side_effects=True, vmem_limit_bytes=48 * 1024 * 1024
        ),
    )(
        send,
        image_tokens,
        w_in,
        conv_kernel.reshape(9, wide),
        conv_bias.reshape(1, wide),
    )
    count = lax.axis_size("row")
    prev = lax.ppermute(product, "row", [(i, i + 1) for i in range(count - 1)])
    out = pl.pallas_call(
        functools.partial(longconv_kernel, row_count, col_count),
        out_shape=jax.ShapeDtypeStruct((flat, width), jnp.bfloat16),
        in_specs=[vmem] * 6,
        out_specs=vmem,
        scratch_shapes=[
            pltpu.VMEM((2 * flat, width), jnp.float32),
            pltpu.VMEM((2 * row_count, 8, width), jnp.float32),
            pltpu.VMEM((flat, width), jnp.float32),
            pltpu.VMEM((flat, width), jnp.float32),
        ],
    )(
        prev,
        product,
        query,
        long_filter,
        skip_gain.reshape(1, width),
        w_out,
    )
    return out.reshape(row_count, col_count, width)


def solution(mesh):
    in_specs = (P("row", "col", None), P(), P(), P(), P(), P(), P())
    out_specs = P("row", "col", None)
    return jax.shard_map(
        on_device, mesh=mesh, in_specs=in_specs, out_specs=out_specs, check_vma=False
    )
```

```python
import functools

import jax
import jax.numpy as jnp
from jax import lax
from jax.experimental import pallas as pl
from jax.experimental.pallas import tpu as pltpu
from jax.sharding import PartitionSpec as P


def extended(block, sides, width):
    for axis, dim in sides:
        count = lax.axis_size(axis)
        forward = [(i, i + 1) for i in range(count - 1)]
        backward = [(target, source) for source, target in forward]
        low = lax.ppermute(
            lax.slice_in_dim(block, block.shape[dim] - width, None, axis=dim), axis, forward
        )
        high = lax.ppermute(lax.slice_in_dim(block, 0, width, axis=dim), axis, backward)
        block = jnp.concatenate([low, block, high], axis=dim)
    return block


def depthwise(padded, kernel, bias, height, span):
    total = jnp.zeros((height, span, padded.shape[2]), jnp.float32) + bias
    for row_off in range(3):
        for col_off in range(3):
            window = padded[row_off : row_off + height, col_off : col_off + span, :].astype(
                jnp.float32
            )
            total = total + window * kernel[row_off, col_off].astype(jnp.float32)
    return total.astype(jnp.bfloat16)


def longconv_kernel(rows, span, prev_ref, own_ref, q_ref, filt_ref, gain_ref, wout_ref, out_ref,
                    ext_ref, fb_ref, qf_ref, gated_ref):
    count = rows * span
    width = own_ref.shape[1]
    ext_ref[0:count, :] = prev_ref[...].astype(jnp.float32)
    ext_ref[count : 2 * count, :] = own_ref[...].astype(jnp.float32)
    qf_ref[...] = q_ref[...].astype(jnp.float32)
    for lag in range(2 * rows):
        fb_ref[lag] = jnp.broadcast_to(filt_ref[lag : lag + 1, :].astype(jnp.float32), (8, width))
    lane_groups = width // 128

    def chunk(i, carry):
        lanes = pl.ds(pl.multiple_of((i % lane_groups) * 128, 128), 128)
        w0 = pl.multiple_of((i // lane_groups) * 8, 8)
        acc = [None] * rows
        for src in range(2 * rows):
            x = ext_ref[pl.ds(src * span + w0, 8), lanes]
            for a in range(max(0, src - rows), rows):
                term = fb_ref[rows + a - src, :, lanes] * x
                acc[a] = term if acc[a] is None else acc[a] + term
        gain = jnp.broadcast_to(gain_ref[:, lanes], (8, 128))
        for a in range(rows):
            own = ext_ref[pl.ds(count + a * span + w0, 8), lanes]
            q = qf_ref[pl.ds(a * span + w0, 8), lanes]
            gated_ref[pl.ds(a * span + w0, 8), lanes] = q * (acc[a] + gain * own)
        return carry

    lax.fori_loop(0, (span // 8) * lane_groups, chunk, 0)
    out_ref[...] = jnp.dot(
        gated_ref[...].astype(jnp.bfloat16), wout_ref[...], preferred_element_type=jnp.float32
    ).astype(out_ref.dtype)


def front_kernel(rows, span, pitch, send_ref, x_ref, w_ref, k_ref, b_ref, q_out, p_out,
                 halo, pext, shifted, kb, bb, hp, send_sem, recv_sem):
    width = x_ref.shape[2]
    wide = w_ref.shape[1]
    r = lax.axis_index("row")
    c = lax.axis_index("col")
    ncol = lax.axis_size("col")
    partner = 1 - r
    mesh_id = pl.DeviceIdType.MESH

    halo[...] = jnp.zeros_like(halo)
    barrier = pltpu.get_barrier_semaphore()
    right = lax.rem(c + 1, ncol)
    left = lax.rem(c + ncol - 1, ncol)
    peers = ((partner, c), (r, right), (r, left), (partner, right), (partner, left))
    for dev in peers:
        pl.semaphore_signal(barrier, 1, device_id=dev, device_id_type=mesh_id)
    pl.semaphore_wait(barrier, len(peers))

    out = [
        pltpu.make_async_remote_copy(send_ref.at[slot], halo.at[slot], send_sem.at[slot],
                                     recv_sem.at[slot], device_id=dev, device_id_type=mesh_id)
        for slot, dev in enumerate(peers)
    ]
    send_when = (None, c < ncol - 1, c > 0, c < ncol - 1, c > 0)
    recv_when = (None, c > 0, c < ncol - 1, c > 0, c < ncol - 1)

    def guarded(cond, fn):
        if cond is None:
            fn()
        else:
            pl.when(cond)(fn)

    for cp, cond in zip(out, send_when):
        guarded(cond, cp.start)

    for i in range(9):
        kb[i] = jnp.broadcast_to(k_ref[i : i + 1, :].astype(jnp.float32), (span, wide))
    bb[...] = jnp.broadcast_to(b_ref[...], (span, wide))
    proj = jnp.dot(x_ref[...].reshape(rows * span, width), w_ref[...],
                   preferred_element_type=jnp.float32)
    proj = proj.astype(jnp.bfloat16).astype(jnp.float32)
    for i in range(rows):
        pext[pl.ds((1 + i) * pitch + 8, span), :] = proj[i * span : (i + 1) * span]
    other_row = r * (rows + 1)
    pext[pl.ds(pl.multiple_of(other_row * pitch, 8), pitch), :] = jnp.zeros((pitch, wide),
                                                                            jnp.float32)

    for cp, cond in zip(out, send_when):
        guarded(cond, cp.wait_send)
    for cp, cond in zip(out, recv_when):
        guarded(cond, cp.wait_recv)

    hp[...] = jnp.dot(halo[...].reshape(5 * span, width), w_ref[...],
                      preferred_element_type=jnp.float32).astype(jnp.bfloat16).astype(jnp.float32)
    halo_row = partner * (rows + 1)
    base = pl.multiple_of(halo_row * pitch, 8)
    pext[pl.ds(base + 8, span), :] = hp[0:span, :]
    pext[pl.ds(base + 7, 1), :] = hp[3 * span : 3 * span + 1, :]
    pext[pl.ds(base + 8 + span, 1), :] = hp[4 * span : 4 * span + 1, :]
    for i in range(rows):
        pext[pl.ds((1 + i) * pitch + 7, 1), :] = hp[pl.ds(span + i, 1), :]
        pext[pl.ds((1 + i) * pitch + 8 + span, 1), :] = hp[pl.ds(2 * span + i, 1), :]

    def shift_body(i, carry):
        window = pext[pl.ds(pl.multiple_of(i * pitch, 8), pitch), :]
        dst = pl.ds(pl.multiple_of(i * span, 8), span)
        shifted[0, dst, :] = window[7 : 7 + span]
        shifted[1, dst, :] = window[8 : 8 + span]
        shifted[2, dst, :] = window[9 : 9 + span]
        return carry

    lax.fori_loop(0, rows + 2, shift_body, 0)

    def row_body(i, carry):
        res = []
        for grp in range(3):
            lanes = pl.ds(grp * width, width)
            acc = bb[:, lanes]
            for a in range(3):
                src = pl.ds(pl.multiple_of((i + a) * span, 8), span)
                for b in range(3):
                    acc = acc + shifted[b, src, lanes] * kb[a * 3 + b, :, lanes]
            res.append(acc.astype(jnp.bfloat16))
        dst = pl.ds(pl.multiple_of(i * span, 16), span)
        q_out[dst, :] = res[0]
        p_out[dst, :] = (res[1].astype(jnp.float32) * res[2].astype(jnp.float32)).astype(
            jnp.bfloat16)
        return carry

    lax.fori_loop(0, rows, row_body, 0)


def on_device(image_tokens, w_in, conv_kernel, conv_bias, long_filter, skip_gain, w_out):
    row_count, col_count, width = image_tokens.shape
    pitch = 48
    flat = row_count * col_count
    wide = w_in.shape[1]
    vmem = pl.BlockSpec(memory_space=pltpu.VMEM)
    edge = lax.dynamic_index_in_dim(
        image_tokens, (1 - lax.axis_index("row")) * (row_count - 1), 0, keepdims=False)
    corner_shape = (col_count, width)
    send = jnp.stack([
        edge,
        image_tokens[:, col_count - 1],
        image_tokens[:, 0],
        jnp.broadcast_to(edge[col_count - 1], corner_shape),
        jnp.broadcast_to(edge[0], corner_shape),
    ])
    query, product = pl.pallas_call(
        functools.partial(front_kernel, row_count, col_count, pitch),
        out_shape=(
            jax.ShapeDtypeStruct((flat, width), jnp.bfloat16),
            jax.ShapeDtypeStruct((flat, width), jnp.bfloat16),
        ),
        in_specs=[vmem] * 5,
        out_specs=(vmem, vmem),
        scratch_shapes=[
            pltpu.VMEM((5, col_count, width), jnp.bfloat16),
            pltpu.VMEM(((row_count + 2) * pitch, wide), jnp.float32),
            pltpu.VMEM((3, (row_count + 2) * col_count, wide), jnp.float32),
            pltpu.VMEM((9, col_count, wide), jnp.float32),
            pltpu.VMEM((col_count, wide), jnp.float32),
            pltpu.VMEM((5 * col_count, wide), jnp.float32),
            pltpu.SemaphoreType.DMA((5,)),
            pltpu.SemaphoreType.DMA((5,)),
        ],
        compiler_params=pltpu.CompilerParams(
            collective_id=0, has_side_effects=True, vmem_limit_bytes=48 * 1024 * 1024
        ),
    )(
        send,
        image_tokens,
        w_in,
        conv_kernel.reshape(9, wide),
        conv_bias.reshape(1, wide),
    )
    count = lax.axis_size("row")
    prev = lax.ppermute(product, "row", [(i, i + 1) for i in range(count - 1)])
    out = pl.pallas_call(
        functools.partial(longconv_kernel, row_count, col_count),
        out_shape=jax.ShapeDtypeStruct((flat, width), jnp.bfloat16),
        in_specs=[vmem] * 6,
        out_specs=vmem,
        scratch_shapes=[
            pltpu.VMEM((2 * flat, width), jnp.float32),
            pltpu.VMEM((2 * row_count, 8, width), jnp.float32),
            pltpu.VMEM((flat, width), jnp.float32),
            pltpu.VMEM((flat, width), jnp.float32),
        ],
    )(
        prev,
        product,
        query,
        long_filter,
        skip_gain.reshape(1, width),
        w_out,
    )
    return out.reshape(row_count, col_count, width)


def solution(mesh):
    in_specs = (P("row", "col", None), P(), P(), P(), P(), P(), P())
    out_specs = P("row", "col", None)
    return jax.shard_map(
        on_device, mesh=mesh, in_specs=in_specs, out_specs=out_specs, check_vma=False
    )
```

```python
import functools

import jax
import jax.numpy as jnp
from jax import lax
from jax.experimental import pallas as pl
from jax.experimental.pallas import tpu as pltpu
from jax.sharding import PartitionSpec as P


def layer_kernel(rows, span, pitch, x_ref, w_ref, k_ref, b_ref, filt_ref, gain_ref, wout_ref,
                 out_ref, pext, shifted, kb, bb, send_col, recv_col, recv_row, own_b, prev_b,
                 ext, fb, qf, gated, send_sem, recv_sem):
    width = out_ref.shape[1]
    wide = w_ref.shape[1]
    count = rows * span
    r = lax.axis_index("row")
    c = lax.axis_index("col")
    ncol = lax.axis_size("col")
    partner = 1 - r
    edge = partner * (rows - 1)
    mesh_id = pl.DeviceIdType.MESH
    right = lax.rem(c + 1, ncol)
    left = lax.rem(c + ncol - 1, ncol)
    peers = ((r, right), (r, left), (partner, right), (partner, left), (partner, c), (partner, c))

    recv_col[...] = jnp.zeros_like(recv_col)
    barrier = pltpu.get_barrier_semaphore()
    for dev in peers[:5]:
        pl.semaphore_signal(barrier, 1, device_id=dev, device_id_type=mesh_id)

    for i in range(9):
        kb[i] = jnp.broadcast_to(k_ref[i : i + 1, :].astype(jnp.float32), (span, wide))
    bb[...] = jnp.broadcast_to(b_ref[...], (span, wide))
    proj = jnp.dot(x_ref[...], w_ref[...], preferred_element_type=jnp.float32)
    proj = proj.astype(jnp.bfloat16).astype(jnp.float32)
    for i in range(rows):
        pext[pl.ds((1 + i) * pitch + 8, span), :] = proj[i * span : (i + 1) * span]
    other_row = r * (rows + 1)
    pext[pl.ds(pl.multiple_of(other_row * pitch, 8), pitch), :] = jnp.zeros((pitch, wide),
                                                                            jnp.float32)
    for i in range(rows):
        send_col[0, i : i + 1, :] = pext[pl.ds((1 + i) * pitch + 8 + span - 1, 1), :]
        send_col[1, i : i + 1, :] = pext[pl.ds((1 + i) * pitch + 8, 1), :]
    edge_base = pl.multiple_of((1 + edge) * pitch, 8)
    send_col[2, 0:8, :] = jnp.broadcast_to(pext[pl.ds(edge_base + 8 + span - 1, 1), :], (8, wide))
    send_col[3, 0:8, :] = jnp.broadcast_to(pext[pl.ds(edge_base + 8, 1), :], (8, wide))

    pl.semaphore_wait(barrier, 5)
    copies = [
        pltpu.make_async_remote_copy(send_col.at[slot], recv_col.at[slot], send_sem.at[slot],
                                     recv_sem.at[slot], device_id=peers[slot],
                                     device_id_type=mesh_id)
        for slot in range(4)
    ]
    copies.append(pltpu.make_async_remote_copy(
        pext.at[pl.ds(edge_base + 8, span)], recv_row, send_sem.at[4], recv_sem.at[4],
        device_id=peers[4], device_id_type=mesh_id))
    product_copy = pltpu.make_async_remote_copy(
        own_b, prev_b, send_sem.at[5], recv_sem.at[5], device_id=peers[5],
        device_id_type=mesh_id)
    send_when = (c < ncol - 1, c > 0, c < ncol - 1, c > 0, None)
    recv_when = (c > 0, c < ncol - 1, c > 0, c < ncol - 1, None)

    def guarded(cond, fn):
        if cond is None:
            fn()
        else:
            pl.when(cond)(fn)

    for cp, cond in zip(copies, send_when):
        guarded(cond, cp.start)
    for lag in range(2 * rows):
        fb[lag] = jnp.broadcast_to(filt_ref[lag : lag + 1, :].astype(jnp.float32), (8, width))
    for cp, cond in zip(copies, send_when):
        guarded(cond, cp.wait_send)
    for cp, cond in zip(copies, recv_when):
        guarded(cond, cp.wait_recv)

    halo_base = pl.multiple_of(partner * (rows + 1) * pitch, 8)
    pext[pl.ds(halo_base + 8, span), :] = recv_row[...]
    for i in range(rows):
        pext[pl.ds((1 + i) * pitch + 7, 1), :] = recv_col[0, i : i + 1, :]
        pext[pl.ds((1 + i) * pitch + 8 + span, 1), :] = recv_col[1, i : i + 1, :]
    pext[pl.ds(halo_base + 7, 1), :] = recv_col[2, 0:1, :]
    pext[pl.ds(halo_base + 8 + span, 1), :] = recv_col[3, 0:1, :]

    def shift_body(i, carry):
        window = pext[pl.ds(pl.multiple_of(i * pitch, 8), pitch), :]
        dst = pl.ds(pl.multiple_of(i * span, 8), span)
        shifted[0, dst, :] = window[7 : 7 + span]
        shifted[1, dst, :] = window[8 : 8 + span]
        shifted[2, dst, :] = window[9 : 9 + span]
        return carry

    lax.fori_loop(0, rows + 2, shift_body, 0)

    def row_body(i, carry):
        res = []
        for grp in range(3):
            lanes = pl.ds(grp * width, width)
            acc = bb[:, lanes]
            for a in range(3):
                src = pl.ds(pl.multiple_of((i + a) * span, 8), span)
                for b in range(3):
                    acc = acc + shifted[b, src, lanes] * kb[a * 3 + b, :, lanes]
            res.append(acc.astype(jnp.bfloat16).astype(jnp.float32))
        dst = pl.ds(pl.multiple_of(i * span, 16), span)
        qf[dst, :] = res[0]
        prod = (res[1] * res[2]).astype(jnp.bfloat16)
        own_b[dst, :] = prod
        ext[pl.ds(pl.multiple_of(count + i * span, 16), span), :] = prod.astype(jnp.float32)
        return carry

    lax.fori_loop(0, rows, row_body, 0)

    @pl.when(r == 0)
    def _():
        product_copy.start()

    lane_groups = width // 128

    def own_pass(i, carry):
        lanes = pl.ds(pl.multiple_of((i % lane_groups) * 128, 128), 128)
        w0 = pl.multiple_of((i // lane_groups) * 8, 8)
        acc = [None] * rows
        for src in range(rows, 2 * rows):
            x = ext[pl.ds(src * span + w0, 8), lanes]
            for a in range(src - rows, rows):
                term = fb[rows + a - src, :, lanes] * x
                acc[a] = term if acc[a] is None else acc[a] + term
        for a in range(rows):
            gated[pl.ds(a * span + w0, 8), lanes] = acc[a]
        return carry

    lax.fori_loop(0, (span // 8) * lane_groups, own_pass, 0)

    @pl.when(r == 0)
    def _():
        product_copy.wait_send()
        ext[0:count, :] = jnp.zeros((count, width), jnp.float32)

    @pl.when(r == 1)
    def _():
        product_copy.wait_recv()
        ext[0:count, :] = prev_b[...].astype(jnp.float32)

    def prev_pass(i, carry):
        lanes = pl.ds(pl.multiple_of((i % lane_groups) * 128, 128), 128)
        w0 = pl.multiple_of((i // lane_groups) * 8, 8)
        acc = [gated[pl.ds(a * span + w0, 8), lanes] for a in range(rows)]
        for src in range(rows):
            x = ext[pl.ds(src * span + w0, 8), lanes]
            for a in range(rows):
                acc[a] = acc[a] + fb[rows + a - src, :, lanes] * x
        gain = jnp.broadcast_to(gain_ref[:, lanes], (8, 128))
        for a in range(rows):
            own = ext[pl.ds(count + a * span + w0, 8), lanes]
            q = qf[pl.ds(a * span + w0, 8), lanes]
            gated[pl.ds(a * span + w0, 8), lanes] = q * (acc[a] + gain * own)
        return carry

    lax.fori_loop(0, (span // 8) * lane_groups, prev_pass, 0)
    out_ref[...] = jnp.dot(
        gated[...].astype(jnp.bfloat16), wout_ref[...], preferred_element_type=jnp.float32
    ).astype(out_ref.dtype)


def on_device(image_tokens, w_in, conv_kernel, conv_bias, long_filter, skip_gain, w_out):
    row_count, col_count, width = image_tokens.shape
    pitch = 48
    flat = row_count * col_count
    wide = w_in.shape[1]
    vmem = pl.BlockSpec(memory_space=pltpu.VMEM)
    out = pl.pallas_call(
        functools.partial(layer_kernel, row_count, col_count, pitch),
        out_shape=jax.ShapeDtypeStruct((flat, width), jnp.bfloat16),
        in_specs=[vmem] * 7,
        out_specs=vmem,
        scratch_shapes=[
            pltpu.VMEM(((row_count + 2) * pitch, wide), jnp.float32),
            pltpu.VMEM((3, (row_count + 2) * col_count, wide), jnp.float32),
            pltpu.VMEM((9, col_count, wide), jnp.float32),
            pltpu.VMEM((col_count, wide), jnp.float32),
            pltpu.VMEM((4, row_count, wide), jnp.float32),
            pltpu.VMEM((4, row_count, wide), jnp.float32),
            pltpu.VMEM((col_count, wide), jnp.float32),
            pltpu.VMEM((flat, width), jnp.bfloat16),
            pltpu.VMEM((flat, width), jnp.bfloat16),
            pltpu.VMEM((2 * flat, width), jnp.float32),
            pltpu.VMEM((2 * row_count, 8, width), jnp.float32),
            pltpu.VMEM((flat, width), jnp.float32),
            pltpu.VMEM((flat, width), jnp.float32),
            pltpu.SemaphoreType.DMA((6,)),
            pltpu.SemaphoreType.DMA((6,)),
        ],
        compiler_params=pltpu.CompilerParams(
            collective_id=0, has_side_effects=True, vmem_limit_bytes=48 * 1024 * 1024
        ),
    )(
        image_tokens.reshape(flat, width),
        w_in,
        conv_kernel.reshape(9, wide),
        conv_bias.reshape(1, wide),
        long_filter,
        skip_gain.reshape(1, width),
        w_out,
    )
    return out.reshape(row_count, col_count, width)


def solution(mesh):
    in_specs = (P("row", "col", None), P(), P(), P(), P(), P(), P())
    out_specs = P("row", "col", None)
    return jax.shard_map(
        on_device, mesh=mesh, in_specs=in_specs, out_specs=out_specs, check_vma=False
    )
```

```python
import functools

import jax
import jax.numpy as jnp
from jax import lax
from jax.experimental import pallas as pl
from jax.experimental.pallas import tpu as pltpu
from jax.sharding import PartitionSpec as P


def layer_kernel(rows, span, pitch, x_ref, w_ref, k_ref, b_ref, filt_ref, gain_ref, wout_ref,
                 out_ref, pext, shifted, kb, bb, send_col, recv_col, recv_row, own_b, prev_b,
                 ext, fb, qf, gated, send_sem, recv_sem):
    width = out_ref.shape[1]
    wide = w_ref.shape[1]
    count = rows * span
    r = lax.axis_index("row")
    c = lax.axis_index("col")
    ncol = lax.axis_size("col")
    partner = 1 - r
    edge = partner * (rows - 1)
    mesh_id = pl.DeviceIdType.MESH
    right = lax.rem(c + 1, ncol)
    left = lax.rem(c + ncol - 1, ncol)
    peers = ((r, right), (r, left), (partner, right), (partner, left), (partner, c), (partner, c))

    recv_col[...] = jnp.zeros_like(recv_col)
    barrier = pltpu.get_barrier_semaphore()
    conds = (c < ncol - 1, c > 0, c < ncol - 1, c > 0)
    for dev, cond in zip(peers[:4], conds):
        @pl.when(cond)
        def _():
            pl.semaphore_signal(barrier, 1, device_id=dev, device_id_type=mesh_id)
    pl.semaphore_signal(barrier, 1, device_id=peers[4], device_id_type=mesh_id)
    has_left = (c + ncol - 1) // ncol
    has_right = (2 * ncol - 3 - c) // (ncol - 1)

    for i in range(9):
        kb[i] = jnp.broadcast_to(k_ref[i : i + 1, :].astype(jnp.float32), (span, wide))
    bb[...] = jnp.broadcast_to(b_ref[...], (span, wide))
    proj = jnp.dot(x_ref[...], w_ref[...], preferred_element_type=jnp.float32)
    proj = proj.astype(jnp.bfloat16).astype(jnp.float32)
    for i in range(rows):
        pext[pl.ds((1 + i) * pitch + 8, span), :] = proj[i * span : (i + 1) * span]
    other_row = r * (rows + 1)
    pext[pl.ds(pl.multiple_of(other_row * pitch, 8), pitch), :] = jnp.zeros((pitch, wide),
                                                                            jnp.float32)
    for i in range(rows):
        send_col[0, i : i + 1, :] = pext[pl.ds((1 + i) * pitch + 8 + span - 1, 1), :]
        send_col[1, i : i + 1, :] = pext[pl.ds((1 + i) * pitch + 8, 1), :]
    edge_base = pl.multiple_of((1 + edge) * pitch, 8)
    send_col[2, 0:8, :] = jnp.broadcast_to(pext[pl.ds(edge_base + 8 + span - 1, 1), :], (8, wide))
    send_col[3, 0:8, :] = jnp.broadcast_to(pext[pl.ds(edge_base + 8, 1), :], (8, wide))

    pl.semaphore_wait(barrier, 1 + 2 * has_left + 2 * has_right)
    copies = [
        pltpu.make_async_remote_copy(send_col.at[slot], recv_col.at[slot], send_sem.at[slot],
                                     recv_sem.at[slot], device_id=peers[slot],
                                     device_id_type=mesh_id)
        for slot in range(4)
    ]
    copies.append(pltpu.make_async_remote_copy(
        pext.at[pl.ds(edge_base + 8, span)], recv_row, send_sem.at[4], recv_sem.at[4],
        device_id=peers[4], device_id_type=mesh_id))
    product_copy = pltpu.make_async_remote_copy(
        own_b, prev_b, send_sem.at[5], recv_sem.at[5], device_id=peers[5],
        device_id_type=mesh_id)
    send_when = (c < ncol - 1, c > 0, c < ncol - 1, c > 0, None)
    recv_when = (c > 0, c < ncol - 1, c > 0, c < ncol - 1, None)

    def guarded(cond, fn):
        if cond is None:
            fn()
        else:
            pl.when(cond)(fn)

    for cp, cond in zip(copies, send_when):
        guarded(cond, cp.start)
    for lag in range(2 * rows):
        fb[lag] = jnp.broadcast_to(filt_ref[lag : lag + 1, :].astype(jnp.float32), (8, width))
    for cp, cond in zip(copies, send_when):
        guarded(cond, cp.wait_send)
    for cp, cond in zip(copies, recv_when):
        guarded(cond, cp.wait_recv)

    halo_base = pl.multiple_of(partner * (rows + 1) * pitch, 8)
    pext[pl.ds(halo_base + 8, span), :] = recv_row[...]
    for i in range(rows):
        pext[pl.ds((1 + i) * pitch + 7, 1), :] = recv_col[0, i : i + 1, :]
        pext[pl.ds((1 + i) * pitch + 8 + span, 1), :] = recv_col[1, i : i + 1, :]
    pext[pl.ds(halo_base + 7, 1), :] = recv_col[2, 0:1, :]
    pext[pl.ds(halo_base + 8 + span, 1), :] = recv_col[3, 0:1, :]

    def shift_body(i, carry):
        window = pext[pl.ds(pl.multiple_of(i * pitch, 8), pitch), :]
        dst = pl.ds(pl.multiple_of(i * span, 8), span)
        shifted[0, dst, :] = window[7 : 7 + span]
        shifted[1, dst, :] = window[8 : 8 + span]
        shifted[2, dst, :] = window[9 : 9 + span]
        return carry

    lax.fori_loop(0, rows + 2, shift_body, 0)

    def row_body(i, carry):
        res = []
        for grp in range(3):
            lanes = pl.ds(grp * width, width)
            acc = bb[:, lanes]
            for a in range(3):
                src = pl.ds(pl.multiple_of((i + a) * span, 8), span)
                for b in range(3):
                    acc = acc + shifted[b, src, lanes] * kb[a * 3 + b, :, lanes]
            res.append(acc.astype(jnp.bfloat16).astype(jnp.float32))
        dst = pl.ds(pl.multiple_of(i * span, 16), span)
        qf[dst, :] = res[0]
        prod = (res[1] * res[2]).astype(jnp.bfloat16)
        own_b[dst, :] = prod
        ext[pl.ds(pl.multiple_of(count + i * span, 16), span), :] = prod.astype(jnp.float32)
        return carry

    lax.fori_loop(0, rows, row_body, 0)

    @pl.when(r == 0)
    def _():
        product_copy.start()

    lane_groups = width // 128

    def own_pass(i, carry):
        lanes = pl.ds(pl.multiple_of((i % lane_groups) * 128, 128), 128)
        w0 = pl.multiple_of((i // lane_groups) * 8, 8)
        acc = [None] * rows
        for src in range(rows, 2 * rows):
            x = ext[pl.ds(src * span + w0, 8), lanes]
            for a in range(src - rows, rows):
                term = fb[rows + a - src, :, lanes] * x
                acc[a] = term if acc[a] is None else acc[a] + term
        for a in range(rows):
            gated[pl.ds(a * span + w0, 8), lanes] = acc[a]
        return carry

    lax.fori_loop(0, (span // 8) * lane_groups, own_pass, 0)

    @pl.when(r == 0)
    def _():
        product_copy.wait_send()
        ext[0:count, :] = jnp.zeros((count, width), jnp.float32)

    @pl.when(r == 1)
    def _():
        product_copy.wait_recv()
        ext[0:count, :] = prev_b[...].astype(jnp.float32)

    def prev_pass(i, carry):
        lanes = pl.ds(pl.multiple_of((i % lane_groups) * 128, 128), 128)
        w0 = pl.multiple_of((i // lane_groups) * 8, 8)
        acc = [gated[pl.ds(a * span + w0, 8), lanes] for a in range(rows)]
        for src in range(rows):
            x = ext[pl.ds(src * span + w0, 8), lanes]
            for a in range(rows):
                acc[a] = acc[a] + fb[rows + a - src, :, lanes] * x
        gain = jnp.broadcast_to(gain_ref[:, lanes], (8, 128))
        for a in range(rows):
            own = ext[pl.ds(count + a * span + w0, 8), lanes]
            q = qf[pl.ds(a * span + w0, 8), lanes]
            gated[pl.ds(a * span + w0, 8), lanes] = q * (acc[a] + gain * own)
        return carry

    lax.fori_loop(0, (span // 8) * lane_groups, prev_pass, 0)
    out_ref[...] = jnp.dot(
        gated[...].astype(jnp.bfloat16), wout_ref[...], preferred_element_type=jnp.float32
    ).astype(out_ref.dtype)


def on_device(image_tokens, w_in, conv_kernel, conv_bias, long_filter, skip_gain, w_out):
    row_count, col_count, width = image_tokens.shape
    pitch = 48
    flat = row_count * col_count
    wide = w_in.shape[1]
    vmem = pl.BlockSpec(memory_space=pltpu.VMEM)
    out = pl.pallas_call(
        functools.partial(layer_kernel, row_count, col_count, pitch),
        out_shape=jax.ShapeDtypeStruct((flat, width), jnp.bfloat16),
        in_specs=[vmem] * 7,
        out_specs=vmem,
        scratch_shapes=[
            pltpu.VMEM(((row_count + 2) * pitch, wide), jnp.float32),
            pltpu.VMEM((3, (row_count + 2) * col_count, wide), jnp.float32),
            pltpu.VMEM((9, col_count, wide), jnp.float32),
            pltpu.VMEM((col_count, wide), jnp.float32),
            pltpu.VMEM((4, row_count, wide), jnp.float32),
            pltpu.VMEM((4, row_count, wide), jnp.float32),
            pltpu.VMEM((col_count, wide), jnp.float32),
            pltpu.VMEM((flat, width), jnp.bfloat16),
            pltpu.VMEM((flat, width), jnp.bfloat16),
            pltpu.VMEM((2 * flat, width), jnp.float32),
            pltpu.VMEM((2 * row_count, 8, width), jnp.float32),
            pltpu.VMEM((flat, width), jnp.float32),
            pltpu.VMEM((flat, width), jnp.float32),
            pltpu.SemaphoreType.DMA((6,)),
            pltpu.SemaphoreType.DMA((6,)),
        ],
        compiler_params=pltpu.CompilerParams(
            collective_id=0, has_side_effects=True, vmem_limit_bytes=48 * 1024 * 1024
        ),
    )(
        image_tokens.reshape(flat, width),
        w_in,
        conv_kernel.reshape(9, wide),
        conv_bias.reshape(1, wide),
        long_filter,
        skip_gain.reshape(1, width),
        w_out,
    )
    return out.reshape(row_count, col_count, width)


def solution(mesh):
    in_specs = (P("row", "col", None), P(), P(), P(), P(), P(), P())
    out_specs = P("row", "col", None)
    return jax.shard_map(
        on_device, mesh=mesh, in_specs=in_specs, out_specs=out_specs, check_vma=False
    )
```

```python
import functools

import jax
import jax.numpy as jnp
from jax import lax
from jax.experimental import pallas as pl
from jax.experimental.pallas import tpu as pltpu
from jax.sharding import PartitionSpec as P


def layer_kernel(rows, span, pitch, x_hbm, w_hbm, k_hbm, b_hbm, filt_hbm, gain_hbm, wout_hbm,
                 out_ref, x_ref, w_ref, k_ref, b_ref, filt_ref, gain_ref, wout_ref, load_sem, pext, shifted, kb, bb, send_col, recv_col, recv_row, own_b, prev_b,
                 ext, fb, qf, gated, send_sem, recv_sem):
    width = out_ref.shape[1]
    wide = w_ref.shape[1]
    count = rows * span
    r = lax.axis_index("row")
    c = lax.axis_index("col")
    ncol = lax.axis_size("col")
    partner = 1 - r
    edge = partner * (rows - 1)
    mesh_id = pl.DeviceIdType.MESH
    right = lax.rem(c + 1, ncol)
    left = lax.rem(c + ncol - 1, ncol)
    peers = ((r, right), (r, left), (partner, right), (partner, left), (partner, c), (partner, c))

    recv_col[...] = jnp.zeros_like(recv_col)
    barrier = pltpu.get_barrier_semaphore()
    conds = (c < ncol - 1, c > 0, c < ncol - 1, c > 0)
    for dev, cond in zip(peers[:4], conds):
        @pl.when(cond)
        def _():
            pl.semaphore_signal(barrier, 1, device_id=dev, device_id_type=mesh_id)
    pl.semaphore_signal(barrier, 1, device_id=peers[4], device_id_type=mesh_id)
    has_left = (c + ncol - 1) // ncol
    has_right = (2 * ncol - 3 - c) // (ncol - 1)

    loads = [
        pltpu.make_async_copy(src, dst, load_sem.at[i])
        for i, (src, dst) in enumerate((
            (x_hbm, x_ref), (w_hbm, w_ref), (k_hbm, k_ref), (b_hbm, b_ref),
            (filt_hbm, filt_ref), (gain_hbm, gain_ref), (wout_hbm, wout_ref)))
    ]
    for cp in loads:
        cp.start()
    for cp in loads[:4]:
        cp.wait()
    for i in range(9):
        kb[i] = jnp.broadcast_to(
            k_ref[i // 3, i % 3 : i % 3 + 1, :].astype(jnp.float32), (span, wide))
    bb[...] = jnp.broadcast_to(b_ref[...].reshape(1, wide), (span, wide))
    proj = jnp.dot(x_ref[...], w_ref[...], preferred_element_type=jnp.float32)
    proj = proj.astype(jnp.bfloat16).astype(jnp.float32)
    for i in range(rows):
        pext[pl.ds((1 + i) * pitch + 8, span), :] = proj[i * span : (i + 1) * span]
    other_row = r * (rows + 1)
    pext[pl.ds(pl.multiple_of(other_row * pitch, 8), pitch), :] = jnp.zeros((pitch, wide),
                                                                            jnp.float32)
    for i in range(rows):
        send_col[0, i : i + 1, :] = pext[pl.ds((1 + i) * pitch + 8 + span - 1, 1), :]
        send_col[1, i : i + 1, :] = pext[pl.ds((1 + i) * pitch + 8, 1), :]
    edge_base = pl.multiple_of((1 + edge) * pitch, 8)
    send_col[2, 0:8, :] = jnp.broadcast_to(pext[pl.ds(edge_base + 8 + span - 1, 1), :], (8, wide))
    send_col[3, 0:8, :] = jnp.broadcast_to(pext[pl.ds(edge_base + 8, 1), :], (8, wide))

    pl.semaphore_wait(barrier, 1 + 2 * has_left + 2 * has_right)
    copies = [
        pltpu.make_async_remote_copy(send_col.at[slot], recv_col.at[slot], send_sem.at[slot],
                                     recv_sem.at[slot], device_id=peers[slot],
                                     device_id_type=mesh_id)
        for slot in range(4)
    ]
    copies.append(pltpu.make_async_remote_copy(
        pext.at[pl.ds(edge_base + 8, span)], recv_row, send_sem.at[4], recv_sem.at[4],
        device_id=peers[4], device_id_type=mesh_id))
    product_copy = pltpu.make_async_remote_copy(
        own_b, prev_b, send_sem.at[5], recv_sem.at[5], device_id=peers[5],
        device_id_type=mesh_id)
    send_when = (c < ncol - 1, c > 0, c < ncol - 1, c > 0, None)
    recv_when = (c > 0, c < ncol - 1, c > 0, c < ncol - 1, None)

    def guarded(cond, fn):
        if cond is None:
            fn()
        else:
            pl.when(cond)(fn)

    for cp, cond in zip(copies, send_when):
        guarded(cond, cp.start)
    for cp in loads[4:]:
        cp.wait()
    for lag in range(2 * rows):
        fb[lag] = jnp.broadcast_to(filt_ref[lag : lag + 1, :].astype(jnp.float32), (8, width))
    for cp, cond in zip(copies, send_when):
        guarded(cond, cp.wait_send)
    for cp, cond in zip(copies, recv_when):
        guarded(cond, cp.wait_recv)

    halo_base = pl.multiple_of(partner * (rows + 1) * pitch, 8)
    pext[pl.ds(halo_base + 8, span), :] = recv_row[...]
    for i in range(rows):
        pext[pl.ds((1 + i) * pitch + 7, 1), :] = recv_col[0, i : i + 1, :]
        pext[pl.ds((1 + i) * pitch + 8 + span, 1), :] = recv_col[1, i : i + 1, :]
    pext[pl.ds(halo_base + 7, 1), :] = recv_col[2, 0:1, :]
    pext[pl.ds(halo_base + 8 + span, 1), :] = recv_col[3, 0:1, :]

    def shift_body(i, carry):
        window = pext[pl.ds(pl.multiple_of(i * pitch, 8), pitch), :]
        dst = pl.ds(pl.multiple_of(i * span, 8), span)
        shifted[0, dst, :] = window[7 : 7 + span]
        shifted[1, dst, :] = window[8 : 8 + span]
        shifted[2, dst, :] = window[9 : 9 + span]
        return carry

    lax.fori_loop(0, rows + 2, shift_body, 0)

    def row_body(i, carry):
        res = []
        for grp in range(3):
            lanes = pl.ds(grp * width, width)
            acc = bb[:, lanes]
            for a in range(3):
                src = pl.ds(pl.multiple_of((i + a) * span, 8), span)
                for b in range(3):
                    acc = acc + shifted[b, src, lanes] * kb[a * 3 + b, :, lanes]
            res.append(acc.astype(jnp.bfloat16).astype(jnp.float32))
        dst = pl.ds(pl.multiple_of(i * span, 16), span)
        qf[dst, :] = res[0]
        prod = (res[1] * res[2]).astype(jnp.bfloat16)
        own_b[dst, :] = prod
        ext[pl.ds(pl.multiple_of(count + i * span, 16), span), :] = prod.astype(jnp.float32)
        return carry

    lax.fori_loop(0, rows, row_body, 0)

    @pl.when(r == 0)
    def _():
        product_copy.start()

    lane_groups = width // 128

    def own_pass(i, carry):
        lanes = pl.ds(pl.multiple_of((i % lane_groups) * 128, 128), 128)
        w0 = pl.multiple_of((i // lane_groups) * 8, 8)
        acc = [None] * rows
        for src in range(rows, 2 * rows):
            x = ext[pl.ds(src * span + w0, 8), lanes]
            for a in range(src - rows, rows):
                term = fb[rows + a - src, :, lanes] * x
                acc[a] = term if acc[a] is None else acc[a] + term
        for a in range(rows):
            gated[pl.ds(a * span + w0, 8), lanes] = acc[a]
        return carry

    lax.fori_loop(0, (span // 8) * lane_groups, own_pass, 0)

    @pl.when(r == 0)
    def _():
        product_copy.wait_send()
        ext[0:count, :] = jnp.zeros((count, width), jnp.float32)

    @pl.when(r == 1)
    def _():
        product_copy.wait_recv()
        ext[0:count, :] = prev_b[...].astype(jnp.float32)

    def prev_pass(i, carry):
        lanes = pl.ds(pl.multiple_of((i % lane_groups) * 128, 128), 128)
        w0 = pl.multiple_of((i // lane_groups) * 8, 8)
        acc = [gated[pl.ds(a * span + w0, 8), lanes] for a in range(rows)]
        for src in range(rows):
            x = ext[pl.ds(src * span + w0, 8), lanes]
            for a in range(rows):
                acc[a] = acc[a] + fb[rows + a - src, :, lanes] * x
        gain = jnp.broadcast_to(gain_ref[lanes].reshape(1, 128), (8, 128))
        for a in range(rows):
            own = ext[pl.ds(count + a * span + w0, 8), lanes]
            q = qf[pl.ds(a * span + w0, 8), lanes]
            gated[pl.ds(a * span + w0, 8), lanes] = q * (acc[a] + gain * own)
        return carry

    lax.fori_loop(0, (span // 8) * lane_groups, prev_pass, 0)
    out_ref[...] = jnp.dot(
        gated[...].astype(jnp.bfloat16), wout_ref[...], preferred_element_type=jnp.float32
    ).astype(out_ref.dtype)


def on_device(image_tokens, w_in, conv_kernel, conv_bias, long_filter, skip_gain, w_out):
    row_count, col_count, width = image_tokens.shape
    pitch = 48
    flat = row_count * col_count
    wide = w_in.shape[1]
    vmem = pl.BlockSpec(memory_space=pltpu.VMEM)
    out = pl.pallas_call(
        functools.partial(layer_kernel, row_count, col_count, pitch),
        out_shape=jax.ShapeDtypeStruct((flat, width), jnp.bfloat16),
        in_specs=[pl.BlockSpec(memory_space=pl.ANY)] * 7,
        out_specs=vmem,
        scratch_shapes=[
            pltpu.VMEM((flat, width), jnp.bfloat16),
            pltpu.VMEM(w_in.shape, jnp.bfloat16),
            pltpu.VMEM(conv_kernel.shape, jnp.bfloat16),
            pltpu.VMEM(conv_bias.shape, jnp.float32),
            pltpu.VMEM(long_filter.shape, jnp.bfloat16),
            pltpu.VMEM(skip_gain.shape, jnp.float32),
            pltpu.VMEM(w_out.shape, jnp.bfloat16),
            pltpu.SemaphoreType.DMA((7,)),
            pltpu.VMEM(((row_count + 2) * pitch, wide), jnp.float32),
            pltpu.VMEM((3, (row_count + 2) * col_count, wide), jnp.float32),
            pltpu.VMEM((9, col_count, wide), jnp.float32),
            pltpu.VMEM((col_count, wide), jnp.float32),
            pltpu.VMEM((4, row_count, wide), jnp.float32),
            pltpu.VMEM((4, row_count, wide), jnp.float32),
            pltpu.VMEM((col_count, wide), jnp.float32),
            pltpu.VMEM((flat, width), jnp.bfloat16),
            pltpu.VMEM((flat, width), jnp.bfloat16),
            pltpu.VMEM((2 * flat, width), jnp.float32),
            pltpu.VMEM((2 * row_count, 8, width), jnp.float32),
            pltpu.VMEM((flat, width), jnp.float32),
            pltpu.VMEM((flat, width), jnp.float32),
            pltpu.SemaphoreType.DMA((6,)),
            pltpu.SemaphoreType.DMA((6,)),
        ],
        compiler_params=pltpu.CompilerParams(
            collective_id=0, has_side_effects=True, vmem_limit_bytes=67043328
        ),
    )(
        image_tokens.reshape(flat, width),
        w_in,
        conv_kernel,
        conv_bias,
        long_filter,
        skip_gain,
        w_out,
    )
    return out.reshape(row_count, col_count, width)


def solution(mesh):
    in_specs = (P("row", "col", None), P(), P(), P(), P(), P(), P())
    out_specs = P("row", "col", None)
    return jax.shard_map(
        on_device, mesh=mesh, in_specs=in_specs, out_specs=out_specs, check_vma=False
    )
```

```python
import functools

import jax
import jax.numpy as jnp
from jax import lax
from jax.experimental import pallas as pl
from jax.experimental.pallas import tpu as pltpu
from jax.sharding import PartitionSpec as P


def layer_kernel(rows, span, pitch, x_hbm, w_hbm, k_hbm, b_hbm, filt_hbm, gain_hbm, wout_hbm,
                 out_ref, x_ref, w_ref, k_ref, b_ref, filt_ref, gain_ref, wout_ref, load_sem, pext, shifted, kb, bb, send_col, recv_col, recv_row, own_b, prev_b,
                 ext, fb, qf, gated, send_sem, recv_sem):
    width = out_ref.shape[1]
    wide = w_ref.shape[1]
    count = rows * span
    r = lax.axis_index("row")
    c = lax.axis_index("col")
    ncol = lax.axis_size("col")
    partner = 1 - r
    edge = partner * (rows - 1)
    mesh_id = pl.DeviceIdType.MESH
    right = lax.rem(c + 1, ncol)
    left = lax.rem(c + ncol - 1, ncol)
    peers = ((r, right), (r, left), (partner, right), (partner, left), (partner, c), (partner, c))

    recv_col[...] = jnp.zeros_like(recv_col)
    barrier = pltpu.get_barrier_semaphore()
    conds = (c < ncol - 1, c > 0, c < ncol - 1, c > 0)
    for dev, cond in zip(peers[:4], conds):
        @pl.when(cond)
        def _():
            pl.semaphore_signal(barrier, 1, device_id=dev, device_id_type=mesh_id)
    pl.semaphore_signal(barrier, 1, device_id=peers[4], device_id_type=mesh_id)
    has_left = (c + ncol - 1) // ncol
    has_right = (2 * ncol - 3 - c) // (ncol - 1)

    loads = [
        pltpu.make_async_copy(src, dst, load_sem.at[i])
        for i, (src, dst) in enumerate((
            (x_hbm, x_ref), (w_hbm, w_ref), (k_hbm, k_ref), (b_hbm, b_ref),
            (filt_hbm, filt_ref), (gain_hbm, gain_ref), (wout_hbm, wout_ref)))
    ]
    for cp in loads:
        cp.start()
    for cp in loads[:4]:
        cp.wait()
    for i in range(9):
        kb[i] = jnp.broadcast_to(
            k_ref[i // 3, i % 3 : i % 3 + 1, :].astype(jnp.float32), (span, wide))
    bb[...] = jnp.broadcast_to(b_ref[...].reshape(1, wide), (span, wide))
    proj = jnp.dot(x_ref[...], w_ref[...], preferred_element_type=jnp.float32)
    proj = proj.astype(jnp.bfloat16).astype(jnp.float32)
    for i in range(rows):
        pext[pl.ds((1 + i) * pitch + 8, span), :] = proj[i * span : (i + 1) * span]
    other_row = r * (rows + 1)
    pext[pl.ds(pl.multiple_of(other_row * pitch, 8), pitch), :] = jnp.zeros((pitch, wide),
                                                                            jnp.float32)
    for i in range(rows):
        send_col[0, i : i + 1, :] = pext[pl.ds((1 + i) * pitch + 8 + span - 1, 1), :]
        send_col[1, i : i + 1, :] = pext[pl.ds((1 + i) * pitch + 8, 1), :]
    edge_base = pl.multiple_of((1 + edge) * pitch, 8)
    send_col[2, 0:8, :] = jnp.broadcast_to(pext[pl.ds(edge_base + 8 + span - 1, 1), :], (8, wide))
    send_col[3, 0:8, :] = jnp.broadcast_to(pext[pl.ds(edge_base + 8, 1), :], (8, wide))

    pl.semaphore_wait(barrier, 1 + 2 * has_left + 2 * has_right)
    copies = [
        pltpu.make_async_remote_copy(send_col.at[slot], recv_col.at[slot], send_sem.at[slot],
                                     recv_sem.at[slot], device_id=peers[slot],
                                     device_id_type=mesh_id)
        for slot in range(4)
    ]
    copies.append(pltpu.make_async_remote_copy(
        pext.at[pl.ds(edge_base + 8, span)], recv_row, send_sem.at[4], recv_sem.at[4],
        device_id=peers[4], device_id_type=mesh_id))
    piece = 8 * span
    pieces = rows // 8

    def product_copy(k):
        return pltpu.make_async_remote_copy(
            own_b.at[pl.ds(k * piece, piece)], prev_b.at[pl.ds(k * piece, piece)],
            send_sem.at[5 + k], recv_sem.at[5 + k], device_id=peers[5],
            device_id_type=mesh_id)
    send_when = (c < ncol - 1, c > 0, c < ncol - 1, c > 0, None)
    recv_when = (c > 0, c < ncol - 1, c > 0, c < ncol - 1, None)

    def guarded(cond, fn):
        if cond is None:
            fn()
        else:
            pl.when(cond)(fn)

    for cp, cond in zip(copies, send_when):
        guarded(cond, cp.start)
    for cp in loads[4:]:
        cp.wait()
    for lag in range(2 * rows):
        fb[lag] = jnp.broadcast_to(filt_ref[lag : lag + 1, :].astype(jnp.float32), (8, width))
    for cp, cond in zip(copies, send_when):
        guarded(cond, cp.wait_send)
    for cp, cond in zip(copies, recv_when):
        guarded(cond, cp.wait_recv)

    halo_base = pl.multiple_of(partner * (rows + 1) * pitch, 8)
    pext[pl.ds(halo_base + 8, span), :] = recv_row[...]
    for i in range(rows):
        pext[pl.ds((1 + i) * pitch + 7, 1), :] = recv_col[0, i : i + 1, :]
        pext[pl.ds((1 + i) * pitch + 8 + span, 1), :] = recv_col[1, i : i + 1, :]
    pext[pl.ds(halo_base + 7, 1), :] = recv_col[2, 0:1, :]
    pext[pl.ds(halo_base + 8 + span, 1), :] = recv_col[3, 0:1, :]

    def shift_body(i, carry):
        window = pext[pl.ds(pl.multiple_of(i * pitch, 8), pitch), :]
        dst = pl.ds(pl.multiple_of(i * span, 8), span)
        shifted[0, dst, :] = window[7 : 7 + span]
        shifted[1, dst, :] = window[8 : 8 + span]
        shifted[2, dst, :] = window[9 : 9 + span]
        return carry

    lax.fori_loop(0, rows + 2, shift_body, 0)

    def row_body(i, carry):
        @pl.when(jnp.logical_and(r == 0, jnp.logical_and(i > 0, i % 8 == 0)))
        def _():
            product_copy(i // 8 - 1).start()

        res = []
        for grp in range(3):
            lanes = pl.ds(grp * width, width)
            acc = bb[:, lanes]
            for a in range(3):
                src = pl.ds(pl.multiple_of((i + a) * span, 8), span)
                for b in range(3):
                    acc = acc + shifted[b, src, lanes] * kb[a * 3 + b, :, lanes]
            res.append(acc.astype(jnp.bfloat16).astype(jnp.float32))
        dst = pl.ds(pl.multiple_of(i * span, 16), span)
        qf[dst, :] = res[0]
        prod = (res[1] * res[2]).astype(jnp.bfloat16)
        own_b[dst, :] = prod
        ext[pl.ds(pl.multiple_of(count + i * span, 16), span), :] = prod.astype(jnp.float32)
        return carry

    lax.fori_loop(0, rows, row_body, 0)

    @pl.when(r == 0)
    def _():
        product_copy(pieces - 1).start()

    lane_groups = width // 128

    def own_pass(i, carry):
        lanes = pl.ds(pl.multiple_of((i % lane_groups) * 128, 128), 128)
        w0 = pl.multiple_of((i // lane_groups) * 8, 8)
        acc = [None] * rows
        for src in range(rows, 2 * rows):
            x = ext[pl.ds(src * span + w0, 8), lanes]
            for a in range(src - rows, rows):
                term = fb[rows + a - src, :, lanes] * x
                acc[a] = term if acc[a] is None else acc[a] + term
        for a in range(rows):
            gated[pl.ds(a * span + w0, 8), lanes] = acc[a]
        return carry

    lax.fori_loop(0, (span // 8) * lane_groups, own_pass, 0)

    @pl.when(r == 0)
    def _():
        for k in range(pieces):
            product_copy(k).wait_send()
        ext[0:count, :] = jnp.zeros((count, width), jnp.float32)

    @pl.when(r == 1)
    def _():
        for k in range(pieces):
            product_copy(k).wait_recv()
        ext[0:count, :] = prev_b[...].astype(jnp.float32)

    def prev_pass(i, carry):
        lanes = pl.ds(pl.multiple_of((i % lane_groups) * 128, 128), 128)
        w0 = pl.multiple_of((i // lane_groups) * 8, 8)
        acc = [gated[pl.ds(a * span + w0, 8), lanes] for a in range(rows)]
        for src in range(rows):
            x = ext[pl.ds(src * span + w0, 8), lanes]
            for a in range(rows):
                acc[a] = acc[a] + fb[rows + a - src, :, lanes] * x
        gain = jnp.broadcast_to(gain_ref[lanes].reshape(1, 128), (8, 128))
        for a in range(rows):
            own = ext[pl.ds(count + a * span + w0, 8), lanes]
            q = qf[pl.ds(a * span + w0, 8), lanes]
            gated[pl.ds(a * span + w0, 8), lanes] = q * (acc[a] + gain * own)
        return carry

    lax.fori_loop(0, (span // 8) * lane_groups, prev_pass, 0)
    out_ref[...] = jnp.dot(
        gated[...].astype(jnp.bfloat16), wout_ref[...], preferred_element_type=jnp.float32
    ).astype(out_ref.dtype)


def on_device(image_tokens, w_in, conv_kernel, conv_bias, long_filter, skip_gain, w_out):
    row_count, col_count, width = image_tokens.shape
    pitch = 48
    flat = row_count * col_count
    wide = w_in.shape[1]
    vmem = pl.BlockSpec(memory_space=pltpu.VMEM)
    out = pl.pallas_call(
        functools.partial(layer_kernel, row_count, col_count, pitch),
        out_shape=jax.ShapeDtypeStruct((flat, width), jnp.bfloat16),
        in_specs=[pl.BlockSpec(memory_space=pl.ANY)] * 7,
        out_specs=vmem,
        scratch_shapes=[
            pltpu.VMEM((flat, width), jnp.bfloat16),
            pltpu.VMEM(w_in.shape, jnp.bfloat16),
            pltpu.VMEM(conv_kernel.shape, jnp.bfloat16),
            pltpu.VMEM(conv_bias.shape, jnp.float32),
            pltpu.VMEM(long_filter.shape, jnp.bfloat16),
            pltpu.VMEM(skip_gain.shape, jnp.float32),
            pltpu.VMEM(w_out.shape, jnp.bfloat16),
            pltpu.SemaphoreType.DMA((7,)),
            pltpu.VMEM(((row_count + 2) * pitch, wide), jnp.float32),
            pltpu.VMEM((3, (row_count + 2) * col_count, wide), jnp.float32),
            pltpu.VMEM((9, col_count, wide), jnp.float32),
            pltpu.VMEM((col_count, wide), jnp.float32),
            pltpu.VMEM((4, row_count, wide), jnp.float32),
            pltpu.VMEM((4, row_count, wide), jnp.float32),
            pltpu.VMEM((col_count, wide), jnp.float32),
            pltpu.VMEM((flat, width), jnp.bfloat16),
            pltpu.VMEM((flat, width), jnp.bfloat16),
            pltpu.VMEM((2 * flat, width), jnp.float32),
            pltpu.VMEM((2 * row_count, 8, width), jnp.float32),
            pltpu.VMEM((flat, width), jnp.float32),
            pltpu.VMEM((flat, width), jnp.float32),
            pltpu.SemaphoreType.DMA((5 + row_count // 8,)),
            pltpu.SemaphoreType.DMA((5 + row_count // 8,)),
        ],
        compiler_params=pltpu.CompilerParams(
            collective_id=0, has_side_effects=True, vmem_limit_bytes=67043328
        ),
    )(
        image_tokens.reshape(flat, width),
        w_in,
        conv_kernel,
        conv_bias,
        long_filter,
        skip_gain,
        w_out,
    )
    return out.reshape(row_count, col_count, width)


def solution(mesh):
    in_specs = (P("row", "col", None), P(), P(), P(), P(), P(), P())
    out_specs = P("row", "col", None)
    return jax.shard_map(
        on_device, mesh=mesh, in_specs=in_specs, out_specs=out_specs, check_vma=False
    )
```

```python
import functools

import jax
import jax.numpy as jnp
from jax import lax
from jax.experimental import pallas as pl
from jax.experimental.pallas import tpu as pltpu
from jax.sharding import PartitionSpec as P


def layer_kernel(rows, span, pitch, x_hbm, w_hbm, k_hbm, b_hbm, filt_hbm, gain_hbm, wout_hbm,
                 out_ref, x_ref, w_ref, k_ref, b_ref, filt_ref, gain_ref, wout_ref, load_sem, pext,
                 shifted, kb, bb, send_col, recv_col, recv_row, own_b, prev_b, stage, send_row,
                 send_cor, recv_cor, ext, fb, qf, gated, send_sem, recv_sem):
    width = out_ref.shape[1]
    wide = w_ref.shape[1]
    count = rows * span
    r = lax.axis_index("row")
    c = lax.axis_index("col")
    ncol = lax.axis_size("col")
    partner = 1 - r
    edge = partner * (rows - 1)
    mesh_id = pl.DeviceIdType.MESH
    right = lax.rem(c + 1, ncol)
    left = lax.rem(c + ncol - 1, ncol)
    peers = ((r, right), (r, left), (partner, right), (partner, left), (partner, c), (partner, c))

    recv_col[...] = jnp.zeros_like(recv_col)
    recv_cor[...] = jnp.zeros_like(recv_cor)
    barrier = pltpu.get_barrier_semaphore()
    conds = (c < ncol - 1, c > 0, c < ncol - 1, c > 0)
    for dev, cond in zip(peers[:4], conds):
        @pl.when(cond)
        def _():
            pl.semaphore_signal(barrier, 1, device_id=dev, device_id_type=mesh_id)
    pl.semaphore_signal(barrier, 1, device_id=peers[4], device_id_type=mesh_id)
    has_left = (c + ncol - 1) // ncol
    has_right = (2 * ncol - 3 - c) // (ncol - 1)

    loads = [
        pltpu.make_async_copy(src, dst, load_sem.at[i])
        for i, (src, dst) in enumerate((
            (x_hbm, x_ref), (w_hbm, w_ref), (k_hbm, k_ref), (b_hbm, b_ref),
            (filt_hbm, filt_ref), (gain_hbm, gain_ref), (wout_hbm, wout_ref)))
    ]
    for cp in loads:
        cp.start()
    for cp in loads[:4]:
        cp.wait()
    for i in range(9):
        kb[i] = jnp.broadcast_to(
            k_ref[i // 3, i % 3 : i % 3 + 1, :].astype(jnp.float32), (span, wide))
    bb[...] = jnp.broadcast_to(b_ref[...].reshape(1, wide), (span, wide))
    proj = jnp.dot(x_ref[...], w_ref[...], preferred_element_type=jnp.float32)
    proj = proj.astype(jnp.bfloat16).astype(jnp.float32)
    for i in range(rows):
        pext[pl.ds((1 + i) * pitch + 8, span), :] = proj[i * span : (i + 1) * span]
    other_row = r * (rows + 1)
    pext[pl.ds(pl.multiple_of(other_row * pitch, 8), pitch), :] = jnp.zeros((pitch, wide),
                                                                            jnp.float32)
    for i in range(rows):
        stage[0, i : i + 1, :] = pext[pl.ds((1 + i) * pitch + 8 + span - 1, 1), :]
        stage[1, i : i + 1, :] = pext[pl.ds((1 + i) * pitch + 8, 1), :]
    send_col[0] = stage[0].astype(jnp.bfloat16)
    send_col[1] = stage[1].astype(jnp.bfloat16)
    edge_base = pl.multiple_of((1 + edge) * pitch, 8)
    send_row[...] = pext[pl.ds(edge_base + 8, span), :].astype(jnp.bfloat16)
    corner_rows = send_cor.shape[1]
    send_cor[0] = jnp.broadcast_to(pext[pl.ds(edge_base + 8 + span - 1, 1), :],
                                   (corner_rows, wide)).astype(jnp.bfloat16)
    send_cor[1] = jnp.broadcast_to(pext[pl.ds(edge_base + 8, 1), :],
                                   (corner_rows, wide)).astype(jnp.bfloat16)

    pl.semaphore_wait(barrier, 1 + 2 * has_left + 2 * has_right)
    pairs = ((send_col.at[0], recv_col.at[0]), (send_col.at[1], recv_col.at[1]),
             (send_cor.at[0], recv_cor.at[0]), (send_cor.at[1], recv_cor.at[1]),
             (send_row, recv_row))
    copies = [
        pltpu.make_async_remote_copy(src_ref, dst_ref, send_sem.at[slot], recv_sem.at[slot],
                                     device_id=peers[slot], device_id_type=mesh_id)
        for slot, (src_ref, dst_ref) in enumerate(pairs)
    ]
    piece = 8 * span
    pieces = rows // 8

    def product_copy(k):
        return pltpu.make_async_remote_copy(
            own_b.at[pl.ds(k * piece, piece)], prev_b.at[pl.ds(k * piece, piece)],
            send_sem.at[5 + k], recv_sem.at[5 + k], device_id=peers[5],
            device_id_type=mesh_id)
    send_when = (c < ncol - 1, c > 0, c < ncol - 1, c > 0, None)
    recv_when = (c > 0, c < ncol - 1, c > 0, c < ncol - 1, None)

    def guarded(cond, fn):
        if cond is None:
            fn()
        else:
            pl.when(cond)(fn)

    for cp, cond in zip(copies, send_when):
        guarded(cond, cp.start)
    for cp in loads[4:]:
        cp.wait()
    for lag in range(2 * rows):
        fb[lag] = jnp.broadcast_to(filt_ref[lag : lag + 1, :].astype(jnp.float32), (8, width))
    for cp, cond in zip(copies, send_when):
        guarded(cond, cp.wait_send)
    for cp, cond in zip(copies, recv_when):
        guarded(cond, cp.wait_recv)

    halo_base = pl.multiple_of(partner * (rows + 1) * pitch, 8)
    pext[pl.ds(halo_base + 8, span), :] = recv_row[...].astype(jnp.float32)
    stage[0] = recv_col[0].astype(jnp.float32)
    stage[1] = recv_col[1].astype(jnp.float32)
    for i in range(rows):
        pext[pl.ds((1 + i) * pitch + 7, 1), :] = stage[0, i : i + 1, :]
        pext[pl.ds((1 + i) * pitch + 8 + span, 1), :] = stage[1, i : i + 1, :]
    pext[pl.ds(halo_base + 7, 1), :] = recv_cor[0, 0:1, :].astype(jnp.float32)
    pext[pl.ds(halo_base + 8 + span, 1), :] = recv_cor[1, 0:1, :].astype(jnp.float32)

    def shift_body(i, carry):
        window = pext[pl.ds(pl.multiple_of(i * pitch, 8), pitch), :]
        dst = pl.ds(pl.multiple_of(i * span, 8), span)
        shifted[0, dst, :] = window[7 : 7 + span]
        shifted[1, dst, :] = window[8 : 8 + span]
        shifted[2, dst, :] = window[9 : 9 + span]
        return carry

    lax.fori_loop(0, rows + 2, shift_body, 0)

    def row_body(i, carry):
        @pl.when(jnp.logical_and(r == 0, jnp.logical_and(i > 0, i % 8 == 0)))
        def _():
            product_copy(i // 8 - 1).start()

        res = []
        for grp in range(3):
            lanes = pl.ds(grp * width, width)
            acc = bb[:, lanes]
            for a in range(3):
                src = pl.ds(pl.multiple_of((i + a) * span, 8), span)
                for b in range(3):
                    acc = acc + shifted[b, src, lanes] * kb[a * 3 + b, :, lanes]
            res.append(acc.astype(jnp.bfloat16).astype(jnp.float32))
        dst = pl.ds(pl.multiple_of(i * span, 16), span)
        qf[dst, :] = res[0]
        prod = (res[1] * res[2]).astype(jnp.bfloat16)
        own_b[dst, :] = prod
        ext[pl.ds(pl.multiple_of(count + i * span, 16), span), :] = prod.astype(jnp.float32)
        return carry

    lax.fori_loop(0, rows, row_body, 0)

    @pl.when(r == 0)
    def _():
        product_copy(pieces - 1).start()

    lane_groups = width // 128

    def own_pass(i, carry):
        lanes = pl.ds(pl.multiple_of((i % lane_groups) * 128, 128), 128)
        w0 = pl.multiple_of((i // lane_groups) * 8, 8)
        acc = [None] * rows
        for src in range(rows, 2 * rows):
            x = ext[pl.ds(src * span + w0, 8), lanes]
            for a in range(src - rows, rows):
                term = fb[rows + a - src, :, lanes] * x
                acc[a] = term if acc[a] is None else acc[a] + term
        for a in range(rows):
            gated[pl.ds(a * span + w0, 8), lanes] = acc[a]
        return carry

    lax.fori_loop(0, (span // 8) * lane_groups, own_pass, 0)

    @pl.when(r == 0)
    def _():
        for k in range(pieces):
            product_copy(k).wait_send()
        ext[0:count, :] = jnp.zeros((count, width), jnp.float32)

    @pl.when(r == 1)
    def _():
        for k in range(pieces):
            product_copy(k).wait_recv()
        ext[0:count, :] = prev_b[...].astype(jnp.float32)

    def prev_pass(i, carry):
        lanes = pl.ds(pl.multiple_of((i % lane_groups) * 128, 128), 128)
        w0 = pl.multiple_of((i // lane_groups) * 8, 8)
        acc = [gated[pl.ds(a * span + w0, 8), lanes] for a in range(rows)]
        for src in range(rows):
            x = ext[pl.ds(src * span + w0, 8), lanes]
            for a in range(rows):
                acc[a] = acc[a] + fb[rows + a - src, :, lanes] * x
        gain = jnp.broadcast_to(gain_ref[lanes].reshape(1, 128), (8, 128))
        for a in range(rows):
            own = ext[pl.ds(count + a * span + w0, 8), lanes]
            q = qf[pl.ds(a * span + w0, 8), lanes]
            gated[pl.ds(a * span + w0, 8), lanes] = q * (acc[a] + gain * own)
        return carry

    lax.fori_loop(0, (span // 8) * lane_groups, prev_pass, 0)
    out_ref[...] = jnp.dot(
        gated[...].astype(jnp.bfloat16), wout_ref[...], preferred_element_type=jnp.float32
    ).astype(out_ref.dtype)


def on_device(image_tokens, w_in, conv_kernel, conv_bias, long_filter, skip_gain, w_out):
    row_count, col_count, width = image_tokens.shape
    pitch = 48
    flat = row_count * col_count
    wide = w_in.shape[1]
    vmem = pl.BlockSpec(memory_space=pltpu.VMEM)
    out = pl.pallas_call(
        functools.partial(layer_kernel, row_count, col_count, pitch),
        out_shape=jax.ShapeDtypeStruct((flat, width), jnp.bfloat16),
        in_specs=[pl.BlockSpec(memory_space=pl.ANY)] * 7,
        out_specs=vmem,
        scratch_shapes=[
            pltpu.VMEM((flat, width), jnp.bfloat16),
            pltpu.VMEM(w_in.shape, jnp.bfloat16),
            pltpu.VMEM(conv_kernel.shape, jnp.bfloat16),
            pltpu.VMEM(conv_bias.shape, jnp.float32),
            pltpu.VMEM(long_filter.shape, jnp.bfloat16),
            pltpu.VMEM(skip_gain.shape, jnp.float32),
            pltpu.VMEM(w_out.shape, jnp.bfloat16),
            pltpu.SemaphoreType.DMA((7,)),
            pltpu.VMEM(((row_count + 2) * pitch, wide), jnp.float32),
            pltpu.VMEM((3, (row_count + 2) * col_count, wide), jnp.float32),
            pltpu.VMEM((9, col_count, wide), jnp.float32),
            pltpu.VMEM((col_count, wide), jnp.float32),
            pltpu.VMEM((2, row_count, wide), jnp.bfloat16),
            pltpu.VMEM((2, row_count, wide), jnp.bfloat16),
            pltpu.VMEM((col_count, wide), jnp.bfloat16),
            pltpu.VMEM((flat, width), jnp.bfloat16),
            pltpu.VMEM((flat, width), jnp.bfloat16),
            pltpu.VMEM((2, row_count, wide), jnp.float32),
            pltpu.VMEM((col_count, wide), jnp.bfloat16),
            pltpu.VMEM((2, 16, wide), jnp.bfloat16),
            pltpu.VMEM((2, 16, wide), jnp.bfloat16),
            pltpu.VMEM((2 * flat, width), jnp.float32),
            pltpu.VMEM((2 * row_count, 8, width), jnp.float32),
            pltpu.VMEM((flat, width), jnp.float32),
            pltpu.VMEM((flat, width), jnp.float32),
            pltpu.SemaphoreType.DMA((5 + row_count // 8,)),
            pltpu.SemaphoreType.DMA((5 + row_count // 8,)),
        ],
        compiler_params=pltpu.CompilerParams(
            collective_id=0, has_side_effects=True, vmem_limit_bytes=67043328
        ),
    )(
        image_tokens.reshape(flat, width),
        w_in,
        conv_kernel,
        conv_bias,
        long_filter,
        skip_gain,
        w_out,
    )
    return out.reshape(row_count, col_count, width)


def solution(mesh):
    in_specs = (P("row", "col", None), P(), P(), P(), P(), P(), P())
    out_specs = P("row", "col", None)
    return jax.shard_map(
        on_device, mesh=mesh, in_specs=in_specs, out_specs=out_specs, check_vma=False
    )
```

```python
import functools

import jax
import jax.numpy as jnp
from jax import lax
from jax.experimental import pallas as pl
from jax.experimental.pallas import tpu as pltpu
from jax.sharding import PartitionSpec as P


def layer_kernel(rows, span, pitch, x_hbm, w_hbm, k_hbm, b_hbm, filt_hbm, gain_hbm, wout_hbm,
                 out_ref, x_ref, w_ref, k_ref, b_ref, filt_ref, gain_ref, wout_ref, load_sem, pext,
                 shifted, kb, bb, send_col, recv_col, recv_row, own_b, prev_b, stage, send_row,
                 send_cor, recv_cor, ext, fb, qf, gated, send_sem, recv_sem):
    width = out_ref.shape[1]
    wide = w_ref.shape[1]
    count = rows * span
    r = lax.axis_index("row")
    c = lax.axis_index("col")
    ncol = lax.axis_size("col")
    partner = 1 - r
    edge = partner * (rows - 1)
    mesh_id = pl.DeviceIdType.MESH
    right = lax.rem(c + 1, ncol)
    left = lax.rem(c + ncol - 1, ncol)
    peers = ((r, right), (r, left), (partner, right), (partner, left), (partner, c), (partner, c))

    recv_col[...] = jnp.zeros_like(recv_col)
    recv_cor[...] = jnp.zeros_like(recv_cor)
    barrier = pltpu.get_barrier_semaphore()
    conds = (c < ncol - 1, c > 0, c < ncol - 1, c > 0)
    for dev, cond in zip(peers[:4], conds):
        @pl.when(cond)
        def _():
            pl.semaphore_signal(barrier, 1, device_id=dev, device_id_type=mesh_id)
    pl.semaphore_signal(barrier, 1, device_id=peers[4], device_id_type=mesh_id)
    has_left = (c + ncol - 1) // ncol
    has_right = (2 * ncol - 3 - c) // (ncol - 1)

    loads = [
        pltpu.make_async_copy(src, dst, load_sem.at[i])
        for i, (src, dst) in enumerate((
            (x_hbm, x_ref), (w_hbm, w_ref), (k_hbm, k_ref), (b_hbm, b_ref),
            (filt_hbm, filt_ref), (gain_hbm, gain_ref), (wout_hbm, wout_ref)))
    ]
    for cp in loads:
        cp.start()
    for cp in loads[:4]:
        cp.wait()
    for i in range(9):
        kb[i] = jnp.broadcast_to(
            k_ref[i // 3, i % 3 : i % 3 + 1, :].astype(jnp.float32), (span, wide))
    bb[...] = jnp.broadcast_to(b_ref[...].reshape(1, wide), (span, wide))
    proj = jnp.dot(x_ref[...], w_ref[...], preferred_element_type=jnp.float32)
    proj = proj.astype(jnp.bfloat16).astype(jnp.float32)
    for i in range(rows):
        pext[pl.ds((1 + i) * pitch + 8, span), :] = proj[i * span : (i + 1) * span]
    other_row = r * (rows + 1)
    pext[pl.ds(pl.multiple_of(other_row * pitch, 8), pitch), :] = jnp.zeros((pitch, wide),
                                                                            jnp.float32)
    for i in range(rows):
        stage[0, i : i + 1, :] = pext[pl.ds((1 + i) * pitch + 8 + span - 1, 1), :]
        stage[1, i : i + 1, :] = pext[pl.ds((1 + i) * pitch + 8, 1), :]
    send_col[0] = stage[0].astype(jnp.bfloat16)
    send_col[1] = stage[1].astype(jnp.bfloat16)
    edge_base = pl.multiple_of((1 + edge) * pitch, 8)
    send_row[...] = pext[pl.ds(edge_base + 8, span), :].astype(jnp.bfloat16)
    corner_rows = send_cor.shape[1]
    send_cor[0] = jnp.broadcast_to(pext[pl.ds(edge_base + 8 + span - 1, 1), :],
                                   (corner_rows, wide)).astype(jnp.bfloat16)
    send_cor[1] = jnp.broadcast_to(pext[pl.ds(edge_base + 8, 1), :],
                                   (corner_rows, wide)).astype(jnp.bfloat16)

    pl.semaphore_wait(barrier, 1 + 2 * has_left + 2 * has_right)
    pairs = ((send_col.at[0], recv_col.at[0]), (send_col.at[1], recv_col.at[1]),
             (send_cor.at[0], recv_cor.at[0]), (send_cor.at[1], recv_cor.at[1]),
             (send_row, recv_row))
    copies = [
        pltpu.make_async_remote_copy(src_ref, dst_ref, send_sem.at[slot], recv_sem.at[slot],
                                     device_id=peers[slot], device_id_type=mesh_id)
        for slot, (src_ref, dst_ref) in enumerate(pairs)
    ]
    piece = 8 * span
    pieces = rows // 8

    def product_copy(k):
        return pltpu.make_async_remote_copy(
            own_b.at[pl.ds(k * piece, piece)], prev_b.at[pl.ds(k * piece, piece)],
            send_sem.at[5 + k], recv_sem.at[5 + k], device_id=peers[5],
            device_id_type=mesh_id)
    send_when = (c < ncol - 1, c > 0, c < ncol - 1, c > 0, None)
    recv_when = (c > 0, c < ncol - 1, c > 0, c < ncol - 1, None)

    def guarded(cond, fn):
        if cond is None:
            fn()
        else:
            pl.when(cond)(fn)

    for cp, cond in zip(copies, send_when):
        guarded(cond, cp.start)
    for cp in loads[4:]:
        cp.wait()
    for lag in range(2 * rows):
        fb[lag] = jnp.broadcast_to(filt_ref[lag : lag + 1, :].astype(jnp.float32), (8, width))
    for cp, cond in zip(copies, send_when):
        guarded(cond, cp.wait_send)
    for cp, cond in zip(copies, recv_when):
        guarded(cond, cp.wait_recv)

    halo_base = pl.multiple_of(partner * (rows + 1) * pitch, 8)
    pext[pl.ds(halo_base + 8, span), :] = recv_row[...].astype(jnp.float32)
    stage[0] = recv_col[0].astype(jnp.float32)
    stage[1] = recv_col[1].astype(jnp.float32)
    for i in range(rows):
        pext[pl.ds((1 + i) * pitch + 7, 1), :] = stage[0, i : i + 1, :]
        pext[pl.ds((1 + i) * pitch + 8 + span, 1), :] = stage[1, i : i + 1, :]
    pext[pl.ds(halo_base + 7, 1), :] = recv_cor[0, 0:1, :].astype(jnp.float32)
    pext[pl.ds(halo_base + 8 + span, 1), :] = recv_cor[1, 0:1, :].astype(jnp.float32)

    def shift_body(i, carry):
        window = pext[pl.ds(pl.multiple_of(i * pitch, 8), pitch), :]
        dst = pl.ds(pl.multiple_of(i * span, 8), span)
        shifted[0, dst, :] = window[7 : 7 + span]
        shifted[1, dst, :] = window[8 : 8 + span]
        shifted[2, dst, :] = window[9 : 9 + span]
        return carry

    lax.fori_loop(0, rows + 2, shift_body, 0)

    def row_body(i, carry):
        @pl.when(jnp.logical_and(r == 0, jnp.logical_and(i > 0, i % 8 == 0)))
        def _():
            product_copy(i // 8 - 1).start()

        res = []
        for grp in range(3):
            lanes = pl.ds(grp * width, width)
            acc = bb[:, lanes]
            for a in range(3):
                src = pl.ds(pl.multiple_of((i + a) * span, 8), span)
                for b in range(3):
                    acc = acc + shifted[b, src, lanes] * kb[a * 3 + b, :, lanes]
            res.append(acc.astype(jnp.bfloat16).astype(jnp.float32))
        dst = pl.ds(pl.multiple_of(i * span, 16), span)
        qf[dst, :] = res[0]
        prod = (res[1] * res[2]).astype(jnp.bfloat16)
        own_b[dst, :] = prod
        ext[pl.ds(pl.multiple_of(count + i * span, 16), span), :] = prod.astype(jnp.float32)
        return carry

    lax.fori_loop(0, rows, row_body, 0)

    @pl.when(r == 0)
    def _():
        product_copy(pieces - 1).start()

    lane_groups = width // 128

    def own_pass(i, carry):
        lanes = pl.ds(pl.multiple_of((i % lane_groups) * 128, 128), 128)
        w0 = pl.multiple_of((i // lane_groups) * 8, 8)
        acc = [None] * rows
        for src in range(rows, 2 * rows):
            x = ext[pl.ds(src * span + w0, 8), lanes]
            for a in range(src - rows, rows):
                term = fb[rows + a - src, :, lanes] * x
                acc[a] = term if acc[a] is None else acc[a] + term
        for a in range(rows):
            gated[pl.ds(a * span + w0, 8), lanes] = acc[a]
        return carry

    lax.fori_loop(0, (span // 8) * lane_groups, own_pass, 0)

    @pl.when(r == 0)
    def _():
        for k in range(pieces):
            product_copy(k).wait_send()
        ext[0:count, :] = jnp.zeros((count, width), jnp.float32)

    @pl.when(r == 1)
    def _():
        for k in range(pieces):
            product_copy(k).wait_recv()
        ext[0:count, :] = prev_b[...].astype(jnp.float32)

    def prev_pass(i, carry):
        lanes = pl.ds(pl.multiple_of((i % lane_groups) * 128, 128), 128)
        w0 = pl.multiple_of((i // lane_groups) * 8, 8)
        acc = [gated[pl.ds(a * span + w0, 8), lanes] for a in range(rows)]
        for src in range(rows):
            x = ext[pl.ds(src * span + w0, 8), lanes]
            for a in range(rows):
                acc[a] = acc[a] + fb[rows + a - src, :, lanes] * x
        gain = jnp.broadcast_to(gain_ref[lanes].reshape(1, 128), (8, 128))
        for a in range(rows):
            own = ext[pl.ds(count + a * span + w0, 8), lanes]
            q = qf[pl.ds(a * span + w0, 8), lanes]
            gated[pl.ds(a * span + w0, 8), lanes] = q * (acc[a] + gain * own)
        return carry

    lax.fori_loop(0, (span // 8) * lane_groups, prev_pass, 0)
    out_ref[...] = gated[...].astype(out_ref.dtype)


def project_kernel(g_hbm, w_hbm, out_ref, g_ref, w_ref, sem):
    loads = [pltpu.make_async_copy(g_hbm, g_ref, sem.at[0]),
             pltpu.make_async_copy(w_hbm, w_ref, sem.at[1])]
    for cp in loads:
        cp.start()
    for cp in loads:
        cp.wait()
    out_ref[...] = jnp.dot(
        g_ref[...], w_ref[...], preferred_element_type=jnp.float32
    ).astype(out_ref.dtype)


def on_device(image_tokens, w_in, conv_kernel, conv_bias, long_filter, skip_gain, w_out):
    row_count, col_count, width = image_tokens.shape
    pitch = 48
    flat = row_count * col_count
    wide = w_in.shape[1]
    vmem = pl.BlockSpec(memory_space=pltpu.VMEM)
    out = pl.pallas_call(
        functools.partial(layer_kernel, row_count, col_count, pitch),
        out_shape=jax.ShapeDtypeStruct((flat, width), jnp.bfloat16),
        in_specs=[pl.BlockSpec(memory_space=pl.ANY)] * 7,
        out_specs=vmem,
        scratch_shapes=[
            pltpu.VMEM((flat, width), jnp.bfloat16),
            pltpu.VMEM(w_in.shape, jnp.bfloat16),
            pltpu.VMEM(conv_kernel.shape, jnp.bfloat16),
            pltpu.VMEM(conv_bias.shape, jnp.float32),
            pltpu.VMEM(long_filter.shape, jnp.bfloat16),
            pltpu.VMEM(skip_gain.shape, jnp.float32),
            pltpu.VMEM(w_out.shape, jnp.bfloat16),
            pltpu.SemaphoreType.DMA((7,)),
            pltpu.VMEM(((row_count + 2) * pitch, wide), jnp.float32),
            pltpu.VMEM((3, (row_count + 2) * col_count, wide), jnp.float32),
            pltpu.VMEM((9, col_count, wide), jnp.float32),
            pltpu.VMEM((col_count, wide), jnp.float32),
            pltpu.VMEM((2, row_count, wide), jnp.bfloat16),
            pltpu.VMEM((2, row_count, wide), jnp.bfloat16),
            pltpu.VMEM((col_count, wide), jnp.bfloat16),
            pltpu.VMEM((flat, width), jnp.bfloat16),
            pltpu.VMEM((flat, width), jnp.bfloat16),
            pltpu.VMEM((2, row_count, wide), jnp.float32),
            pltpu.VMEM((col_count, wide), jnp.bfloat16),
            pltpu.VMEM((2, 16, wide), jnp.bfloat16),
            pltpu.VMEM((2, 16, wide), jnp.bfloat16),
            pltpu.VMEM((2 * flat, width), jnp.float32),
            pltpu.VMEM((2 * row_count, 8, width), jnp.float32),
            pltpu.VMEM((flat, width), jnp.float32),
            pltpu.VMEM((flat, width), jnp.float32),
            pltpu.SemaphoreType.DMA((5 + row_count // 8,)),
            pltpu.SemaphoreType.DMA((5 + row_count // 8,)),
        ],
        compiler_params=pltpu.CompilerParams(
            collective_id=0, has_side_effects=True, vmem_limit_bytes=67043328
        ),
    )(
        image_tokens.reshape(flat, width),
        w_in,
        conv_kernel,
        conv_bias,
        long_filter,
        skip_gain,
        w_out,
    )
    out = pl.pallas_call(
        project_kernel,
        out_shape=jax.ShapeDtypeStruct((flat, width), jnp.bfloat16),
        in_specs=[pl.BlockSpec(memory_space=pl.ANY)] * 2,
        out_specs=vmem,
        scratch_shapes=[
            pltpu.VMEM((flat, width), jnp.bfloat16),
            pltpu.VMEM(w_out.shape, jnp.bfloat16),
            pltpu.SemaphoreType.DMA((2,)),
        ],
    )(out, w_out)
    return out.reshape(row_count, col_count, width)


def solution(mesh):
    in_specs = (P("row", "col", None), P(), P(), P(), P(), P(), P())
    out_specs = P("row", "col", None)
    return jax.shard_map(
        on_device, mesh=mesh, in_specs=in_specs, out_specs=out_specs, check_vma=False
    )
```

```python
import functools

import jax
import jax.numpy as jnp
from jax import lax
from jax.experimental import pallas as pl
from jax.experimental.pallas import tpu as pltpu
from jax.sharding import PartitionSpec as P


def layer_kernel(rows, span, pitch, x_hbm, w_hbm, k_hbm, b_hbm, filt_hbm, gain_hbm, wout_hbm,
                 out_ref, x_ref, w_ref, k_ref, b_ref, filt_ref, gain_ref, wout_ref, load_sem, pext,
                 shifted, kb, bb, send_col, recv_col, recv_row, own_b, prev_b, stage, send_row,
                 send_cor, recv_cor, ext, fb, qf, gated, send_sem, recv_sem):
    width = out_ref.shape[1]
    wide = w_ref.shape[1]
    count = rows * span
    r = lax.axis_index("row")
    c = lax.axis_index("col")
    ncol = lax.axis_size("col")
    partner = 1 - r
    edge = partner * (rows - 1)
    mesh_id = pl.DeviceIdType.MESH
    right = lax.rem(c + 1, ncol)
    left = lax.rem(c + ncol - 1, ncol)
    peers = ((r, right), (r, left), (partner, right), (partner, left), (partner, c), (partner, c))

    recv_col[...] = jnp.zeros_like(recv_col)
    recv_cor[...] = jnp.zeros_like(recv_cor)
    barrier = pltpu.get_barrier_semaphore()
    conds = (c < ncol - 1, c > 0, c < ncol - 1, c > 0)
    for dev, cond in zip(peers[:4], conds):
        @pl.when(cond)
        def _():
            pl.semaphore_signal(barrier, 1, device_id=dev, device_id_type=mesh_id)
    pl.semaphore_signal(barrier, 1, device_id=peers[4], device_id_type=mesh_id)
    has_left = (c + ncol - 1) // ncol
    has_right = (2 * ncol - 3 - c) // (ncol - 1)

    loads = [
        pltpu.make_async_copy(src, dst, load_sem.at[i])
        for i, (src, dst) in enumerate((
            (x_hbm, x_ref), (w_hbm, w_ref), (k_hbm, k_ref), (b_hbm, b_ref),
            (filt_hbm, filt_ref), (gain_hbm, gain_ref), (wout_hbm, wout_ref)))
    ]
    for cp in loads:
        cp.start()
    for cp in loads[:4]:
        cp.wait()
    for i in range(9):
        kb[i] = jnp.broadcast_to(
            k_ref[i // 3, i % 3 : i % 3 + 1, :].astype(jnp.float32), (span, wide))
    bb[...] = jnp.broadcast_to(b_ref[...].reshape(1, wide), (span, wide))
    proj = jnp.dot(x_ref[...], w_ref[...], preferred_element_type=jnp.float32)
    proj = proj.astype(jnp.bfloat16).astype(jnp.float32)
    for i in range(rows):
        pext[pl.ds((1 + i) * pitch + 8, span), :] = proj[i * span : (i + 1) * span]
    other_row = r * (rows + 1)
    pext[pl.ds(pl.multiple_of(other_row * pitch, 8), pitch), :] = jnp.zeros((pitch, wide),
                                                                            jnp.float32)
    for i in range(rows):
        stage[0, i : i + 1, :] = pext[pl.ds((1 + i) * pitch + 8 + span - 1, 1), :]
        stage[1, i : i + 1, :] = pext[pl.ds((1 + i) * pitch + 8, 1), :]
    send_col[0] = stage[0].astype(jnp.bfloat16)
    send_col[1] = stage[1].astype(jnp.bfloat16)
    edge_base = pl.multiple_of((1 + edge) * pitch, 8)
    send_row[...] = pext[pl.ds(edge_base + 8, span), :].astype(jnp.bfloat16)
    corner_rows = send_cor.shape[1]
    send_cor[0] = jnp.broadcast_to(pext[pl.ds(edge_base + 8 + span - 1, 1), :],
                                   (corner_rows, wide)).astype(jnp.bfloat16)
    send_cor[1] = jnp.broadcast_to(pext[pl.ds(edge_base + 8, 1), :],
                                   (corner_rows, wide)).astype(jnp.bfloat16)

    pl.semaphore_wait(barrier, 1 + 2 * has_left + 2 * has_right)
    pairs = ((send_col.at[0], recv_col.at[0]), (send_col.at[1], recv_col.at[1]),
             (send_cor.at[0], recv_cor.at[0]), (send_cor.at[1], recv_cor.at[1]),
             (send_row, recv_row))
    copies = [
        pltpu.make_async_remote_copy(src_ref, dst_ref, send_sem.at[slot], recv_sem.at[slot],
                                     device_id=peers[slot], device_id_type=mesh_id)
        for slot, (src_ref, dst_ref) in enumerate(pairs)
    ]
    product_copy = pltpu.make_async_remote_copy(
        own_b, prev_b, send_sem.at[5], recv_sem.at[5], device_id=peers[5],
        device_id_type=mesh_id)
    send_when = (c < ncol - 1, c > 0, c < ncol - 1, c > 0, None)
    recv_when = (c > 0, c < ncol - 1, c > 0, c < ncol - 1, None)

    def guarded(cond, fn):
        if cond is None:
            fn()
        else:
            pl.when(cond)(fn)

    for cp, cond in zip(copies, send_when):
        guarded(cond, cp.start)
    for cp in loads[4:]:
        cp.wait()
    for lag in range(2 * rows):
        fb[lag] = jnp.broadcast_to(filt_ref[lag : lag + 1, :].astype(jnp.float32), (8, width))
    copies[4].wait_send()
    copies[4].wait_recv()
    halo_base = pl.multiple_of(partner * (rows + 1) * pitch, 8)
    pext[pl.ds(halo_base + 8, span), :] = recv_row[...].astype(jnp.float32)

    def shift_body(i, carry):
        window = pext[pl.ds(pl.multiple_of(i * pitch, 8), pitch), :]
        dst = pl.ds(pl.multiple_of(i * span, 8), span)
        shifted[0, dst, :] = window[7 : 7 + span]
        shifted[1, dst, :] = window[8 : 8 + span]
        shifted[2, dst, :] = window[9 : 9 + span]
        return carry

    def depthwise(i, w0, size):
        res = []
        for grp in range(3):
            lanes = pl.ds(grp * width, width)
            acc = bb[0:size, lanes]
            for a in range(3):
                src = pl.ds(pl.multiple_of((i + a) * span, 8) + w0, size)
                for b in range(3):
                    acc = acc + shifted[b, src, lanes] * kb[a * 3 + b, 0:size, lanes]
            res.append(acc.astype(jnp.bfloat16).astype(jnp.float32))
        qf[pl.ds(pl.multiple_of(i * span, 8) + w0, size), :] = res[0]
        ext[pl.ds(pl.multiple_of(count + i * span, 8) + w0, size), :] = (
            (res[1] * res[2]).astype(jnp.bfloat16).astype(jnp.float32))

    def inner_body(i, carry):
        depthwise(i, 8, span - 16)
        return carry

    def outer_body(i, carry):
        depthwise(i, 0, 8)
        depthwise(i, span - 8, 8)
        return carry

    lane_groups = width // 128
    chunks = (span // 8) * lane_groups

    def own_pass(i, carry):
        lanes = pl.ds(pl.multiple_of((i % lane_groups) * 128, 128), 128)
        w0 = pl.multiple_of((i // lane_groups) * 8, 8)
        acc = [None] * rows
        for src in range(rows, 2 * rows):
            x = ext[pl.ds(src * span + w0, 8), lanes]
            for a in range(src - rows, rows):
                term = fb[rows + a - src, :, lanes] * x
                acc[a] = term if acc[a] is None else acc[a] + term
        for a in range(rows):
            gated[pl.ds(a * span + w0, 8), lanes] = acc[a]
        return carry

    lax.fori_loop(0, rows + 2, shift_body, 0)
    lax.fori_loop(0, rows, inner_body, 0)
    lax.fori_loop(lane_groups, chunks - lane_groups, own_pass, 0)

    for cp, cond in zip(copies[:4], send_when[:4]):
        guarded(cond, cp.wait_send)
    for cp, cond in zip(copies[:4], recv_when[:4]):
        guarded(cond, cp.wait_recv)
    stage[0] = recv_col[0].astype(jnp.float32)
    stage[1] = recv_col[1].astype(jnp.float32)
    for i in range(rows):
        pext[pl.ds((1 + i) * pitch + 7, 1), :] = stage[0, i : i + 1, :]
        pext[pl.ds((1 + i) * pitch + 8 + span, 1), :] = stage[1, i : i + 1, :]
    pext[pl.ds(halo_base + 7, 1), :] = recv_cor[0, 0:1, :].astype(jnp.float32)
    pext[pl.ds(halo_base + 8 + span, 1), :] = recv_cor[1, 0:1, :].astype(jnp.float32)
    lax.fori_loop(0, rows + 2, shift_body, 0)
    lax.fori_loop(0, rows, outer_body, 0)
    own_b[...] = ext[count : 2 * count, :].astype(jnp.bfloat16)

    @pl.when(r == 0)
    def _():
        product_copy.start()

    lax.fori_loop(0, lane_groups, own_pass, 0)
    lax.fori_loop(chunks - lane_groups, chunks, own_pass, 0)

    @pl.when(r == 0)
    def _():
        product_copy.wait_send()
        ext[0:count, :] = jnp.zeros((count, width), jnp.float32)

    @pl.when(r == 1)
    def _():
        product_copy.wait_recv()
        ext[0:count, :] = prev_b[...].astype(jnp.float32)

    def prev_pass(i, carry):
        lanes = pl.ds(pl.multiple_of((i % lane_groups) * 128, 128), 128)
        w0 = pl.multiple_of((i // lane_groups) * 8, 8)
        acc = [gated[pl.ds(a * span + w0, 8), lanes] for a in range(rows)]
        for src in range(rows):
            x = ext[pl.ds(src * span + w0, 8), lanes]
            for a in range(rows):
                acc[a] = acc[a] + fb[rows + a - src, :, lanes] * x
        gain = jnp.broadcast_to(gain_ref[lanes].reshape(1, 128), (8, 128))
        for a in range(rows):
            own = ext[pl.ds(count + a * span + w0, 8), lanes]
            q = qf[pl.ds(a * span + w0, 8), lanes]
            gated[pl.ds(a * span + w0, 8), lanes] = q * (acc[a] + gain * own)
        return carry

    lax.fori_loop(0, (span // 8) * lane_groups, prev_pass, 0)
    out_ref[...] = gated[...].astype(out_ref.dtype)


def project_kernel(g_hbm, w_hbm, out_ref, g_ref, w_ref, sem):
    loads = [pltpu.make_async_copy(g_hbm, g_ref, sem.at[0]),
             pltpu.make_async_copy(w_hbm, w_ref, sem.at[1])]
    for cp in loads:
        cp.start()
    for cp in loads:
        cp.wait()
    out_ref[...] = jnp.dot(
        g_ref[...], w_ref[...], preferred_element_type=jnp.float32
    ).astype(out_ref.dtype)


def on_device(image_tokens, w_in, conv_kernel, conv_bias, long_filter, skip_gain, w_out):
    row_count, col_count, width = image_tokens.shape
    pitch = 48
    flat = row_count * col_count
    wide = w_in.shape[1]
    vmem = pl.BlockSpec(memory_space=pltpu.VMEM)
    out = pl.pallas_call(
        functools.partial(layer_kernel, row_count, col_count, pitch),
        out_shape=jax.ShapeDtypeStruct((flat, width), jnp.bfloat16),
        in_specs=[pl.BlockSpec(memory_space=pl.ANY)] * 7,
        out_specs=vmem,
        scratch_shapes=[
            pltpu.VMEM((flat, width), jnp.bfloat16),
            pltpu.VMEM(w_in.shape, jnp.bfloat16),
            pltpu.VMEM(conv_kernel.shape, jnp.bfloat16),
            pltpu.VMEM(conv_bias.shape, jnp.float32),
            pltpu.VMEM(long_filter.shape, jnp.bfloat16),
            pltpu.VMEM(skip_gain.shape, jnp.float32),
            pltpu.VMEM(w_out.shape, jnp.bfloat16),
            pltpu.SemaphoreType.DMA((7,)),
            pltpu.VMEM(((row_count + 2) * pitch, wide), jnp.float32),
            pltpu.VMEM((3, (row_count + 2) * col_count, wide), jnp.float32),
            pltpu.VMEM((9, col_count, wide), jnp.float32),
            pltpu.VMEM((col_count, wide), jnp.float32),
            pltpu.VMEM((2, row_count, wide), jnp.bfloat16),
            pltpu.VMEM((2, row_count, wide), jnp.bfloat16),
            pltpu.VMEM((col_count, wide), jnp.bfloat16),
            pltpu.VMEM((flat, width), jnp.bfloat16),
            pltpu.VMEM((flat, width), jnp.bfloat16),
            pltpu.VMEM((2, row_count, wide), jnp.float32),
            pltpu.VMEM((col_count, wide), jnp.bfloat16),
            pltpu.VMEM((2, 16, wide), jnp.bfloat16),
            pltpu.VMEM((2, 16, wide), jnp.bfloat16),
            pltpu.VMEM((2 * flat, width), jnp.float32),
            pltpu.VMEM((2 * row_count, 8, width), jnp.float32),
            pltpu.VMEM((flat, width), jnp.float32),
            pltpu.VMEM((flat, width), jnp.float32),
            pltpu.SemaphoreType.DMA((6,)),
            pltpu.SemaphoreType.DMA((6,)),
        ],
        compiler_params=pltpu.CompilerParams(
            collective_id=0, has_side_effects=True, vmem_limit_bytes=67043328
        ),
    )(
        image_tokens.reshape(flat, width),
        w_in,
        conv_kernel,
        conv_bias,
        long_filter,
        skip_gain,
        w_out,
    )
    out = pl.pallas_call(
        project_kernel,
        out_shape=jax.ShapeDtypeStruct((flat, width), jnp.bfloat16),
        in_specs=[pl.BlockSpec(memory_space=pl.ANY)] * 2,
        out_specs=vmem,
        scratch_shapes=[
            pltpu.VMEM((flat, width), jnp.bfloat16),
            pltpu.VMEM(w_out.shape, jnp.bfloat16),
            pltpu.SemaphoreType.DMA((2,)),
        ],
    )(out, w_out)
    return out.reshape(row_count, col_count, width)


def solution(mesh):
    in_specs = (P("row", "col", None), P(), P(), P(), P(), P(), P())
    out_specs = P("row", "col", None)
    return jax.shard_map(
        on_device, mesh=mesh, in_specs=in_specs, out_specs=out_specs, check_vma=False
    )
```

```python
import functools

import jax
import jax.numpy as jnp
from jax import lax
from jax.experimental import pallas as pl
from jax.experimental.pallas import tpu as pltpu
from jax.sharding import PartitionSpec as P


def layer_kernel(rows, span, pitch, x_hbm, w_hbm, k_hbm, b_hbm, filt_hbm, gain_hbm, wout_hbm,
                 out_ref, x_ref, w_ref, k_ref, b_ref, filt_ref, gain_ref, wout_ref, load_sem, pext,
                 shifted, kb, bb, send_col, recv_col, recv_row, own_b, prev_b, stage, send_row,
                 send_cor, recv_cor, ext, fb, qf, gated, send_sem, recv_sem):
    width = out_ref.shape[1]
    wide = w_ref.shape[1]
    count = rows * span
    r = lax.axis_index("row")
    c = lax.axis_index("col")
    ncol = lax.axis_size("col")
    partner = 1 - r
    edge = partner * (rows - 1)
    mesh_id = pl.DeviceIdType.MESH
    right = lax.rem(c + 1, ncol)
    left = lax.rem(c + ncol - 1, ncol)
    peers = ((r, right), (r, left), (partner, right), (partner, left), (partner, c), (partner, c))

    recv_col[...] = jnp.zeros_like(recv_col)
    recv_cor[...] = jnp.zeros_like(recv_cor)
    barrier = pltpu.get_barrier_semaphore()
    conds = (c < ncol - 1, c > 0, c < ncol - 1, c > 0)
    for dev, cond in zip(peers[:4], conds):
        @pl.when(cond)
        def _():
            pl.semaphore_signal(barrier, 1, device_id=dev, device_id_type=mesh_id)
    pl.semaphore_signal(barrier, 1, device_id=peers[4], device_id_type=mesh_id)
    has_left = (c + ncol - 1) // ncol
    has_right = (2 * ncol - 3 - c) // (ncol - 1)

    loads = [
        pltpu.make_async_copy(src, dst, load_sem.at[i])
        for i, (src, dst) in enumerate((
            (x_hbm, x_ref), (w_hbm, w_ref), (k_hbm, k_ref), (b_hbm, b_ref),
            (filt_hbm, filt_ref), (gain_hbm, gain_ref), (wout_hbm, wout_ref)))
    ]
    for cp in loads:
        cp.start()
    for cp in loads[:4]:
        cp.wait()
    for i in range(9):
        kb[i] = jnp.broadcast_to(
            k_ref[i // 3, i % 3 : i % 3 + 1, :].astype(jnp.float32), (span, wide))
    bb[...] = jnp.broadcast_to(b_ref[...].reshape(1, wide), (span, wide))
    proj = jnp.dot(x_ref[...], w_ref[...], preferred_element_type=jnp.float32)
    proj = proj.astype(jnp.bfloat16).astype(jnp.float32)
    for i in range(rows):
        pext[pl.ds((1 + i) * pitch + 8, span), :] = proj[i * span : (i + 1) * span]
    other_row = r * (rows + 1)
    pext[pl.ds(pl.multiple_of(other_row * pitch, 8), pitch), :] = jnp.zeros((pitch, wide),
                                                                            jnp.float32)
    for i in range(rows):
        stage[0, i : i + 1, :] = pext[pl.ds((1 + i) * pitch + 8 + span - 1, 1), :]
        stage[1, i : i + 1, :] = pext[pl.ds((1 + i) * pitch + 8, 1), :]
    send_col[0] = stage[0].astype(jnp.bfloat16)
    send_col[1] = stage[1].astype(jnp.bfloat16)
    edge_base = pl.multiple_of((1 + edge) * pitch, 8)
    send_row[...] = pext[pl.ds(edge_base + 8, span), :].astype(jnp.bfloat16)
    corner_rows = send_cor.shape[1]
    send_cor[0] = jnp.broadcast_to(pext[pl.ds(edge_base + 8 + span - 1, 1), :],
                                   (corner_rows, wide)).astype(jnp.bfloat16)
    send_cor[1] = jnp.broadcast_to(pext[pl.ds(edge_base + 8, 1), :],
                                   (corner_rows, wide)).astype(jnp.bfloat16)

    pl.semaphore_wait(barrier, 1 + 2 * has_left + 2 * has_right)
    pairs = ((send_col.at[0], recv_col.at[0]), (send_col.at[1], recv_col.at[1]),
             (send_cor.at[0], recv_cor.at[0]), (send_cor.at[1], recv_cor.at[1]),
             (send_row, recv_row))
    copies = [
        pltpu.make_async_remote_copy(src_ref, dst_ref, send_sem.at[slot], recv_sem.at[slot],
                                     device_id=peers[slot], device_id_type=mesh_id)
        for slot, (src_ref, dst_ref) in enumerate(pairs)
    ]
    product_copy = pltpu.make_async_remote_copy(
        own_b, prev_b, send_sem.at[5], recv_sem.at[5], device_id=peers[5],
        device_id_type=mesh_id)
    send_when = (c < ncol - 1, c > 0, c < ncol - 1, c > 0, None)
    recv_when = (c > 0, c < ncol - 1, c > 0, c < ncol - 1, None)

    def guarded(cond, fn):
        if cond is None:
            fn()
        else:
            pl.when(cond)(fn)

    for cp, cond in zip(copies, send_when):
        guarded(cond, cp.start)
    for cp in loads[4:]:
        cp.wait()
    for lag in range(2 * rows):
        fb[lag] = jnp.broadcast_to(filt_ref[lag : lag + 1, :].astype(jnp.float32), (8, width))
    copies[4].wait_send()
    copies[4].wait_recv()
    halo_base = pl.multiple_of(partner * (rows + 1) * pitch, 8)
    pext[pl.ds(halo_base + 8, span), :] = recv_row[...].astype(jnp.float32)

    def shift_body(i, carry):
        window = pext[pl.ds(pl.multiple_of(i * pitch, 8), pitch), :]
        dst = pl.ds(pl.multiple_of(i * span, 8), span)
        shifted[0, dst, :] = window[7 : 7 + span]
        shifted[1, dst, :] = window[8 : 8 + span]
        shifted[2, dst, :] = window[9 : 9 + span]
        return carry

    def depthwise(i, w0, size):
        res = []
        for grp in range(3):
            lanes = pl.ds(grp * width, width)
            acc = bb[0:size, lanes]
            for a in range(3):
                src = pl.ds(pl.multiple_of((i + a) * span, 8) + w0, size)
                for b in range(3):
                    acc = acc + shifted[b, src, lanes] * kb[a * 3 + b, 0:size, lanes]
            res.append(acc.astype(jnp.bfloat16).astype(jnp.float32))
        qf[pl.ds(pl.multiple_of(i * span, 8) + w0, size), :] = res[0]
        ext[pl.ds(pl.multiple_of(count + i * span, 8) + w0, size), :] = (
            (res[1] * res[2]).astype(jnp.bfloat16).astype(jnp.float32))

    def inner_body(i, carry):
        depthwise(i, 8, span - 16)
        return carry

    def outer_body(i, carry):
        depthwise(i, 0, 8)
        depthwise(i, span - 8, 8)
        return carry

    lane_groups = width // 128
    chunks = (span // 8) * lane_groups

    def own_pass(i, carry):
        lanes = pl.ds(pl.multiple_of((i % lane_groups) * 128, 128), 128)
        w0 = pl.multiple_of((i // lane_groups) * 8, 8)
        acc = [None] * rows
        for src in range(rows, 2 * rows):
            x = ext[pl.ds(src * span + w0, 8), lanes]
            for a in range(src - rows, rows):
                term = fb[rows + a - src, :, lanes] * x
                acc[a] = term if acc[a] is None else acc[a] + term
        for a in range(rows):
            gated[pl.ds(a * span + w0, 8), lanes] = acc[a]
        return carry

    lax.fori_loop(0, rows + 2, shift_body, 0)
    lax.fori_loop(0, rows, inner_body, 0)
    lax.fori_loop(lane_groups, chunks - lane_groups, own_pass, 0)

    for cp, cond in zip(copies[:4], send_when[:4]):
        guarded(cond, cp.wait_send)
    for cp, cond in zip(copies[:4], recv_when[:4]):
        guarded(cond, cp.wait_recv)
    stage[0] = recv_col[0].astype(jnp.float32)
    stage[1] = recv_col[1].astype(jnp.float32)
    for i in range(rows):
        pext[pl.ds((1 + i) * pitch + 7, 1), :] = stage[0, i : i + 1, :]
        pext[pl.ds((1 + i) * pitch + 8 + span, 1), :] = stage[1, i : i + 1, :]
    pext[pl.ds(halo_base + 7, 1), :] = recv_cor[0, 0:1, :].astype(jnp.float32)
    pext[pl.ds(halo_base + 8 + span, 1), :] = recv_cor[1, 0:1, :].astype(jnp.float32)
    lax.fori_loop(0, rows + 2, shift_body, 0)
    lax.fori_loop(0, rows, outer_body, 0)
    own_b[...] = ext[count : 2 * count, :].astype(jnp.bfloat16)

    @pl.when(r == 0)
    def _():
        product_copy.start()

    lax.fori_loop(0, lane_groups, own_pass, 0)
    lax.fori_loop(chunks - lane_groups, chunks, own_pass, 0)

    @pl.when(r == 0)
    def _():
        product_copy.wait_send()
        ext[0:count, :] = jnp.zeros((count, width), jnp.float32)

    @pl.when(r == 1)
    def _():
        product_copy.wait_recv()
        ext[0:count, :] = prev_b[...].astype(jnp.float32)

    def prev_pass(i, carry):
        lanes = pl.ds(pl.multiple_of((i % lane_groups) * 128, 128), 128)
        w0 = pl.multiple_of((i // lane_groups) * 8, 8)
        acc = [gated[pl.ds(a * span + w0, 8), lanes] for a in range(rows)]
        for src in range(rows):
            x = ext[pl.ds(src * span + w0, 8), lanes]
            for a in range(rows):
                acc[a] = acc[a] + fb[rows + a - src, :, lanes] * x
        gain = jnp.broadcast_to(gain_ref[lanes].reshape(1, 128), (8, 128))
        for a in range(rows):
            own = ext[pl.ds(count + a * span + w0, 8), lanes]
            q = qf[pl.ds(a * span + w0, 8), lanes]
            gated[pl.ds(a * span + w0, 8), lanes] = q * (acc[a] + gain * own)
        return carry

    lax.fori_loop(0, (span // 8) * lane_groups, prev_pass, 0)
    out_ref[...] = gated[...].astype(out_ref.dtype)


def on_device(image_tokens, w_in, conv_kernel, conv_bias, long_filter, skip_gain, w_out):
    row_count, col_count, width = image_tokens.shape
    pitch = 48
    flat = row_count * col_count
    wide = w_in.shape[1]
    vmem = pl.BlockSpec(memory_space=pltpu.VMEM)
    out = pl.pallas_call(
        functools.partial(layer_kernel, row_count, col_count, pitch),
        out_shape=jax.ShapeDtypeStruct((flat, width), jnp.bfloat16),
        in_specs=[pl.BlockSpec(memory_space=pl.ANY)] * 7,
        out_specs=vmem,
        scratch_shapes=[
            pltpu.VMEM((flat, width), jnp.bfloat16),
            pltpu.VMEM(w_in.shape, jnp.bfloat16),
            pltpu.VMEM(conv_kernel.shape, jnp.bfloat16),
            pltpu.VMEM(conv_bias.shape, jnp.float32),
            pltpu.VMEM(long_filter.shape, jnp.bfloat16),
            pltpu.VMEM(skip_gain.shape, jnp.float32),
            pltpu.VMEM(w_out.shape, jnp.bfloat16),
            pltpu.SemaphoreType.DMA((7,)),
            pltpu.VMEM(((row_count + 2) * pitch, wide), jnp.float32),
            pltpu.VMEM((3, (row_count + 2) * col_count, wide), jnp.float32),
            pltpu.VMEM((9, col_count, wide), jnp.float32),
            pltpu.VMEM((col_count, wide), jnp.float32),
            pltpu.VMEM((2, row_count, wide), jnp.bfloat16),
            pltpu.VMEM((2, row_count, wide), jnp.bfloat16),
            pltpu.VMEM((col_count, wide), jnp.bfloat16),
            pltpu.VMEM((flat, width), jnp.bfloat16),
            pltpu.VMEM((flat, width), jnp.bfloat16),
            pltpu.VMEM((2, row_count, wide), jnp.float32),
            pltpu.VMEM((col_count, wide), jnp.bfloat16),
            pltpu.VMEM((2, 16, wide), jnp.bfloat16),
            pltpu.VMEM((2, 16, wide), jnp.bfloat16),
            pltpu.VMEM((2 * flat, width), jnp.float32),
            pltpu.VMEM((2 * row_count, 8, width), jnp.float32),
            pltpu.VMEM((flat, width), jnp.float32),
            pltpu.VMEM((flat, width), jnp.float32),
            pltpu.SemaphoreType.DMA((6,)),
            pltpu.SemaphoreType.DMA((6,)),
        ],
        compiler_params=pltpu.CompilerParams(
            collective_id=0, has_side_effects=True, vmem_limit_bytes=67043328
        ),
    )(
        image_tokens.reshape(flat, width),
        w_in,
        conv_kernel,
        conv_bias,
        long_filter,
        skip_gain,
        w_out,
    )
    out = jnp.dot(out, w_out, preferred_element_type=jnp.float32).astype(jnp.bfloat16)
    return out.reshape(row_count, col_count, width)


def solution(mesh):
    in_specs = (P("row", "col", None), P(), P(), P(), P(), P(), P())
    out_specs = P("row", "col", None)
    return jax.shard_map(
        on_device, mesh=mesh, in_specs=in_specs, out_specs=out_specs, check_vma=False
    )
```

```python
import functools

import jax
import jax.numpy as jnp
from jax import lax
from jax.experimental import pallas as pl
from jax.experimental.pallas import tpu as pltpu
from jax.sharding import PartitionSpec as P


def layer_kernel(rows, span, pitch, x_hbm, w_hbm, k_hbm, b_hbm, filt_hbm, gain_hbm, wout_hbm,
                 out_ref, x_ref, w_ref, k_ref, b_ref, filt_ref, gain_ref, wout_ref, load_sem, pext,
                 shifted, kb, bb, send_col, recv_col, recv_row, stage, send_row,
                 send_cor, recv_cor, ext, fb, qf, gated, send_sem, recv_sem):
    width = out_ref.shape[1]
    wide = w_ref.shape[1]
    count = rows * span
    r = lax.axis_index("row")
    c = lax.axis_index("col")
    ncol = lax.axis_size("col")
    partner = 1 - r
    edge = partner * (rows - 1)
    mesh_id = pl.DeviceIdType.MESH
    right = lax.rem(c + 1, ncol)
    left = lax.rem(c + ncol - 1, ncol)
    peers = ((r, right), (r, left), (partner, right), (partner, left), (partner, c), (partner, c))

    recv_col[...] = jnp.zeros_like(recv_col)
    recv_cor[...] = jnp.zeros_like(recv_cor)
    barrier = pltpu.get_barrier_semaphore()
    conds = (c < ncol - 1, c > 0, c < ncol - 1, c > 0)
    for dev, cond in zip(peers[:4], conds):
        @pl.when(cond)
        def _():
            pl.semaphore_signal(barrier, 1, device_id=dev, device_id_type=mesh_id)
    pl.semaphore_signal(barrier, 1, device_id=peers[4], device_id_type=mesh_id)
    has_left = (c + ncol - 1) // ncol
    has_right = (2 * ncol - 3 - c) // (ncol - 1)

    loads = [
        pltpu.make_async_copy(src, dst, load_sem.at[i])
        for i, (src, dst) in enumerate((
            (x_hbm, x_ref), (w_hbm, w_ref), (k_hbm, k_ref), (b_hbm, b_ref),
            (filt_hbm, filt_ref), (gain_hbm, gain_ref), (wout_hbm, wout_ref)))
    ]
    for cp in loads:
        cp.start()
    for cp in loads[:4]:
        cp.wait()
    for i in range(9):
        kb[i] = jnp.broadcast_to(
            k_ref[i // 3, i % 3 : i % 3 + 1, :].astype(jnp.float32), (span, wide))
    bb[...] = jnp.broadcast_to(b_ref[...].reshape(1, wide), (span, wide))
    proj = jnp.dot(x_ref[...], w_ref[...], preferred_element_type=jnp.float32)
    proj = proj.astype(jnp.bfloat16).astype(jnp.float32)
    for i in range(rows):
        pext[pl.ds((1 + i) * pitch + 8, span), :] = proj[i * span : (i + 1) * span]
    other_row = r * (rows + 1)
    pext[pl.ds(pl.multiple_of(other_row * pitch, 8), pitch), :] = jnp.zeros((pitch, wide),
                                                                            jnp.float32)
    for i in range(rows):
        stage[0, i : i + 1, :] = pext[pl.ds((1 + i) * pitch + 8 + span - 1, 1), :]
        stage[1, i : i + 1, :] = pext[pl.ds((1 + i) * pitch + 8, 1), :]
    send_col[0] = stage[0].astype(jnp.bfloat16)
    send_col[1] = stage[1].astype(jnp.bfloat16)
    edge_base = pl.multiple_of((1 + edge) * pitch, 8)
    send_row[...] = pext[pl.ds(edge_base + 8, span), :].astype(jnp.bfloat16)
    corner_rows = send_cor.shape[1]
    send_cor[0] = jnp.broadcast_to(pext[pl.ds(edge_base + 8 + span - 1, 1), :],
                                   (corner_rows, wide)).astype(jnp.bfloat16)
    send_cor[1] = jnp.broadcast_to(pext[pl.ds(edge_base + 8, 1), :],
                                   (corner_rows, wide)).astype(jnp.bfloat16)

    pl.semaphore_wait(barrier, 1 + 2 * has_left + 2 * has_right)
    pairs = ((send_col.at[0], recv_col.at[0]), (send_col.at[1], recv_col.at[1]),
             (send_cor.at[0], recv_cor.at[0]), (send_cor.at[1], recv_cor.at[1]),
             (send_row, recv_row))
    copies = [
        pltpu.make_async_remote_copy(src_ref, dst_ref, send_sem.at[slot], recv_sem.at[slot],
                                     device_id=peers[slot], device_id_type=mesh_id)
        for slot, (src_ref, dst_ref) in enumerate(pairs)
    ]
    spans = ((8, span - 16), (0, 8), (span - 8, 8))
    product_copies = [
        pltpu.make_async_remote_copy(
            ext.at[pl.ds(rows, rows), pl.ds(w0, size), :],
            ext.at[pl.ds(0, rows), pl.ds(w0, size), :],
            send_sem.at[5 + k], recv_sem.at[5 + k], device_id=peers[5], device_id_type=mesh_id)
        for k, (w0, size) in enumerate(spans)
    ]
    send_when = (c < ncol - 1, c > 0, c < ncol - 1, c > 0, None)
    recv_when = (c > 0, c < ncol - 1, c > 0, c < ncol - 1, None)

    def guarded(cond, fn):
        if cond is None:
            fn()
        else:
            pl.when(cond)(fn)

    for cp, cond in zip(copies, send_when):
        guarded(cond, cp.start)
    for cp in loads[4:]:
        cp.wait()
    for lag in range(2 * rows):
        fb[lag] = jnp.broadcast_to(filt_ref[lag : lag + 1, :].astype(jnp.float32), (8, width))
    copies[4].wait_send()
    copies[4].wait_recv()
    halo_base = pl.multiple_of(partner * (rows + 1) * pitch, 8)
    pext[pl.ds(halo_base + 8, span), :] = recv_row[...].astype(jnp.float32)

    def shift_body(i, carry):
        window = pext[pl.ds(pl.multiple_of(i * pitch, 8), pitch), :]
        dst = pl.ds(pl.multiple_of(i * span, 8), span)
        shifted[0, dst, :] = window[7 : 7 + span]
        shifted[1, dst, :] = window[8 : 8 + span]
        shifted[2, dst, :] = window[9 : 9 + span]
        return carry

    def depthwise(i, w0, size):
        res = []
        for grp in range(3):
            lanes = pl.ds(grp * width, width)
            acc = bb[0:size, lanes]
            for a in range(3):
                src = pl.ds(pl.multiple_of((i + a) * span, 8) + w0, size)
                for b in range(3):
                    acc = acc + shifted[b, src, lanes] * kb[a * 3 + b, 0:size, lanes]
            res.append(acc.astype(jnp.bfloat16).astype(jnp.float32))
        qf[pl.ds(pl.multiple_of(i * span, 8) + w0, size), :] = res[0]
        ext[rows + i, pl.ds(w0, size), :] = (
            (res[1] * res[2]).astype(jnp.bfloat16).astype(jnp.float32))

    def inner_body(i, carry):
        depthwise(i, 8, span - 16)
        return carry

    def outer_body(i, carry):
        depthwise(i, 0, 8)
        depthwise(i, span - 8, 8)
        return carry

    lane_groups = width // 128
    chunks = (span // 8) * lane_groups

    def own_pass(i, carry):
        lanes = pl.ds(pl.multiple_of((i % lane_groups) * 128, 128), 128)
        w0 = pl.multiple_of((i // lane_groups) * 8, 8)
        acc = [None] * rows
        for src in range(rows, 2 * rows):
            x = ext[src, pl.ds(w0, 8), lanes]
            for a in range(src - rows, rows):
                term = fb[rows + a - src, :, lanes] * x
                acc[a] = term if acc[a] is None else acc[a] + term
        for a in range(rows):
            gated[pl.ds(a * span + w0, 8), lanes] = acc[a]
        return carry

    def prev_pass(i, carry):
        lanes = pl.ds(pl.multiple_of((i % lane_groups) * 128, 128), 128)
        w0 = pl.multiple_of((i // lane_groups) * 8, 8)
        acc = [gated[pl.ds(a * span + w0, 8), lanes] for a in range(rows)]
        for src in range(rows):
            x = ext[src, pl.ds(w0, 8), lanes]
            for a in range(rows):
                acc[a] = acc[a] + fb[rows + a - src, :, lanes] * x
        gain = jnp.broadcast_to(gain_ref[lanes].reshape(1, 128), (8, 128))
        for a in range(rows):
            own = ext[rows + a, pl.ds(w0, 8), lanes]
            q = qf[pl.ds(a * span + w0, 8), lanes]
            gated[pl.ds(a * span + w0, 8), lanes] = q * (acc[a] + gain * own)
        return carry

    @pl.when(r == 0)
    def _():
        ext[0:rows] = jnp.zeros((rows, span, width), jnp.float32)

    lax.fori_loop(0, rows + 2, shift_body, 0)
    lax.fori_loop(0, rows, inner_body, 0)

    @pl.when(r == 0)
    def _():
        product_copies[0].start()

    lax.fori_loop(lane_groups, chunks - lane_groups, own_pass, 0)

    @pl.when(r == 1)
    def _():
        product_copies[0].wait_recv()

    lax.fori_loop(lane_groups, chunks - lane_groups, prev_pass, 0)

    @pl.when(r == 0)
    def _():
        product_copies[0].wait_send()

    for cp, cond in zip(copies[:4], send_when[:4]):
        guarded(cond, cp.wait_send)
    for cp, cond in zip(copies[:4], recv_when[:4]):
        guarded(cond, cp.wait_recv)
    stage[0] = recv_col[0].astype(jnp.float32)
    stage[1] = recv_col[1].astype(jnp.float32)
    for i in range(rows):
        pext[pl.ds((1 + i) * pitch + 7, 1), :] = stage[0, i : i + 1, :]
        pext[pl.ds((1 + i) * pitch + 8 + span, 1), :] = stage[1, i : i + 1, :]
    pext[pl.ds(halo_base + 7, 1), :] = recv_cor[0, 0:1, :].astype(jnp.float32)
    pext[pl.ds(halo_base + 8 + span, 1), :] = recv_cor[1, 0:1, :].astype(jnp.float32)
    lax.fori_loop(0, rows + 2, shift_body, 0)
    lax.fori_loop(0, rows, outer_body, 0)

    @pl.when(r == 0)
    def _():
        product_copies[1].start()
        product_copies[2].start()

    lax.fori_loop(0, lane_groups, own_pass, 0)
    lax.fori_loop(chunks - lane_groups, chunks, own_pass, 0)

    @pl.when(r == 1)
    def _():
        product_copies[1].wait_recv()
        product_copies[2].wait_recv()

    lax.fori_loop(0, lane_groups, prev_pass, 0)
    lax.fori_loop(chunks - lane_groups, chunks, prev_pass, 0)

    @pl.when(r == 0)
    def _():
        for cp in product_copies[1:]:
            cp.wait_send()
    out_ref[...] = gated[...].astype(out_ref.dtype)


def on_device(image_tokens, w_in, conv_kernel, conv_bias, long_filter, skip_gain, w_out):
    row_count, col_count, width = image_tokens.shape
    pitch = 48
    flat = row_count * col_count
    wide = w_in.shape[1]
    vmem = pl.BlockSpec(memory_space=pltpu.VMEM)
    out = pl.pallas_call(
        functools.partial(layer_kernel, row_count, col_count, pitch),
        out_shape=jax.ShapeDtypeStruct((flat, width), jnp.bfloat16),
        in_specs=[pl.BlockSpec(memory_space=pl.ANY)] * 7,
        out_specs=vmem,
        scratch_shapes=[
            pltpu.VMEM((flat, width), jnp.bfloat16),
            pltpu.VMEM(w_in.shape, jnp.bfloat16),
            pltpu.VMEM(conv_kernel.shape, jnp.bfloat16),
            pltpu.VMEM(conv_bias.shape, jnp.float32),
            pltpu.VMEM(long_filter.shape, jnp.bfloat16),
            pltpu.VMEM(skip_gain.shape, jnp.float32),
            pltpu.VMEM(w_out.shape, jnp.bfloat16),
            pltpu.SemaphoreType.DMA((7,)),
            pltpu.VMEM(((row_count + 2) * pitch, wide), jnp.float32),
            pltpu.VMEM((3, (row_count + 2) * col_count, wide), jnp.float32),
            pltpu.VMEM((9, col_count, wide), jnp.float32),
            pltpu.VMEM((col_count, wide), jnp.float32),
            pltpu.VMEM((2, row_count, wide), jnp.bfloat16),
            pltpu.VMEM((2, row_count, wide), jnp.bfloat16),
            pltpu.VMEM((col_count, wide), jnp.bfloat16),
            pltpu.VMEM((2, row_count, wide), jnp.float32),
            pltpu.VMEM((col_count, wide), jnp.bfloat16),
            pltpu.VMEM((2, 16, wide), jnp.bfloat16),
            pltpu.VMEM((2, 16, wide), jnp.bfloat16),
            pltpu.VMEM((2 * row_count, col_count, width), jnp.float32),
            pltpu.VMEM((2 * row_count, 8, width), jnp.float32),
            pltpu.VMEM((flat, width), jnp.float32),
            pltpu.VMEM((flat, width), jnp.float32),
            pltpu.SemaphoreType.DMA((8,)),
            pltpu.SemaphoreType.DMA((8,)),
        ],
        compiler_params=pltpu.CompilerParams(
            collective_id=0, has_side_effects=True, vmem_limit_bytes=67043328
        ),
    )(
        image_tokens.reshape(flat, width),
        w_in,
        conv_kernel,
        conv_bias,
        long_filter,
        skip_gain,
        w_out,
    )
    out = jnp.dot(out, w_out, preferred_element_type=jnp.float32).astype(jnp.bfloat16)
    return out.reshape(row_count, col_count, width)


def solution(mesh):
    in_specs = (P("row", "col", None), P(), P(), P(), P(), P(), P())
    out_specs = P("row", "col", None)
    return jax.shard_map(
        on_device, mesh=mesh, in_specs=in_specs, out_specs=out_specs, check_vma=False
    )
```

```python
import functools

import jax
import jax.numpy as jnp
from jax import lax
from jax.experimental import pallas as pl
from jax.experimental.pallas import tpu as pltpu
from jax.sharding import PartitionSpec as P


def layer_kernel(rows, span, pitch, x_hbm, w_hbm, k_hbm, b_hbm, filt_hbm, gain_hbm, wout_hbm,
                 out_ref, x_ref, w_ref, k_ref, b_ref, filt_ref, gain_ref, wout_ref, load_sem, pext,
                 shifted, kb, bb, send_col, recv_col, recv_row, stage, send_row,
                 send_cor, recv_cor, ext, fb, qf, gated, send_sem, recv_sem):
    width = out_ref.shape[1]
    wide = w_ref.shape[1]
    count = rows * span
    r = lax.axis_index("row")
    c = lax.axis_index("col")
    ncol = lax.axis_size("col")
    partner = 1 - r
    edge = partner * (rows - 1)
    mesh_id = pl.DeviceIdType.MESH
    right = lax.rem(c + 1, ncol)
    left = lax.rem(c + ncol - 1, ncol)
    peers = ((r, right), (r, left), (partner, right), (partner, left), (partner, c), (partner, c))

    recv_col[...] = jnp.zeros_like(recv_col)
    recv_cor[...] = jnp.zeros_like(recv_cor)
    barrier = pltpu.get_barrier_semaphore()
    conds = (c < ncol - 1, c > 0, c < ncol - 1, c > 0)
    for dev, cond in zip(peers[:4], conds):
        @pl.when(cond)
        def _():
            pl.semaphore_signal(barrier, 1, device_id=dev, device_id_type=mesh_id)
    pl.semaphore_signal(barrier, 1, device_id=peers[4], device_id_type=mesh_id)
    has_left = (c + ncol - 1) // ncol
    has_right = (2 * ncol - 3 - c) // (ncol - 1)

    loads = [
        pltpu.make_async_copy(src, dst, load_sem.at[i])
        for i, (src, dst) in enumerate((
            (x_hbm, x_ref), (w_hbm, w_ref), (k_hbm, k_ref), (b_hbm, b_ref),
            (filt_hbm, filt_ref), (gain_hbm, gain_ref), (wout_hbm, wout_ref)))
    ]
    for cp in loads:
        cp.start()
    for cp in loads[:4]:
        cp.wait()
    for i in range(9):
        kb[i] = jnp.broadcast_to(
            k_ref[i // 3, i % 3 : i % 3 + 1, :].astype(jnp.float32), (span, wide))
    bb[...] = jnp.broadcast_to(b_ref[...].reshape(1, wide), (span, wide))
    proj = jnp.dot(x_ref[...], w_ref[...], preferred_element_type=jnp.float32)
    proj = proj.astype(jnp.bfloat16).astype(jnp.float32)
    for i in range(rows):
        pext[pl.ds((1 + i) * pitch + 8, span), :] = proj[i * span : (i + 1) * span]
    other_row = r * (rows + 1)
    pext[pl.ds(pl.multiple_of(other_row * pitch, 8), pitch), :] = jnp.zeros((pitch, wide),
                                                                            jnp.float32)
    for i in range(rows):
        stage[0, i : i + 1, :] = pext[pl.ds((1 + i) * pitch + 8 + span - 1, 1), :]
        stage[1, i : i + 1, :] = pext[pl.ds((1 + i) * pitch + 8, 1), :]
    send_col[0] = stage[0].astype(jnp.bfloat16)
    send_col[1] = stage[1].astype(jnp.bfloat16)
    edge_base = pl.multiple_of((1 + edge) * pitch, 8)
    send_row[...] = pext[pl.ds(edge_base + 8, span), :].astype(jnp.bfloat16)
    corner_rows = send_cor.shape[1]
    send_cor[0] = jnp.broadcast_to(pext[pl.ds(edge_base + 8 + span - 1, 1), :],
                                   (corner_rows, wide)).astype(jnp.bfloat16)
    send_cor[1] = jnp.broadcast_to(pext[pl.ds(edge_base + 8, 1), :],
                                   (corner_rows, wide)).astype(jnp.bfloat16)

    def shift_body(i, carry):
        window = pext[pl.ds(pl.multiple_of(i * pitch, 8), pitch), :]
        dst = pl.ds(pl.multiple_of(i * span, 8), span)
        shifted[0, dst, :] = window[7 : 7 + span]
        shifted[1, dst, :] = window[8 : 8 + span]
        shifted[2, dst, :] = window[9 : 9 + span]
        return carry

    def depthwise(i, w0, size):
        res = []
        for grp in range(3):
            lanes = pl.ds(grp * width, width)
            acc = bb[0:size, lanes]
            for a in range(3):
                src = pl.ds(pl.multiple_of((i + a) * span, 8) + w0, size)
                for b in range(3):
                    acc = acc + shifted[b, src, lanes] * kb[a * 3 + b, 0:size, lanes]
            res.append(acc.astype(jnp.bfloat16).astype(jnp.float32))
        qf[pl.ds(pl.multiple_of(i * span, 8) + w0, size), :] = res[0]
        ext[rows + i, pl.ds(w0, size), :] = (
            (res[1] * res[2]).astype(jnp.bfloat16).astype(jnp.float32))

    def inner_body(i, carry):
        depthwise(i, 8, span - 16)
        return carry

    lax.fori_loop(0, rows + 2, shift_body, 0)
    lax.fori_loop(r, r + rows - 1, inner_body, 0)

    pl.semaphore_wait(barrier, 1 + 2 * has_left + 2 * has_right)
    pairs = ((send_col.at[0], recv_col.at[0]), (send_col.at[1], recv_col.at[1]),
             (send_cor.at[0], recv_cor.at[0]), (send_cor.at[1], recv_cor.at[1]),
             (send_row, recv_row))
    copies = [
        pltpu.make_async_remote_copy(src_ref, dst_ref, send_sem.at[slot], recv_sem.at[slot],
                                     device_id=peers[slot], device_id_type=mesh_id)
        for slot, (src_ref, dst_ref) in enumerate(pairs)
    ]
    spans = ((8, span - 16), (0, 8), (span - 8, 8))
    product_copies = [
        pltpu.make_async_remote_copy(
            ext.at[pl.ds(rows, rows), pl.ds(w0, size), :],
            ext.at[pl.ds(0, rows), pl.ds(w0, size), :],
            send_sem.at[5 + k], recv_sem.at[5 + k], device_id=peers[5], device_id_type=mesh_id)
        for k, (w0, size) in enumerate(spans)
    ]
    send_when = (c < ncol - 1, c > 0, c < ncol - 1, c > 0, None)
    recv_when = (c > 0, c < ncol - 1, c > 0, c < ncol - 1, None)

    def guarded(cond, fn):
        if cond is None:
            fn()
        else:
            pl.when(cond)(fn)

    for cp, cond in zip(copies, send_when):
        guarded(cond, cp.start)
    for cp in loads[4:]:
        cp.wait()
    for lag in range(2 * rows):
        fb[lag] = jnp.broadcast_to(filt_ref[lag : lag + 1, :].astype(jnp.float32), (8, width))
    copies[4].wait_send()
    copies[4].wait_recv()
    halo_base = pl.multiple_of(partner * (rows + 1) * pitch, 8)
    pext[pl.ds(halo_base + 8, span), :] = recv_row[...].astype(jnp.float32)

    def outer_body(i, carry):
        depthwise(i, 0, 8)
        depthwise(i, span - 8, 8)
        return carry

    lane_groups = width // 128
    chunks = (span // 8) * lane_groups

    def own_pass(i, carry):
        lanes = pl.ds(pl.multiple_of((i % lane_groups) * 128, 128), 128)
        w0 = pl.multiple_of((i // lane_groups) * 8, 8)
        acc = [None] * rows
        for src in range(rows, 2 * rows):
            x = ext[src, pl.ds(w0, 8), lanes]
            for a in range(src - rows, rows):
                term = fb[rows + a - src, :, lanes] * x
                acc[a] = term if acc[a] is None else acc[a] + term
        for a in range(rows):
            gated[pl.ds(a * span + w0, 8), lanes] = acc[a]
        return carry

    def prev_pass(i, carry):
        lanes = pl.ds(pl.multiple_of((i % lane_groups) * 128, 128), 128)
        w0 = pl.multiple_of((i // lane_groups) * 8, 8)
        acc = [gated[pl.ds(a * span + w0, 8), lanes] for a in range(rows)]
        for src in range(rows):
            x = ext[src, pl.ds(w0, 8), lanes]
            for a in range(rows):
                acc[a] = acc[a] + fb[rows + a - src, :, lanes] * x
        gain = jnp.broadcast_to(gain_ref[lanes].reshape(1, 128), (8, 128))
        for a in range(rows):
            own = ext[rows + a, pl.ds(w0, 8), lanes]
            q = qf[pl.ds(a * span + w0, 8), lanes]
            gated[pl.ds(a * span + w0, 8), lanes] = q * (acc[a] + gain * own)
        return carry

    @pl.when(r == 0)
    def _():
        ext[0:rows] = jnp.zeros((rows, span, width), jnp.float32)

    shift_body(partner * (rows + 1), 0)
    inner_body(partner * (rows - 1), 0)

    @pl.when(r == 0)
    def _():
        product_copies[0].start()

    lax.fori_loop(lane_groups, chunks - lane_groups, own_pass, 0)

    @pl.when(r == 1)
    def _():
        product_copies[0].wait_recv()

    lax.fori_loop(lane_groups, chunks - lane_groups, prev_pass, 0)

    @pl.when(r == 0)
    def _():
        product_copies[0].wait_send()

    for cp, cond in zip(copies[:4], send_when[:4]):
        guarded(cond, cp.wait_send)
    for cp, cond in zip(copies[:4], recv_when[:4]):
        guarded(cond, cp.wait_recv)
    stage[0] = recv_col[0].astype(jnp.float32)
    stage[1] = recv_col[1].astype(jnp.float32)
    for i in range(rows):
        pext[pl.ds((1 + i) * pitch + 7, 1), :] = stage[0, i : i + 1, :]
        pext[pl.ds((1 + i) * pitch + 8 + span, 1), :] = stage[1, i : i + 1, :]
    pext[pl.ds(halo_base + 7, 1), :] = recv_cor[0, 0:1, :].astype(jnp.float32)
    pext[pl.ds(halo_base + 8 + span, 1), :] = recv_cor[1, 0:1, :].astype(jnp.float32)
    lax.fori_loop(0, rows + 2, shift_body, 0)
    lax.fori_loop(0, rows, outer_body, 0)

    @pl.when(r == 0)
    def _():
        product_copies[1].start()
        product_copies[2].start()

    lax.fori_loop(0, lane_groups, own_pass, 0)
    lax.fori_loop(chunks - lane_groups, chunks, own_pass, 0)

    @pl.when(r == 1)
    def _():
        product_copies[1].wait_recv()
        product_copies[2].wait_recv()

    lax.fori_loop(0, lane_groups, prev_pass, 0)
    lax.fori_loop(chunks - lane_groups, chunks, prev_pass, 0)

    @pl.when(r == 0)
    def _():
        for cp in product_copies[1:]:
            cp.wait_send()
    out_ref[...] = gated[...].astype(out_ref.dtype)


def on_device(image_tokens, w_in, conv_kernel, conv_bias, long_filter, skip_gain, w_out):
    row_count, col_count, width = image_tokens.shape
    pitch = 48
    flat = row_count * col_count
    wide = w_in.shape[1]
    vmem = pl.BlockSpec(memory_space=pltpu.VMEM)
    out = pl.pallas_call(
        functools.partial(layer_kernel, row_count, col_count, pitch),
        out_shape=jax.ShapeDtypeStruct((flat, width), jnp.bfloat16),
        in_specs=[pl.BlockSpec(memory_space=pl.ANY)] * 7,
        out_specs=vmem,
        scratch_shapes=[
            pltpu.VMEM((flat, width), jnp.bfloat16),
            pltpu.VMEM(w_in.shape, jnp.bfloat16),
            pltpu.VMEM(conv_kernel.shape, jnp.bfloat16),
            pltpu.VMEM(conv_bias.shape, jnp.float32),
            pltpu.VMEM(long_filter.shape, jnp.bfloat16),
            pltpu.VMEM(skip_gain.shape, jnp.float32),
            pltpu.VMEM(w_out.shape, jnp.bfloat16),
            pltpu.SemaphoreType.DMA((7,)),
            pltpu.VMEM(((row_count + 2) * pitch, wide), jnp.float32),
            pltpu.VMEM((3, (row_count + 2) * col_count, wide), jnp.float32),
            pltpu.VMEM((9, col_count, wide), jnp.float32),
            pltpu.VMEM((col_count, wide), jnp.float32),
            pltpu.VMEM((2, row_count, wide), jnp.bfloat16),
            pltpu.VMEM((2, row_count, wide), jnp.bfloat16),
            pltpu.VMEM((col_count, wide), jnp.bfloat16),
            pltpu.VMEM((2, row_count, wide), jnp.float32),
            pltpu.VMEM((col_count, wide), jnp.bfloat16),
            pltpu.VMEM((2, 16, wide), jnp.bfloat16),
            pltpu.VMEM((2, 16, wide), jnp.bfloat16),
            pltpu.VMEM((2 * row_count, col_count, width), jnp.float32),
            pltpu.VMEM((2 * row_count, 8, width), jnp.float32),
            pltpu.VMEM((flat, width), jnp.float32),
            pltpu.VMEM((flat, width), jnp.float32),
            pltpu.SemaphoreType.DMA((8,)),
            pltpu.SemaphoreType.DMA((8,)),
        ],
        compiler_params=pltpu.CompilerParams(
            collective_id=0, has_side_effects=True, vmem_limit_bytes=67043328
        ),
    )(
        image_tokens.reshape(flat, width),
        w_in,
        conv_kernel,
        conv_bias,
        long_filter,
        skip_gain,
        w_out,
    )
    out = jnp.dot(out, w_out, preferred_element_type=jnp.float32).astype(jnp.bfloat16)
    return out.reshape(row_count, col_count, width)


def solution(mesh):
    in_specs = (P("row", "col", None), P(), P(), P(), P(), P(), P())
    out_specs = P("row", "col", None)
    return jax.shard_map(
        on_device, mesh=mesh, in_specs=in_specs, out_specs=out_specs, check_vma=False
    )
```

```python
import functools

import jax
import jax.numpy as jnp
from jax import lax
from jax.experimental import pallas as pl
from jax.experimental.pallas import tpu as pltpu
from jax.sharding import PartitionSpec as P


def layer_kernel(rows, span, pitch, x_hbm, w_hbm, k_hbm, b_hbm, filt_hbm, gain_hbm, wout_hbm,
                 out_ref, x_ref, w_ref, k_ref, b_ref, filt_ref, gain_ref, wout_ref, load_sem, pext,
                 shifted, kb, bb, send_col, recv_col, recv_row, stage, send_row,
                 send_cor, recv_cor, ext, fb, qf, gated, send_sem, recv_sem):
    width = out_ref.shape[1]
    wide = w_ref.shape[1]
    count = rows * span
    r = lax.axis_index("row")
    c = lax.axis_index("col")
    ncol = lax.axis_size("col")
    partner = 1 - r
    edge = partner * (rows - 1)
    mesh_id = pl.DeviceIdType.MESH
    right = lax.rem(c + 1, ncol)
    left = lax.rem(c + ncol - 1, ncol)
    peers = ((r, right), (r, left), (partner, right), (partner, left), (partner, c), (partner, c))

    recv_col[...] = jnp.zeros_like(recv_col)
    recv_cor[...] = jnp.zeros_like(recv_cor)
    barrier = pltpu.get_barrier_semaphore()
    conds = (c < ncol - 1, c > 0, c < ncol - 1, c > 0)
    for dev, cond in zip(peers[:4], conds):
        @pl.when(cond)
        def _():
            pl.semaphore_signal(barrier, 1, device_id=dev, device_id_type=mesh_id)
    pl.semaphore_signal(barrier, 1, device_id=peers[4], device_id_type=mesh_id)
    has_left = (c + ncol - 1) // ncol
    has_right = (2 * ncol - 3 - c) // (ncol - 1)

    loads = [
        pltpu.make_async_copy(src, dst, load_sem.at[i])
        for i, (src, dst) in enumerate((
            (x_hbm, x_ref), (w_hbm, w_ref), (k_hbm, k_ref), (b_hbm, b_ref),
            (filt_hbm, filt_ref), (gain_hbm, gain_ref), (wout_hbm, wout_ref)))
    ]
    for cp in loads:
        cp.start()
    for cp in loads[:4]:
        cp.wait()
    for i in range(9):
        kb[i] = jnp.broadcast_to(
            k_ref[i // 3, i % 3 : i % 3 + 1, :].astype(jnp.float32), (span, wide))
    bb[...] = jnp.broadcast_to(b_ref[...].reshape(1, wide), (span, wide))
    proj = jnp.dot(x_ref[...], w_ref[...], preferred_element_type=jnp.float32)
    proj = proj.astype(jnp.bfloat16).astype(jnp.float32)
    for i in range(rows):
        pext[pl.ds((1 + i) * pitch + 8, span), :] = proj[i * span : (i + 1) * span]
    other_row = r * (rows + 1)
    pext[pl.ds(pl.multiple_of(other_row * pitch, 8), pitch), :] = jnp.zeros((pitch, wide),
                                                                            jnp.float32)
    for i in range(rows):
        stage[0, i : i + 1, :] = pext[pl.ds((1 + i) * pitch + 8 + span - 1, 1), :]
        stage[1, i : i + 1, :] = pext[pl.ds((1 + i) * pitch + 8, 1), :]
    send_col[0] = stage[0].astype(jnp.bfloat16)
    send_col[1] = stage[1].astype(jnp.bfloat16)
    edge_base = pl.multiple_of((1 + edge) * pitch, 8)
    send_row[...] = pext[pl.ds(edge_base + 8, span), :].astype(jnp.bfloat16)
    corner_rows = send_cor.shape[1]
    send_cor[0] = jnp.broadcast_to(pext[pl.ds(edge_base + 8 + span - 1, 1), :],
                                   (corner_rows, wide)).astype(jnp.bfloat16)
    send_cor[1] = jnp.broadcast_to(pext[pl.ds(edge_base + 8, 1), :],
                                   (corner_rows, wide)).astype(jnp.bfloat16)

    pl.semaphore_wait(barrier, 1 + 2 * has_left + 2 * has_right)
    pairs = ((send_col.at[0], recv_col.at[0]), (send_col.at[1], recv_col.at[1]),
             (send_cor.at[0], recv_cor.at[0]), (send_cor.at[1], recv_cor.at[1]),
             (send_row, recv_row))
    copies = [
        pltpu.make_async_remote_copy(src_ref, dst_ref, send_sem.at[slot], recv_sem.at[slot],
                                     device_id=peers[slot], device_id_type=mesh_id)
        for slot, (src_ref, dst_ref) in enumerate(pairs)
    ]
    product_copies = [
        pltpu.make_async_remote_copy(
            ext.at[pl.ds(rows, rows), pl.ds(8, span - 16), :],
            ext.at[pl.ds(0, rows), pl.ds(8, span - 16), :],
            send_sem.at[5], recv_sem.at[5], device_id=peers[5], device_id_type=mesh_id)
    ]
    pieces = rows // 8

    def edge_copy(k, side):
        w0 = side * (span - 8)
        slot = 6 + 2 * k + side
        return pltpu.make_async_remote_copy(
            ext.at[pl.ds(rows + 8 * k, 8), pl.ds(w0, 8), :],
            ext.at[pl.ds(8 * k, 8), pl.ds(w0, 8), :],
            send_sem.at[slot], recv_sem.at[slot], device_id=peers[5], device_id_type=mesh_id)
    send_when = (c < ncol - 1, c > 0, c < ncol - 1, c > 0, None)
    recv_when = (c > 0, c < ncol - 1, c > 0, c < ncol - 1, None)

    def guarded(cond, fn):
        if cond is None:
            fn()
        else:
            pl.when(cond)(fn)

    for cp, cond in zip(copies, send_when):
        guarded(cond, cp.start)
    for cp in loads[4:]:
        cp.wait()
    for lag in range(2 * rows):
        fb[lag] = jnp.broadcast_to(filt_ref[lag : lag + 1, :].astype(jnp.float32), (8, width))
    copies[4].wait_send()
    copies[4].wait_recv()
    halo_base = pl.multiple_of(partner * (rows + 1) * pitch, 8)
    pext[pl.ds(halo_base + 8, span), :] = recv_row[...].astype(jnp.float32)

    def shift_body(i, carry):
        window = pext[pl.ds(pl.multiple_of(i * pitch, 8), pitch), :]
        dst = pl.ds(pl.multiple_of(i * span, 8), span)
        shifted[0, dst, :] = window[7 : 7 + span]
        shifted[1, dst, :] = window[8 : 8 + span]
        shifted[2, dst, :] = window[9 : 9 + span]
        return carry

    def depthwise(i, w0, size):
        res = []
        for grp in range(3):
            lanes = pl.ds(grp * width, width)
            acc = bb[0:size, lanes]
            for a in range(3):
                src = pl.ds(pl.multiple_of((i + a) * span, 8) + w0, size)
                for b in range(3):
                    acc = acc + shifted[b, src, lanes] * kb[a * 3 + b, 0:size, lanes]
            res.append(acc.astype(jnp.bfloat16).astype(jnp.float32))
        qf[pl.ds(pl.multiple_of(i * span, 8) + w0, size), :] = res[0]
        ext[rows + i, pl.ds(w0, size), :] = (
            (res[1] * res[2]).astype(jnp.bfloat16).astype(jnp.float32))

    def inner_body(i, carry):
        depthwise(i, 8, span - 16)
        return carry

    def outer_body(i, carry):
        @pl.when(jnp.logical_and(r == 0, jnp.logical_and(i > 0, i % 8 == 0)))
        def _():
            edge_copy(i // 8 - 1, 0).start()
            edge_copy(i // 8 - 1, 1).start()

        depthwise(i, 0, 8)
        depthwise(i, span - 8, 8)
        return carry

    lane_groups = width // 128
    chunks = (span // 8) * lane_groups

    def own_pass(i, carry):
        lanes = pl.ds(pl.multiple_of((i % lane_groups) * 128, 128), 128)
        w0 = pl.multiple_of((i // lane_groups) * 8, 8)
        acc = [None] * rows
        for src in range(rows, 2 * rows):
            x = ext[src, pl.ds(w0, 8), lanes]
            for a in range(src - rows, rows):
                term = fb[rows + a - src, :, lanes] * x
                acc[a] = term if acc[a] is None else acc[a] + term
        for a in range(rows):
            gated[pl.ds(a * span + w0, 8), lanes] = acc[a]
        return carry

    def prev_pass(i, carry):
        lanes = pl.ds(pl.multiple_of((i % lane_groups) * 128, 128), 128)
        w0 = pl.multiple_of((i // lane_groups) * 8, 8)
        acc = [gated[pl.ds(a * span + w0, 8), lanes] for a in range(rows)]
        for src in range(rows):
            x = ext[src, pl.ds(w0, 8), lanes]
            for a in range(rows):
                acc[a] = acc[a] + fb[rows + a - src, :, lanes] * x
        gain = jnp.broadcast_to(gain_ref[lanes].reshape(1, 128), (8, 128))
        for a in range(rows):
            own = ext[rows + a, pl.ds(w0, 8), lanes]
            q = qf[pl.ds(a * span + w0, 8), lanes]
            gated[pl.ds(a * span + w0, 8), lanes] = q * (acc[a] + gain * own)
        return carry

    @pl.when(r == 0)
    def _():
        ext[0:rows] = jnp.zeros((rows, span, width), jnp.float32)

    lax.fori_loop(0, rows + 2, shift_body, 0)
    lax.fori_loop(0, rows, inner_body, 0)

    @pl.when(r == 0)
    def _():
        product_copies[0].start()

    lax.fori_loop(lane_groups, chunks - lane_groups, own_pass, 0)

    @pl.when(r == 1)
    def _():
        product_copies[0].wait_recv()

    lax.fori_loop(lane_groups, chunks - lane_groups, prev_pass, 0)

    @pl.when(r == 0)
    def _():
        product_copies[0].wait_send()

    for cp, cond in zip(copies[:4], send_when[:4]):
        guarded(cond, cp.wait_send)
    for cp, cond in zip(copies[:4], recv_when[:4]):
        guarded(cond, cp.wait_recv)
    stage[0] = recv_col[0].astype(jnp.float32)
    stage[1] = recv_col[1].astype(jnp.float32)
    for i in range(rows):
        pext[pl.ds((1 + i) * pitch + 7, 1), :] = stage[0, i : i + 1, :]
        pext[pl.ds((1 + i) * pitch + 8 + span, 1), :] = stage[1, i : i + 1, :]
    pext[pl.ds(halo_base + 7, 1), :] = recv_cor[0, 0:1, :].astype(jnp.float32)
    pext[pl.ds(halo_base + 8 + span, 1), :] = recv_cor[1, 0:1, :].astype(jnp.float32)
    lax.fori_loop(0, rows + 2, shift_body, 0)
    lax.fori_loop(0, rows, outer_body, 0)

    @pl.when(r == 0)
    def _():
        edge_copy(pieces - 1, 0).start()
        edge_copy(pieces - 1, 1).start()

    lax.fori_loop(0, lane_groups, own_pass, 0)
    lax.fori_loop(chunks - lane_groups, chunks, own_pass, 0)

    @pl.when(r == 1)
    def _():
        for k in range(pieces):
            edge_copy(k, 0).wait_recv()
            edge_copy(k, 1).wait_recv()

    lax.fori_loop(0, lane_groups, prev_pass, 0)
    lax.fori_loop(chunks - lane_groups, chunks, prev_pass, 0)

    @pl.when(r == 0)
    def _():
        for k in range(pieces):
            edge_copy(k, 0).wait_send()
            edge_copy(k, 1).wait_send()
    out_ref[...] = gated[...].astype(out_ref.dtype)


def on_device(image_tokens, w_in, conv_kernel, conv_bias, long_filter, skip_gain, w_out):
    row_count, col_count, width = image_tokens.shape
    pitch = 48
    flat = row_count * col_count
    wide = w_in.shape[1]
    vmem = pl.BlockSpec(memory_space=pltpu.VMEM)
    out = pl.pallas_call(
        functools.partial(layer_kernel, row_count, col_count, pitch),
        out_shape=jax.ShapeDtypeStruct((flat, width), jnp.bfloat16),
        in_specs=[pl.BlockSpec(memory_space=pl.ANY)] * 7,
        out_specs=vmem,
        scratch_shapes=[
            pltpu.VMEM((flat, width), jnp.bfloat16),
            pltpu.VMEM(w_in.shape, jnp.bfloat16),
            pltpu.VMEM(conv_kernel.shape, jnp.bfloat16),
            pltpu.VMEM(conv_bias.shape, jnp.float32),
            pltpu.VMEM(long_filter.shape, jnp.bfloat16),
            pltpu.VMEM(skip_gain.shape, jnp.float32),
            pltpu.VMEM(w_out.shape, jnp.bfloat16),
            pltpu.SemaphoreType.DMA((7,)),
            pltpu.VMEM(((row_count + 2) * pitch, wide), jnp.float32),
            pltpu.VMEM((3, (row_count + 2) * col_count, wide), jnp.float32),
            pltpu.VMEM((9, col_count, wide), jnp.float32),
            pltpu.VMEM((col_count, wide), jnp.float32),
            pltpu.VMEM((2, row_count, wide), jnp.bfloat16),
            pltpu.VMEM((2, row_count, wide), jnp.bfloat16),
            pltpu.VMEM((col_count, wide), jnp.bfloat16),
            pltpu.VMEM((2, row_count, wide), jnp.float32),
            pltpu.VMEM((col_count, wide), jnp.bfloat16),
            pltpu.VMEM((2, 16, wide), jnp.bfloat16),
            pltpu.VMEM((2, 16, wide), jnp.bfloat16),
            pltpu.VMEM((2 * row_count, col_count, width), jnp.float32),
            pltpu.VMEM((2 * row_count, 8, width), jnp.float32),
            pltpu.VMEM((flat, width), jnp.float32),
            pltpu.VMEM((flat, width), jnp.float32),
            pltpu.SemaphoreType.DMA((6 + 2 * (row_count // 8),)),
            pltpu.SemaphoreType.DMA((6 + 2 * (row_count // 8),)),
        ],
        compiler_params=pltpu.CompilerParams(
            collective_id=0, has_side_effects=True, vmem_limit_bytes=67043328
        ),
    )(
        image_tokens.reshape(flat, width),
        w_in,
        conv_kernel,
        conv_bias,
        long_filter,
        skip_gain,
        w_out,
    )
    out = jnp.dot(out, w_out, preferred_element_type=jnp.float32).astype(jnp.bfloat16)
    return out.reshape(row_count, col_count, width)


def solution(mesh):
    in_specs = (P("row", "col", None), P(), P(), P(), P(), P(), P())
    out_specs = P("row", "col", None)
    return jax.shard_map(
        on_device, mesh=mesh, in_specs=in_specs, out_specs=out_specs, check_vma=False
    )
```

```python
import functools

import jax
import jax.numpy as jnp
from jax import lax
from jax.experimental import pallas as pl
from jax.experimental.pallas import tpu as pltpu
from jax.sharding import PartitionSpec as P


def layer_kernel(rows, span, pitch, x_hbm, w_hbm, k_hbm, b_hbm, filt_hbm, gain_hbm, wout_hbm,
                 out_ref, x_ref, w_ref, k_ref, b_ref, filt_ref, gain_ref, wout_ref, load_sem, pext,
                 shifted, kb, bb, send_col, recv_col, recv_row, stage, send_row,
                 send_cor, recv_cor, ext, fb, qf, gated, send_sem, recv_sem):
    width = out_ref.shape[1]
    wide = w_ref.shape[1]
    count = rows * span
    r = lax.axis_index("row")
    c = lax.axis_index("col")
    ncol = lax.axis_size("col")
    partner = 1 - r
    edge = partner * (rows - 1)
    mesh_id = pl.DeviceIdType.MESH
    right = lax.rem(c + 1, ncol)
    left = lax.rem(c + ncol - 1, ncol)
    peers = ((r, right), (r, left), (partner, right), (partner, left), (partner, c), (partner, c))

    recv_col[...] = jnp.zeros_like(recv_col)
    recv_cor[...] = jnp.zeros_like(recv_cor)
    barrier = pltpu.get_barrier_semaphore()
    conds = (c < ncol - 1, c > 0, c < ncol - 1, c > 0)
    for dev, cond in zip(peers[:4], conds):
        @pl.when(cond)
        def _():
            pl.semaphore_signal(barrier, 1, device_id=dev, device_id_type=mesh_id)
    pl.semaphore_signal(barrier, 1, device_id=peers[4], device_id_type=mesh_id)
    has_left = (c + ncol - 1) // ncol
    has_right = (2 * ncol - 3 - c) // (ncol - 1)

    loads = [
        pltpu.make_async_copy(src, dst, load_sem.at[i])
        for i, (src, dst) in enumerate((
            (x_hbm, x_ref), (w_hbm, w_ref), (k_hbm, k_ref), (b_hbm, b_ref),
            (filt_hbm, filt_ref), (gain_hbm, gain_ref), (wout_hbm, wout_ref)))
    ]
    for cp in loads:
        cp.start()
    for cp in loads[:4]:
        cp.wait()
    for i in range(9):
        kb[i] = jnp.broadcast_to(
            k_ref[i // 3, i % 3 : i % 3 + 1, :].astype(jnp.float32), (span, wide))
    bb[...] = jnp.broadcast_to(b_ref[...].reshape(1, wide), (span, wide))
    proj = jnp.dot(x_ref[...], w_ref[...], preferred_element_type=jnp.float32)
    proj = proj.astype(jnp.bfloat16).astype(jnp.float32)
    for i in range(rows):
        pext[pl.ds((1 + i) * pitch + 8, span), :] = proj[i * span : (i + 1) * span]
    other_row = r * (rows + 1)
    pext[pl.ds(pl.multiple_of(other_row * pitch, 8), pitch), :] = jnp.zeros((pitch, wide),
                                                                            jnp.float32)
    for i in range(rows):
        stage[0, i : i + 1, :] = pext[pl.ds((1 + i) * pitch + 8 + span - 1, 1), :]
        stage[1, i : i + 1, :] = pext[pl.ds((1 + i) * pitch + 8, 1), :]
    send_col[0] = stage[0].astype(jnp.bfloat16)
    send_col[1] = stage[1].astype(jnp.bfloat16)
    edge_base = pl.multiple_of((1 + edge) * pitch, 8)
    send_row[...] = pext[pl.ds(edge_base + 8, span), :].astype(jnp.bfloat16)
    corner_rows = send_cor.shape[1]
    send_cor[0] = jnp.broadcast_to(pext[pl.ds(edge_base + 8 + span - 1, 1), :],
                                   (corner_rows, wide)).astype(jnp.bfloat16)
    send_cor[1] = jnp.broadcast_to(pext[pl.ds(edge_base + 8, 1), :],
                                   (corner_rows, wide)).astype(jnp.bfloat16)

    pl.semaphore_wait(barrier, 1 + 2 * has_left + 2 * has_right)
    pairs = ((send_col.at[0], recv_col.at[0]), (send_col.at[1], recv_col.at[1]),
             (send_cor.at[0], recv_cor.at[0]), (send_cor.at[1], recv_cor.at[1]),
             (send_row, recv_row))
    copies = [
        pltpu.make_async_remote_copy(src_ref, dst_ref, send_sem.at[slot], recv_sem.at[slot],
                                     device_id=peers[slot], device_id_type=mesh_id)
        for slot, (src_ref, dst_ref) in enumerate(pairs)
    ]
    pieces = rows // 8

    def inner_copy(k):
        return pltpu.make_async_remote_copy(
            ext.at[pl.ds(rows + 8 * k, 8), pl.ds(8, span - 16), :],
            ext.at[pl.ds(8 * k, 8), pl.ds(8, span - 16), :],
            send_sem.at[5 + 3 * k], recv_sem.at[5 + 3 * k], device_id=peers[5],
            device_id_type=mesh_id)

    def edge_copy(k, side):
        w0 = side * (span - 8)
        slot = 6 + 3 * k + side
        return pltpu.make_async_remote_copy(
            ext.at[pl.ds(rows + 8 * k, 8), pl.ds(w0, 8), :],
            ext.at[pl.ds(8 * k, 8), pl.ds(w0, 8), :],
            send_sem.at[slot], recv_sem.at[slot], device_id=peers[5], device_id_type=mesh_id)
    send_when = (c < ncol - 1, c > 0, c < ncol - 1, c > 0, None)
    recv_when = (c > 0, c < ncol - 1, c > 0, c < ncol - 1, None)

    def guarded(cond, fn):
        if cond is None:
            fn()
        else:
            pl.when(cond)(fn)

    for cp, cond in zip(copies, send_when):
        guarded(cond, cp.start)
    for cp in loads[4:]:
        cp.wait()
    for lag in range(2 * rows):
        fb[lag] = jnp.broadcast_to(filt_ref[lag : lag + 1, :].astype(jnp.float32), (8, width))
    copies[4].wait_send()
    copies[4].wait_recv()
    halo_base = pl.multiple_of(partner * (rows + 1) * pitch, 8)
    pext[pl.ds(halo_base + 8, span), :] = recv_row[...].astype(jnp.float32)

    def shift_body(i, carry):
        window = pext[pl.ds(pl.multiple_of(i * pitch, 8), pitch), :]
        dst = pl.ds(pl.multiple_of(i * span, 8), span)
        shifted[0, dst, :] = window[7 : 7 + span]
        shifted[1, dst, :] = window[8 : 8 + span]
        shifted[2, dst, :] = window[9 : 9 + span]
        return carry

    def depthwise(i, w0, size):
        res = []
        for grp in range(3):
            lanes = pl.ds(grp * width, width)
            acc = bb[0:size, lanes]
            for a in range(3):
                src = pl.ds(pl.multiple_of((i + a) * span, 8) + w0, size)
                for b in range(3):
                    acc = acc + shifted[b, src, lanes] * kb[a * 3 + b, 0:size, lanes]
            res.append(acc.astype(jnp.bfloat16).astype(jnp.float32))
        qf[pl.ds(pl.multiple_of(i * span, 8) + w0, size), :] = res[0]
        ext[rows + i, pl.ds(w0, size), :] = (
            (res[1] * res[2]).astype(jnp.bfloat16).astype(jnp.float32))

    def inner_body(i, carry):
        @pl.when(jnp.logical_and(r == 0, jnp.logical_and(i > 0, i % 8 == 0)))
        def _():
            inner_copy(i // 8 - 1).start()

        depthwise(i, 8, span - 16)
        return carry

    def outer_body(i, carry):
        @pl.when(jnp.logical_and(r == 0, jnp.logical_and(i > 0, i % 8 == 0)))
        def _():
            edge_copy(i // 8 - 1, 0).start()
            edge_copy(i // 8 - 1, 1).start()

        depthwise(i, 0, 8)
        depthwise(i, span - 8, 8)
        return carry

    lane_groups = width // 128
    chunks = (span // 8) * lane_groups

    def own_pass(i, carry):
        lanes = pl.ds(pl.multiple_of((i % lane_groups) * 128, 128), 128)
        w0 = pl.multiple_of((i // lane_groups) * 8, 8)
        acc = [None] * rows
        for src in range(rows, 2 * rows):
            x = ext[src, pl.ds(w0, 8), lanes]
            for a in range(src - rows, rows):
                term = fb[rows + a - src, :, lanes] * x
                acc[a] = term if acc[a] is None else acc[a] + term
        for a in range(rows):
            gated[pl.ds(a * span + w0, 8), lanes] = acc[a]
        return carry

    def prev_pass(i, carry):
        lanes = pl.ds(pl.multiple_of((i % lane_groups) * 128, 128), 128)
        w0 = pl.multiple_of((i // lane_groups) * 8, 8)
        acc = [gated[pl.ds(a * span + w0, 8), lanes] for a in range(rows)]
        for src in range(rows):
            x = ext[src, pl.ds(w0, 8), lanes]
            for a in range(rows):
                acc[a] = acc[a] + fb[rows + a - src, :, lanes] * x
        gain = jnp.broadcast_to(gain_ref[lanes].reshape(1, 128), (8, 128))
        for a in range(rows):
            own = ext[rows + a, pl.ds(w0, 8), lanes]
            q = qf[pl.ds(a * span + w0, 8), lanes]
            gated[pl.ds(a * span + w0, 8), lanes] = q * (acc[a] + gain * own)
        return carry

    @pl.when(r == 0)
    def _():
        ext[0:rows] = jnp.zeros((rows, span, width), jnp.float32)

    lax.fori_loop(0, rows + 2, shift_body, 0)
    lax.fori_loop(0, rows, inner_body, 0)

    @pl.when(r == 0)
    def _():
        inner_copy(pieces - 1).start()

    lax.fori_loop(lane_groups, chunks - lane_groups, own_pass, 0)

    @pl.when(r == 1)
    def _():
        for k in range(pieces):
            inner_copy(k).wait_recv()

    lax.fori_loop(lane_groups, chunks - lane_groups, prev_pass, 0)

    @pl.when(r == 0)
    def _():
        for k in range(pieces):
            inner_copy(k).wait_send()

    for cp, cond in zip(copies[:4], send_when[:4]):
        guarded(cond, cp.wait_send)
    for cp, cond in zip(copies[:4], recv_when[:4]):
        guarded(cond, cp.wait_recv)
    stage[0] = recv_col[0].astype(jnp.float32)
    stage[1] = recv_col[1].astype(jnp.float32)
    for i in range(rows):
        pext[pl.ds((1 + i) * pitch + 7, 1), :] = stage[0, i : i + 1, :]
        pext[pl.ds((1 + i) * pitch + 8 + span, 1), :] = stage[1, i : i + 1, :]
    pext[pl.ds(halo_base + 7, 1), :] = recv_cor[0, 0:1, :].astype(jnp.float32)
    pext[pl.ds(halo_base + 8 + span, 1), :] = recv_cor[1, 0:1, :].astype(jnp.float32)
    lax.fori_loop(0, rows + 2, shift_body, 0)
    lax.fori_loop(0, rows, outer_body, 0)

    @pl.when(r == 0)
    def _():
        edge_copy(pieces - 1, 0).start()
        edge_copy(pieces - 1, 1).start()

    lax.fori_loop(0, lane_groups, own_pass, 0)
    lax.fori_loop(chunks - lane_groups, chunks, own_pass, 0)

    @pl.when(r == 1)
    def _():
        for k in range(pieces):
            edge_copy(k, 0).wait_recv()
            edge_copy(k, 1).wait_recv()

    lax.fori_loop(0, lane_groups, prev_pass, 0)
    lax.fori_loop(chunks - lane_groups, chunks, prev_pass, 0)

    @pl.when(r == 0)
    def _():
        for k in range(pieces):
            edge_copy(k, 0).wait_send()
            edge_copy(k, 1).wait_send()
    out_ref[...] = gated[...].astype(out_ref.dtype)


def on_device(image_tokens, w_in, conv_kernel, conv_bias, long_filter, skip_gain, w_out):
    row_count, col_count, width = image_tokens.shape
    pitch = 48
    flat = row_count * col_count
    wide = w_in.shape[1]
    vmem = pl.BlockSpec(memory_space=pltpu.VMEM)
    out = pl.pallas_call(
        functools.partial(layer_kernel, row_count, col_count, pitch),
        out_shape=jax.ShapeDtypeStruct((flat, width), jnp.bfloat16),
        in_specs=[pl.BlockSpec(memory_space=pl.ANY)] * 7,
        out_specs=vmem,
        scratch_shapes=[
            pltpu.VMEM((flat, width), jnp.bfloat16),
            pltpu.VMEM(w_in.shape, jnp.bfloat16),
            pltpu.VMEM(conv_kernel.shape, jnp.bfloat16),
            pltpu.VMEM(conv_bias.shape, jnp.float32),
            pltpu.VMEM(long_filter.shape, jnp.bfloat16),
            pltpu.VMEM(skip_gain.shape, jnp.float32),
            pltpu.VMEM(w_out.shape, jnp.bfloat16),
            pltpu.SemaphoreType.DMA((7,)),
            pltpu.VMEM(((row_count + 2) * pitch, wide), jnp.float32),
            pltpu.VMEM((3, (row_count + 2) * col_count, wide), jnp.float32),
            pltpu.VMEM((9, col_count, wide), jnp.float32),
            pltpu.VMEM((col_count, wide), jnp.float32),
            pltpu.VMEM((2, row_count, wide), jnp.bfloat16),
            pltpu.VMEM((2, row_count, wide), jnp.bfloat16),
            pltpu.VMEM((col_count, wide), jnp.bfloat16),
            pltpu.VMEM((2, row_count, wide), jnp.float32),
            pltpu.VMEM((col_count, wide), jnp.bfloat16),
            pltpu.VMEM((2, 16, wide), jnp.bfloat16),
            pltpu.VMEM((2, 16, wide), jnp.bfloat16),
            pltpu.VMEM((2 * row_count, col_count, width), jnp.float32),
            pltpu.VMEM((2 * row_count, 8, width), jnp.float32),
            pltpu.VMEM((flat, width), jnp.float32),
            pltpu.VMEM((flat, width), jnp.float32),
            pltpu.SemaphoreType.DMA((5 + 3 * (row_count // 8),)),
            pltpu.SemaphoreType.DMA((5 + 3 * (row_count // 8),)),
        ],
        compiler_params=pltpu.CompilerParams(
            collective_id=0, has_side_effects=True, vmem_limit_bytes=67043328
        ),
    )(
        image_tokens.reshape(flat, width),
        w_in,
        conv_kernel,
        conv_bias,
        long_filter,
        skip_gain,
        w_out,
    )
    out = jnp.dot(out, w_out, preferred_element_type=jnp.float32).astype(jnp.bfloat16)
    return out.reshape(row_count, col_count, width)


def solution(mesh):
    in_specs = (P("row", "col", None), P(), P(), P(), P(), P(), P())
    out_specs = P("row", "col", None)
    return jax.shard_map(
        on_device, mesh=mesh, in_specs=in_specs, out_specs=out_specs, check_vma=False
    )
```

```python
import functools

import jax
import jax.numpy as jnp
from jax import lax
from jax.experimental import pallas as pl
from jax.experimental.pallas import tpu as pltpu
from jax.sharding import PartitionSpec as P


def layer_kernel(rows, span, pitch, x_hbm, w_hbm, k_hbm, b_hbm, filt_hbm, gain_hbm, wout_hbm,
                 out_ref, x_ref, w_ref, k_ref, b_ref, filt_ref, gain_ref, wout_ref, load_sem, pext,
                 shifted, kb, bb, send_col, recv_col, recv_row, stage, send_row,
                 send_cor, recv_cor, ext, fb, qf, gated, send_sem, recv_sem):
    width = out_ref.shape[1]
    wide = w_ref.shape[1]
    count = rows * span
    r = lax.axis_index("row")
    c = lax.axis_index("col")
    ncol = lax.axis_size("col")
    partner = 1 - r
    edge = partner * (rows - 1)
    mesh_id = pl.DeviceIdType.MESH
    right = lax.rem(c + 1, ncol)
    left = lax.rem(c + ncol - 1, ncol)
    peers = ((r, right), (r, left), (partner, right), (partner, left), (partner, c), (partner, c))

    recv_col[...] = jnp.zeros_like(recv_col)
    recv_cor[...] = jnp.zeros_like(recv_cor)
    barrier = pltpu.get_barrier_semaphore()
    conds = (c < ncol - 1, c > 0, c < ncol - 1, c > 0)
    for dev, cond in zip(peers[:4], conds):
        @pl.when(cond)
        def _():
            pl.semaphore_signal(barrier, 1, device_id=dev, device_id_type=mesh_id)
    pl.semaphore_signal(barrier, 1, device_id=peers[4], device_id_type=mesh_id)
    has_left = (c + ncol - 1) // ncol
    has_right = (2 * ncol - 3 - c) // (ncol - 1)

    loads = [
        pltpu.make_async_copy(src, dst, load_sem.at[i])
        for i, (src, dst) in enumerate((
            (x_hbm, x_ref), (w_hbm, w_ref), (k_hbm, k_ref), (b_hbm, b_ref),
            (filt_hbm, filt_ref), (gain_hbm, gain_ref), (wout_hbm, wout_ref)))
    ]
    for cp in loads:
        cp.start()
    for cp in loads[:4]:
        cp.wait()
    for i in range(9):
        kb[i] = jnp.broadcast_to(
            k_ref[i // 3, i % 3 : i % 3 + 1, :].astype(jnp.float32), (span, wide))
    bb[...] = jnp.broadcast_to(b_ref[...].reshape(1, wide), (span, wide))
    proj = jnp.dot(x_ref[...], w_ref[...], preferred_element_type=jnp.float32)
    proj = proj.astype(jnp.bfloat16).astype(jnp.float32)
    for i in range(rows):
        pext[pl.ds((1 + i) * pitch + 8, span), :] = proj[i * span : (i + 1) * span]
    other_row = r * (rows + 1)
    pext[pl.ds(pl.multiple_of(other_row * pitch, 8), pitch), :] = jnp.zeros((pitch, wide),
                                                                            jnp.float32)
    for i in range(rows):
        stage[0, i : i + 1, :] = pext[pl.ds((1 + i) * pitch + 8 + span - 1, 1), :]
        stage[1, i : i + 1, :] = pext[pl.ds((1 + i) * pitch + 8, 1), :]
    send_col[0] = stage[0].astype(jnp.bfloat16)
    send_col[1] = stage[1].astype(jnp.bfloat16)
    edge_base = pl.multiple_of((1 + edge) * pitch, 8)
    send_row[...] = pext[pl.ds(edge_base + 8, span), :].astype(jnp.bfloat16)
    corner_rows = send_cor.shape[1]
    send_cor[0] = jnp.broadcast_to(pext[pl.ds(edge_base + 8 + span - 1, 1), :],
                                   (corner_rows, wide)).astype(jnp.bfloat16)
    send_cor[1] = jnp.broadcast_to(pext[pl.ds(edge_base + 8, 1), :],
                                   (corner_rows, wide)).astype(jnp.bfloat16)

    pl.semaphore_wait(barrier, 1 + 2 * has_left + 2 * has_right)
    pairs = ((send_col.at[0], recv_col.at[0]), (send_col.at[1], recv_col.at[1]),
             (send_cor.at[0], recv_cor.at[0]), (send_cor.at[1], recv_cor.at[1]),
             (send_row, recv_row))
    copies = [
        pltpu.make_async_remote_copy(src_ref, dst_ref, send_sem.at[slot], recv_sem.at[slot],
                                     device_id=peers[slot], device_id_type=mesh_id)
        for slot, (src_ref, dst_ref) in enumerate(pairs)
    ]
    spans = ((8, span - 16), (0, 8), (span - 8, 8))
    product_copies = [
        pltpu.make_async_remote_copy(
            ext.at[pl.ds(rows, rows), pl.ds(w0, size), :],
            ext.at[pl.ds(0, rows), pl.ds(w0, size), :],
            send_sem.at[5 + k], recv_sem.at[5 + k], device_id=peers[5], device_id_type=mesh_id)
        for k, (w0, size) in enumerate(spans)
    ]
    send_when = (c < ncol - 1, c > 0, c < ncol - 1, c > 0, None)
    recv_when = (c > 0, c < ncol - 1, c > 0, c < ncol - 1, None)

    def guarded(cond, fn):
        if cond is None:
            fn()
        else:
            pl.when(cond)(fn)

    for cp, cond in zip(copies, send_when):
        guarded(cond, cp.start)
    for cp in loads[4:]:
        cp.wait()
    for lag in range(2 * rows):
        fb[lag] = jnp.broadcast_to(filt_ref[lag : lag + 1, :].astype(jnp.float32), (8, width))
    copies[4].wait_send()
    copies[4].wait_recv()
    halo_base = pl.multiple_of(partner * (rows + 1) * pitch, 8)
    pext[pl.ds(halo_base + 8, span), :] = recv_row[...].astype(jnp.float32)

    def shift_body(i, carry):
        window = pext[pl.ds(pl.multiple_of(i * pitch, 8), pitch), :]
        dst = pl.ds(pl.multiple_of(i * span, 8), span)
        shifted[0, dst, :] = window[7 : 7 + span]
        shifted[1, dst, :] = window[8 : 8 + span]
        shifted[2, dst, :] = window[9 : 9 + span]
        return carry

    def depthwise(i, w0, size):
        res = []
        for grp in range(3):
            lanes = pl.ds(grp * width, width)
            acc = bb[0:size, lanes]
            for a in range(3):
                src = pl.ds(pl.multiple_of((i + a) * span, 8) + w0, size)
                for b in range(3):
                    acc = acc + shifted[b, src, lanes] * kb[a * 3 + b, 0:size, lanes]
            res.append(acc.astype(jnp.bfloat16).astype(jnp.float32))
        qf[pl.ds(pl.multiple_of(i * span, 8) + w0, size), :] = res[0]
        ext[rows + i, pl.ds(w0, size), :] = (
            (res[1] * res[2]).astype(jnp.bfloat16).astype(jnp.float32))

    def inner_body(i, carry):
        depthwise(i, 8, span - 16)
        return carry

    def outer_body(i, carry):
        depthwise(i, 0, 8)
        depthwise(i, span - 8, 8)
        return carry

    lane_groups = width // 128
    chunks = (span // 8) * lane_groups

    def own_pass(i, carry):
        lanes = pl.ds(pl.multiple_of((i % lane_groups) * 128, 128), 128)
        w0 = pl.multiple_of((i // lane_groups) * 8, 8)
        acc = [None] * rows
        for src in range(rows, 2 * rows):
            x = ext[src, pl.ds(w0, 8), lanes]
            for a in range(src - rows, rows):
                term = fb[rows + a - src, :, lanes] * x
                acc[a] = term if acc[a] is None else acc[a] + term
        for a in range(rows):
            gated[pl.ds(a * span + w0, 8), lanes] = acc[a]
        return carry

    def prev_pass(i, carry):
        lanes = pl.ds(pl.multiple_of((i % lane_groups) * 128, 128), 128)
        w0 = pl.multiple_of((i // lane_groups) * 8, 8)
        acc = [gated[pl.ds(a * span + w0, 8), lanes] for a in range(rows)]
        for src in range(rows):
            x = ext[src, pl.ds(w0, 8), lanes]
            for a in range(rows):
                acc[a] = acc[a] + fb[rows + a - src, :, lanes] * x
        gain = jnp.broadcast_to(gain_ref[lanes].reshape(1, 128), (8, 128))
        for a in range(rows):
            own = ext[rows + a, pl.ds(w0, 8), lanes]
            q = qf[pl.ds(a * span + w0, 8), lanes]
            gated[pl.ds(a * span + w0, 8), lanes] = q * (acc[a] + gain * own)
        return carry

    @pl.when(r == 0)
    def _():
        ext[0:rows] = jnp.zeros((rows, span, width), jnp.float32)

    lax.fori_loop(0, rows + 2, shift_body, 0)
    lax.fori_loop(0, rows, inner_body, 0)

    @pl.when(r == 0)
    def _():
        product_copies[0].start()

    lax.fori_loop(lane_groups, chunks - lane_groups, own_pass, 0)

    @pl.when(r == 1)
    def _():
        product_copies[0].wait_recv()

    lax.fori_loop(lane_groups, chunks - lane_groups, prev_pass, 0)

    @pl.when(r == 0)
    def _():
        product_copies[0].wait_send()

    for cp, cond in zip(copies[:4], send_when[:4]):
        guarded(cond, cp.wait_send)
    for cp, cond in zip(copies[:4], recv_when[:4]):
        guarded(cond, cp.wait_recv)
    stage[0] = recv_col[0].astype(jnp.float32)
    stage[1] = recv_col[1].astype(jnp.float32)
    for i in range(rows):
        pext[pl.ds((1 + i) * pitch + 7, 1), :] = stage[0, i : i + 1, :]
        pext[pl.ds((1 + i) * pitch + 8 + span, 1), :] = stage[1, i : i + 1, :]
    pext[pl.ds(halo_base + 7, 1), :] = recv_cor[0, 0:1, :].astype(jnp.float32)
    pext[pl.ds(halo_base + 8 + span, 1), :] = recv_cor[1, 0:1, :].astype(jnp.float32)
    lax.fori_loop(0, rows + 2, shift_body, 0)
    lax.fori_loop(0, rows, outer_body, 0)

    @pl.when(r == 0)
    def _():
        product_copies[1].start()
        product_copies[2].start()

    lax.fori_loop(0, lane_groups, own_pass, 0)
    lax.fori_loop(chunks - lane_groups, chunks, own_pass, 0)

    @pl.when(r == 1)
    def _():
        product_copies[1].wait_recv()
        product_copies[2].wait_recv()

    lax.fori_loop(0, lane_groups, prev_pass, 0)
    lax.fori_loop(chunks - lane_groups, chunks, prev_pass, 0)

    @pl.when(r == 0)
    def _():
        for cp in product_copies[1:]:
            cp.wait_send()
    out_ref[...] = jnp.dot(
        gated[...].astype(jnp.bfloat16), wout_ref[...], preferred_element_type=jnp.float32)


def on_device(image_tokens, w_in, conv_kernel, conv_bias, long_filter, skip_gain, w_out):
    row_count, col_count, width = image_tokens.shape
    pitch = 48
    flat = row_count * col_count
    wide = w_in.shape[1]
    vmem = pl.BlockSpec(memory_space=pltpu.VMEM)
    out = pl.pallas_call(
        functools.partial(layer_kernel, row_count, col_count, pitch),
        out_shape=jax.ShapeDtypeStruct((flat, width), jnp.float32),
        in_specs=[pl.BlockSpec(memory_space=pl.ANY)] * 7,
        out_specs=vmem,
        scratch_shapes=[
            pltpu.VMEM((flat, width), jnp.bfloat16),
            pltpu.VMEM(w_in.shape, jnp.bfloat16),
            pltpu.VMEM(conv_kernel.shape, jnp.bfloat16),
            pltpu.VMEM(conv_bias.shape, jnp.float32),
            pltpu.VMEM(long_filter.shape, jnp.bfloat16),
            pltpu.VMEM(skip_gain.shape, jnp.float32),
            pltpu.VMEM(w_out.shape, jnp.bfloat16),
            pltpu.SemaphoreType.DMA((7,)),
            pltpu.VMEM(((row_count + 2) * pitch, wide), jnp.float32),
            pltpu.VMEM((3, (row_count + 2) * col_count, wide), jnp.float32),
            pltpu.VMEM((9, col_count, wide), jnp.float32),
            pltpu.VMEM((col_count, wide), jnp.float32),
            pltpu.VMEM((2, row_count, wide), jnp.bfloat16),
            pltpu.VMEM((2, row_count, wide), jnp.bfloat16),
            pltpu.VMEM((col_count, wide), jnp.bfloat16),
            pltpu.VMEM((2, row_count, wide), jnp.float32),
            pltpu.VMEM((col_count, wide), jnp.bfloat16),
            pltpu.VMEM((2, 16, wide), jnp.bfloat16),
            pltpu.VMEM((2, 16, wide), jnp.bfloat16),
            pltpu.VMEM((2 * row_count, col_count, width), jnp.float32),
            pltpu.VMEM((2 * row_count, 8, width), jnp.float32),
            pltpu.VMEM((flat, width), jnp.float32),
            pltpu.VMEM((flat, width), jnp.float32),
            pltpu.SemaphoreType.DMA((8,)),
            pltpu.SemaphoreType.DMA((8,)),
        ],
        compiler_params=pltpu.CompilerParams(
            collective_id=0, has_side_effects=True, vmem_limit_bytes=67043328
        ),
    )(
        image_tokens.reshape(flat, width),
        w_in,
        conv_kernel,
        conv_bias,
        long_filter,
        skip_gain,
        w_out,
    )
    out = out.astype(jnp.bfloat16)
    return out.reshape(row_count, col_count, width)


def solution(mesh):
    in_specs = (P("row", "col", None), P(), P(), P(), P(), P(), P())
    out_specs = P("row", "col", None)
    return jax.shard_map(
        on_device, mesh=mesh, in_specs=in_specs, out_specs=out_specs, check_vma=False
    )
```

```python
import functools

import jax
import jax.numpy as jnp
from jax import lax
from jax.experimental import pallas as pl
from jax.experimental.pallas import tpu as pltpu
from jax.sharding import PartitionSpec as P


def layer_kernel(rows, span, pitch, x_hbm, w_hbm, k_hbm, b_hbm, filt_hbm, gain_hbm, wout_hbm,
                 out_ref, x_ref, w_ref, k_ref, b_ref, filt_ref, gain_ref, wout_ref, load_sem, pext,
                 shifted, kb, bb, send_col, recv_col, recv_row, stage, send_row,
                 send_cor, recv_cor, ext, fb, qf, gated, send_sem, recv_sem):
    width = out_ref.shape[1]
    wide = w_ref.shape[1]
    count = rows * span
    r = lax.axis_index("row")
    c = lax.axis_index("col")
    ncol = lax.axis_size("col")
    partner = 1 - r
    edge = partner * (rows - 1)
    mesh_id = pl.DeviceIdType.MESH
    right = lax.rem(c + 1, ncol)
    left = lax.rem(c + ncol - 1, ncol)
    peers = ((r, right), (r, left), (partner, right), (partner, left), (partner, c), (partner, c))

    recv_col[...] = jnp.zeros_like(recv_col)
    recv_cor[...] = jnp.zeros_like(recv_cor)
    barrier = pltpu.get_barrier_semaphore()
    conds = (c < ncol - 1, c > 0, c < ncol - 1, c > 0)
    for dev, cond in zip(peers[:4], conds):
        @pl.when(cond)
        def _():
            pl.semaphore_signal(barrier, 1, device_id=dev, device_id_type=mesh_id)
    pl.semaphore_signal(barrier, 1, device_id=peers[4], device_id_type=mesh_id)
    has_left = (c + ncol - 1) // ncol
    has_right = (2 * ncol - 3 - c) // (ncol - 1)

    loads = [
        pltpu.make_async_copy(src, dst, load_sem.at[i])
        for i, (src, dst) in enumerate((
            (x_hbm, x_ref), (w_hbm, w_ref), (k_hbm, k_ref), (b_hbm, b_ref),
            (filt_hbm, filt_ref), (gain_hbm, gain_ref), (wout_hbm, wout_ref)))
    ]
    for cp in loads:
        cp.start()
    for cp in loads[:4]:
        cp.wait()
    proj = jnp.dot(x_ref[...], w_ref[...], preferred_element_type=jnp.float32)
    proj = proj.astype(jnp.bfloat16).astype(jnp.float32)
    for i in range(rows):
        pext[pl.ds((1 + i) * pitch + 8, span), :] = proj[i * span : (i + 1) * span]
    other_row = r * (rows + 1)
    pext[pl.ds(pl.multiple_of(other_row * pitch, 8), pitch), :] = jnp.zeros((pitch, wide),
                                                                            jnp.float32)
    for i in range(rows):
        stage[0, i : i + 1, :] = pext[pl.ds((1 + i) * pitch + 8 + span - 1, 1), :]
        stage[1, i : i + 1, :] = pext[pl.ds((1 + i) * pitch + 8, 1), :]
    send_col[0] = stage[0].astype(jnp.bfloat16)
    send_col[1] = stage[1].astype(jnp.bfloat16)
    edge_base = pl.multiple_of((1 + edge) * pitch, 8)
    send_row[...] = pext[pl.ds(edge_base + 8, span), :].astype(jnp.bfloat16)
    corner_rows = send_cor.shape[1]
    send_cor[0] = jnp.broadcast_to(pext[pl.ds(edge_base + 8 + span - 1, 1), :],
                                   (corner_rows, wide)).astype(jnp.bfloat16)
    send_cor[1] = jnp.broadcast_to(pext[pl.ds(edge_base + 8, 1), :],
                                   (corner_rows, wide)).astype(jnp.bfloat16)

    pl.semaphore_wait(barrier, 1 + 2 * has_left + 2 * has_right)
    pairs = ((send_col.at[0], recv_col.at[0]), (send_col.at[1], recv_col.at[1]),
             (send_cor.at[0], recv_cor.at[0]), (send_cor.at[1], recv_cor.at[1]),
             (send_row, recv_row))
    copies = [
        pltpu.make_async_remote_copy(src_ref, dst_ref, send_sem.at[slot], recv_sem.at[slot],
                                     device_id=peers[slot], device_id_type=mesh_id)
        for slot, (src_ref, dst_ref) in enumerate(pairs)
    ]
    spans = ((8, span - 16), (0, 8), (span - 8, 8))
    product_copies = [
        pltpu.make_async_remote_copy(
            ext.at[pl.ds(rows, rows), pl.ds(w0, size), :],
            ext.at[pl.ds(0, rows), pl.ds(w0, size), :],
            send_sem.at[5 + k], recv_sem.at[5 + k], device_id=peers[5], device_id_type=mesh_id)
        for k, (w0, size) in enumerate(spans)
    ]
    send_when = (c < ncol - 1, c > 0, c < ncol - 1, c > 0, None)
    recv_when = (c > 0, c < ncol - 1, c > 0, c < ncol - 1, None)

    def guarded(cond, fn):
        if cond is None:
            fn()
        else:
            pl.when(cond)(fn)

    for cp, cond in zip(copies, send_when):
        guarded(cond, cp.start)
    for i in range(9):
        kb[i] = jnp.broadcast_to(
            k_ref[i // 3, i % 3 : i % 3 + 1, :].astype(jnp.float32), (span, wide))
    bb[...] = jnp.broadcast_to(b_ref[...].reshape(1, wide), (span, wide))
    for cp in loads[4:]:
        cp.wait()
    for lag in range(2 * rows):
        fb[lag] = jnp.broadcast_to(filt_ref[lag : lag + 1, :].astype(jnp.float32), (8, width))
    copies[4].wait_send()
    copies[4].wait_recv()
    halo_base = pl.multiple_of(partner * (rows + 1) * pitch, 8)
    pext[pl.ds(halo_base + 8, span), :] = recv_row[...].astype(jnp.float32)

    def shift_body(i, carry):
        window = pext[pl.ds(pl.multiple_of(i * pitch, 8), pitch), :]
        dst = pl.ds(pl.multiple_of(i * span, 8), span)
        shifted[0, dst, :] = window[7 : 7 + span]
        shifted[1, dst, :] = window[8 : 8 + span]
        shifted[2, dst, :] = window[9 : 9 + span]
        return carry

    def depthwise(i, w0, size):
        res = []
        for grp in range(3):
            lanes = pl.ds(grp * width, width)
            acc = bb[0:size, lanes]
            for a in range(3):
                src = pl.ds(pl.multiple_of((i + a) * span, 8) + w0, size)
                for b in range(3):
                    acc = acc + shifted[b, src, lanes] * kb[a * 3 + b, 0:size, lanes]
            res.append(acc.astype(jnp.bfloat16).astype(jnp.float32))
        qf[pl.ds(pl.multiple_of(i * span, 8) + w0, size), :] = res[0]
        ext[rows + i, pl.ds(w0, size), :] = (
            (res[1] * res[2]).astype(jnp.bfloat16).astype(jnp.float32))

    def inner_body(i, carry):
        depthwise(i, 8, span - 16)
        return carry

    def outer_body(i, carry):
        depthwise(i, 0, 8)
        depthwise(i, span - 8, 8)
        return carry

    lane_groups = width // 128
    chunks = (span // 8) * lane_groups

    def own_pass(i, carry):
        lanes = pl.ds(pl.multiple_of((i % lane_groups) * 128, 128), 128)
        w0 = pl.multiple_of((i // lane_groups) * 8, 8)
        acc = [None] * rows
        for src in range(rows, 2 * rows):
            x = ext[src, pl.ds(w0, 8), lanes]
            for a in range(src - rows, rows):
                term = fb[rows + a - src, :, lanes] * x
                acc[a] = term if acc[a] is None else acc[a] + term
        for a in range(rows):
            gated[pl.ds(a * span + w0, 8), lanes] = acc[a]
        return carry

    def prev_pass(i, carry):
        lanes = pl.ds(pl.multiple_of((i % lane_groups) * 128, 128), 128)
        w0 = pl.multiple_of((i // lane_groups) * 8, 8)
        acc = [gated[pl.ds(a * span + w0, 8), lanes] for a in range(rows)]
        for src in range(rows):
            x = ext[src, pl.ds(w0, 8), lanes]
            for a in range(rows):
                acc[a] = acc[a] + fb[rows + a - src, :, lanes] * x
        gain = jnp.broadcast_to(gain_ref[lanes].reshape(1, 128), (8, 128))
        for a in range(rows):
            own = ext[rows + a, pl.ds(w0, 8), lanes]
            q = qf[pl.ds(a * span + w0, 8), lanes]
            gated[pl.ds(a * span + w0, 8), lanes] = q * (acc[a] + gain * own)
        return carry

    @pl.when(r == 0)
    def _():
        ext[0:rows] = jnp.zeros((rows, span, width), jnp.float32)

    lax.fori_loop(0, rows + 2, shift_body, 0)
    lax.fori_loop(0, rows, inner_body, 0)

    @pl.when(r == 0)
    def _():
        product_copies[0].start()

    lax.fori_loop(lane_groups, chunks - lane_groups, own_pass, 0)

    @pl.when(r == 1)
    def _():
        product_copies[0].wait_recv()

    lax.fori_loop(lane_groups, chunks - lane_groups, prev_pass, 0)

    @pl.when(r == 0)
    def _():
        product_copies[0].wait_send()

    for cp, cond in zip(copies[:4], send_when[:4]):
        guarded(cond, cp.wait_send)
    for cp, cond in zip(copies[:4], recv_when[:4]):
        guarded(cond, cp.wait_recv)
    stage[0] = recv_col[0].astype(jnp.float32)
    stage[1] = recv_col[1].astype(jnp.float32)
    for i in range(rows):
        pext[pl.ds((1 + i) * pitch + 7, 1), :] = stage[0, i : i + 1, :]
        pext[pl.ds((1 + i) * pitch + 8 + span, 1), :] = stage[1, i : i + 1, :]
    pext[pl.ds(halo_base + 7, 1), :] = recv_cor[0, 0:1, :].astype(jnp.float32)
    pext[pl.ds(halo_base + 8 + span, 1), :] = recv_cor[1, 0:1, :].astype(jnp.float32)
    lax.fori_loop(0, rows + 2, shift_body, 0)
    lax.fori_loop(0, rows, outer_body, 0)

    @pl.when(r == 0)
    def _():
        product_copies[1].start()
        product_copies[2].start()

    lax.fori_loop(0, lane_groups, own_pass, 0)
    lax.fori_loop(chunks - lane_groups, chunks, own_pass, 0)

    @pl.when(r == 1)
    def _():
        product_copies[1].wait_recv()
        product_copies[2].wait_recv()

    lax.fori_loop(0, lane_groups, prev_pass, 0)
    lax.fori_loop(chunks - lane_groups, chunks, prev_pass, 0)

    @pl.when(r == 0)
    def _():
        for cp in product_copies[1:]:
            cp.wait_send()
    out_ref[...] = gated[...].astype(out_ref.dtype)


def on_device(image_tokens, w_in, conv_kernel, conv_bias, long_filter, skip_gain, w_out):
    row_count, col_count, width = image_tokens.shape
    pitch = 48
    flat = row_count * col_count
    wide = w_in.shape[1]
    vmem = pl.BlockSpec(memory_space=pltpu.VMEM)
    out = pl.pallas_call(
        functools.partial(layer_kernel, row_count, col_count, pitch),
        out_shape=jax.ShapeDtypeStruct((flat, width), jnp.bfloat16),
        in_specs=[pl.BlockSpec(memory_space=pl.ANY)] * 7,
        out_specs=vmem,
        scratch_shapes=[
            pltpu.VMEM((flat, width), jnp.bfloat16),
            pltpu.VMEM(w_in.shape, jnp.bfloat16),
            pltpu.VMEM(conv_kernel.shape, jnp.bfloat16),
            pltpu.VMEM(conv_bias.shape, jnp.float32),
            pltpu.VMEM(long_filter.shape, jnp.bfloat16),
            pltpu.VMEM(skip_gain.shape, jnp.float32),
            pltpu.VMEM(w_out.shape, jnp.bfloat16),
            pltpu.SemaphoreType.DMA((7,)),
            pltpu.VMEM(((row_count + 2) * pitch, wide), jnp.float32),
            pltpu.VMEM((3, (row_count + 2) * col_count, wide), jnp.float32),
            pltpu.VMEM((9, col_count, wide), jnp.float32),
            pltpu.VMEM((col_count, wide), jnp.float32),
            pltpu.VMEM((2, row_count, wide), jnp.bfloat16),
            pltpu.VMEM((2, row_count, wide), jnp.bfloat16),
            pltpu.VMEM((col_count, wide), jnp.bfloat16),
            pltpu.VMEM((2, row_count, wide), jnp.float32),
            pltpu.VMEM((col_count, wide), jnp.bfloat16),
            pltpu.VMEM((2, 16, wide), jnp.bfloat16),
            pltpu.VMEM((2, 16, wide), jnp.bfloat16),
            pltpu.VMEM((2 * row_count, col_count, width), jnp.float32),
            pltpu.VMEM((2 * row_count, 8, width), jnp.float32),
            pltpu.VMEM((flat, width), jnp.float32),
            pltpu.VMEM((flat, width), jnp.float32),
            pltpu.SemaphoreType.DMA((8,)),
            pltpu.SemaphoreType.DMA((8,)),
        ],
        compiler_params=pltpu.CompilerParams(
            collective_id=0, has_side_effects=True, vmem_limit_bytes=67043328
        ),
    )(
        image_tokens.reshape(flat, width),
        w_in,
        conv_kernel,
        conv_bias,
        long_filter,
        skip_gain,
        w_out,
    )
    out = jnp.dot(out, w_out, preferred_element_type=jnp.float32).astype(jnp.bfloat16)
    return out.reshape(row_count, col_count, width)


def solution(mesh):
    in_specs = (P("row", "col", None), P(), P(), P(), P(), P(), P())
    out_specs = P("row", "col", None)
    return jax.shard_map(
        on_device, mesh=mesh, in_specs=in_specs, out_specs=out_specs, check_vma=False
    )
```

```python
import functools

import jax
import jax.numpy as jnp
from jax import lax
from jax.experimental import pallas as pl
from jax.experimental.pallas import tpu as pltpu
from jax.sharding import PartitionSpec as P


def layer_kernel(rows, span, pitch, x_hbm, w_hbm, k_hbm, b_hbm, filt_hbm, gain_hbm, wout_hbm,
                 out_ref, x_ref, w_ref, k_ref, b_ref, filt_ref, gain_ref, wout_ref, load_sem, pext,
                 shifted, kb, bb, send_col, recv_col, recv_row, stage, send_row,
                 send_cor, recv_cor, ext, fb, qf, gated, send_sem, recv_sem):
    width = out_ref.shape[1]
    wide = w_ref.shape[1]
    count = rows * span
    r = lax.axis_index("row")
    c = lax.axis_index("col")
    ncol = lax.axis_size("col")
    partner = 1 - r
    edge = partner * (rows - 1)
    mesh_id = pl.DeviceIdType.MESH
    right = lax.rem(c + 1, ncol)
    left = lax.rem(c + ncol - 1, ncol)
    peers = ((r, right), (r, left), (partner, right), (partner, left), (partner, c), (partner, c))

    recv_col[...] = jnp.zeros_like(recv_col)
    recv_cor[...] = jnp.zeros_like(recv_cor)
    barrier = pltpu.get_barrier_semaphore()
    conds = (c < ncol - 1, c > 0, c < ncol - 1, c > 0)
    for dev, cond in zip(peers[:4], conds):
        @pl.when(cond)
        def _():
            pl.semaphore_signal(barrier, 1, device_id=dev, device_id_type=mesh_id)
    pl.semaphore_signal(barrier, 1, device_id=peers[4], device_id_type=mesh_id)
    has_left = (c + ncol - 1) // ncol
    has_right = (2 * ncol - 3 - c) // (ncol - 1)

    loads = [
        pltpu.make_async_copy(src, dst, load_sem.at[i])
        for i, (src, dst) in enumerate((
            (x_hbm, x_ref), (w_hbm, w_ref), (k_hbm, k_ref), (b_hbm, b_ref),
            (filt_hbm, filt_ref), (gain_hbm, gain_ref), (wout_hbm, wout_ref)))
    ]
    for cp in loads:
        cp.start()
    for cp in loads[:4]:
        cp.wait()
    proj = jnp.dot(x_ref[...], w_ref[...], preferred_element_type=jnp.float32)
    proj = proj.astype(jnp.bfloat16).astype(jnp.float32)
    for i in range(rows):
        pext[pl.ds((1 + i) * pitch + 8, span), :] = proj[i * span : (i + 1) * span]
    other_row = r * (rows + 1)
    pext[pl.ds(pl.multiple_of(other_row * pitch, 8), pitch), :] = jnp.zeros((pitch, wide),
                                                                            jnp.float32)
    for i in range(rows):
        stage[0, i : i + 1, :] = pext[pl.ds((1 + i) * pitch + 8 + span - 1, 1), :]
        stage[1, i : i + 1, :] = pext[pl.ds((1 + i) * pitch + 8, 1), :]
    send_col[0] = stage[0].astype(jnp.bfloat16)
    send_col[1] = stage[1].astype(jnp.bfloat16)
    edge_base = pl.multiple_of((1 + edge) * pitch, 8)
    send_row[...] = pext[pl.ds(edge_base + 8, span), :].astype(jnp.bfloat16)
    corner_rows = send_cor.shape[1]
    send_cor[0] = jnp.broadcast_to(pext[pl.ds(edge_base + 8 + span - 1, 1), :],
                                   (corner_rows, wide)).astype(jnp.bfloat16)
    send_cor[1] = jnp.broadcast_to(pext[pl.ds(edge_base + 8, 1), :],
                                   (corner_rows, wide)).astype(jnp.bfloat16)

    pl.semaphore_wait(barrier, 1 + 2 * has_left + 2 * has_right)
    pairs = ((send_col.at[0], recv_col.at[0]), (send_col.at[1], recv_col.at[1]),
             (send_cor.at[0], recv_cor.at[0]), (send_cor.at[1], recv_cor.at[1]),
             (send_row, recv_row))
    copies = [
        pltpu.make_async_remote_copy(src_ref, dst_ref, send_sem.at[slot], recv_sem.at[slot],
                                     device_id=peers[slot], device_id_type=mesh_id)
        for slot, (src_ref, dst_ref) in enumerate(pairs)
    ]
    spans = ((8, span - 16), (0, 8), (span - 8, 8))
    product_copies = [
        pltpu.make_async_remote_copy(
            ext.at[pl.ds(rows, rows), pl.ds(w0, size), :],
            ext.at[pl.ds(0, rows), pl.ds(w0, size), :],
            send_sem.at[5 + k], recv_sem.at[5 + k], device_id=peers[5], device_id_type=mesh_id)
        for k, (w0, size) in enumerate(spans)
    ]
    send_when = (c < ncol - 1, c > 0, c < ncol - 1, c > 0, None)
    recv_when = (c > 0, c < ncol - 1, c > 0, c < ncol - 1, None)

    def guarded(cond, fn):
        if cond is None:
            fn()
        else:
            pl.when(cond)(fn)

    for cp, cond in zip(copies, send_when):
        guarded(cond, cp.start)
    for i in range(9):
        kb[i] = jnp.broadcast_to(
            k_ref[i // 3, i % 3 : i % 3 + 1, :].astype(jnp.float32), (span, wide))
    bb[...] = jnp.broadcast_to(b_ref[...].reshape(1, wide), (span, wide))
    for cp in loads[4:]:
        cp.wait()
    for lag in range(2 * rows):
        fb[lag] = jnp.broadcast_to(filt_ref[lag : lag + 1, :].astype(jnp.float32), (8, width))
    copies[4].wait_send()
    copies[4].wait_recv()
    halo_base = pl.multiple_of(partner * (rows + 1) * pitch, 8)
    pext[pl.ds(halo_base + 8, span), :] = recv_row[...].astype(jnp.float32)

    def shift_body(i, carry):
        window = pext[pl.ds(pl.multiple_of(i * pitch, 8), pitch), :]
        dst = pl.ds(pl.multiple_of(i * span, 8), span)
        shifted[0, dst, :] = window[7 : 7 + span]
        shifted[1, dst, :] = window[8 : 8 + span]
        shifted[2, dst, :] = window[9 : 9 + span]
        return carry

    def depthwise(i, w0, size):
        res = []
        for grp in range(3):
            lanes = pl.ds(grp * width, width)
            acc = bb[0:size, lanes]
            for a in range(3):
                src = pl.ds(pl.multiple_of((i + a) * span, 8) + w0, size)
                for b in range(3):
                    acc = acc + shifted[b, src, lanes] * kb[a * 3 + b, 0:size, lanes]
            res.append(acc.astype(jnp.bfloat16).astype(jnp.float32))
        qf[pl.ds(pl.multiple_of(i * span, 8) + w0, size), :] = res[0]
        ext[rows + i, pl.ds(w0, size), :] = (
            (res[1] * res[2]).astype(jnp.bfloat16).astype(jnp.float32))

    def inner_body(i, carry):
        depthwise(i, 8, span - 16)
        return carry

    def outer_body(i, carry):
        depthwise(i, 0, 8)
        depthwise(i, span - 8, 8)
        return carry

    lane_groups = width // 128
    chunks = (span // 8) * lane_groups

    def own_pass(i, carry):
        lanes = pl.ds(pl.multiple_of((i % lane_groups) * 128, 128), 128)
        w0 = pl.multiple_of((i // lane_groups) * 8, 8)
        acc = [None] * rows
        for src in range(rows, 2 * rows):
            x = ext[src, pl.ds(w0, 8), lanes]
            for a in range(src - rows, rows):
                term = fb[rows + a - src, :, lanes] * x
                acc[a] = term if acc[a] is None else acc[a] + term
        for a in range(rows):
            gated[pl.ds(a * span + w0, 8), lanes] = acc[a]
        return carry

    def prev_pass(i, carry):
        lanes = pl.ds(pl.multiple_of((i % lane_groups) * 128, 128), 128)
        w0 = pl.multiple_of((i // lane_groups) * 8, 8)
        acc = [gated[pl.ds(a * span + w0, 8), lanes] for a in range(rows)]
        for src in range(rows):
            x = ext[src, pl.ds(w0, 8), lanes]
            for a in range(rows):
                acc[a] = acc[a] + fb[rows + a - src, :, lanes] * x
        gain = jnp.broadcast_to(gain_ref[lanes].reshape(1, 128), (8, 128))
        for a in range(rows):
            own = ext[rows + a, pl.ds(w0, 8), lanes]
            q = qf[pl.ds(a * span + w0, 8), lanes]
            gated[pl.ds(a * span + w0, 8), lanes] = q * (acc[a] + gain * own)
        return carry

    @pl.when(r == 0)
    def _():
        ext[0:rows] = jnp.zeros((rows, span, width), jnp.float32)

    lax.fori_loop(0, rows + 2, shift_body, 0)
    lax.fori_loop(0, rows, inner_body, 0)

    @pl.when(r == 0)
    def _():
        product_copies[0].start()

    lax.fori_loop(lane_groups, chunks - lane_groups, own_pass, 0)

    @pl.when(r == 1)
    def _():
        product_copies[0].wait_recv()

    lax.fori_loop(lane_groups, chunks - lane_groups, prev_pass, 0)

    @pl.when(r == 0)
    def _():
        product_copies[0].wait_send()

    for cp, cond in zip(copies[:4], send_when[:4]):
        guarded(cond, cp.wait_send)
    for cp, cond in zip(copies[:4], recv_when[:4]):
        guarded(cond, cp.wait_recv)
    stage[0] = recv_col[0].astype(jnp.float32)
    stage[1] = recv_col[1].astype(jnp.float32)
    for i in range(rows):
        shifted[0, pl.ds((1 + i) * span, 1), :] = stage[0, i : i + 1, :]
        shifted[2, pl.ds((1 + i) * span + span - 1, 1), :] = stage[1, i : i + 1, :]
    halo_at = pl.multiple_of(partner * (rows + 1) * span, 8)
    shifted[0, pl.ds(halo_at, 1), :] = recv_cor[0, 0:1, :].astype(jnp.float32)
    shifted[2, pl.ds(halo_at + span - 1, 1), :] = recv_cor[1, 0:1, :].astype(jnp.float32)
    lax.fori_loop(0, rows, outer_body, 0)

    @pl.when(r == 0)
    def _():
        product_copies[1].start()
        product_copies[2].start()

    lax.fori_loop(0, lane_groups, own_pass, 0)
    lax.fori_loop(chunks - lane_groups, chunks, own_pass, 0)

    @pl.when(r == 1)
    def _():
        product_copies[1].wait_recv()
        product_copies[2].wait_recv()

    lax.fori_loop(0, lane_groups, prev_pass, 0)
    lax.fori_loop(chunks - lane_groups, chunks, prev_pass, 0)

    @pl.when(r == 0)
    def _():
        for cp in product_copies[1:]:
            cp.wait_send()
    out_ref[...] = gated[...].astype(out_ref.dtype)


def on_device(image_tokens, w_in, conv_kernel, conv_bias, long_filter, skip_gain, w_out):
    row_count, col_count, width = image_tokens.shape
    pitch = 48
    flat = row_count * col_count
    wide = w_in.shape[1]
    vmem = pl.BlockSpec(memory_space=pltpu.VMEM)
    out = pl.pallas_call(
        functools.partial(layer_kernel, row_count, col_count, pitch),
        out_shape=jax.ShapeDtypeStruct((flat, width), jnp.bfloat16),
        in_specs=[pl.BlockSpec(memory_space=pl.ANY)] * 7,
        out_specs=vmem,
        scratch_shapes=[
            pltpu.VMEM((flat, width), jnp.bfloat16),
            pltpu.VMEM(w_in.shape, jnp.bfloat16),
            pltpu.VMEM(conv_kernel.shape, jnp.bfloat16),
            pltpu.VMEM(conv_bias.shape, jnp.float32),
            pltpu.VMEM(long_filter.shape, jnp.bfloat16),
            pltpu.VMEM(skip_gain.shape, jnp.float32),
            pltpu.VMEM(w_out.shape, jnp.bfloat16),
            pltpu.SemaphoreType.DMA((7,)),
            pltpu.VMEM(((row_count + 2) * pitch, wide), jnp.float32),
            pltpu.VMEM((3, (row_count + 2) * col_count, wide), jnp.float32),
            pltpu.VMEM((9, col_count, wide), jnp.float32),
            pltpu.VMEM((col_count, wide), jnp.float32),
            pltpu.VMEM((2, row_count, wide), jnp.bfloat16),
            pltpu.VMEM((2, row_count, wide), jnp.bfloat16),
            pltpu.VMEM((col_count, wide), jnp.bfloat16),
            pltpu.VMEM((2, row_count, wide), jnp.float32),
            pltpu.VMEM((col_count, wide), jnp.bfloat16),
            pltpu.VMEM((2, 16, wide), jnp.bfloat16),
            pltpu.VMEM((2, 16, wide), jnp.bfloat16),
            pltpu.VMEM((2 * row_count, col_count, width), jnp.float32),
            pltpu.VMEM((2 * row_count, 8, width), jnp.float32),
            pltpu.VMEM((flat, width), jnp.float32),
            pltpu.VMEM((flat, width), jnp.float32),
            pltpu.SemaphoreType.DMA((8,)),
            pltpu.SemaphoreType.DMA((8,)),
        ],
        compiler_params=pltpu.CompilerParams(
            collective_id=0, has_side_effects=True, vmem_limit_bytes=67043328
        ),
    )(
        image_tokens.reshape(flat, width),
        w_in,
        conv_kernel,
        conv_bias,
        long_filter,
        skip_gain,
        w_out,
    )
    out = jnp.dot(out, w_out, preferred_element_type=jnp.float32).astype(jnp.bfloat16)
    return out.reshape(row_count, col_count, width)


def solution(mesh):
    in_specs = (P("row", "col", None), P(), P(), P(), P(), P(), P())
    out_specs = P("row", "col", None)
    return jax.shard_map(
        on_device, mesh=mesh, in_specs=in_specs, out_specs=out_specs, check_vma=False
    )
```

```python
import functools

import jax
import jax.numpy as jnp
from jax import lax
from jax.experimental import pallas as pl
from jax.experimental.pallas import tpu as pltpu
from jax.sharding import PartitionSpec as P


def layer_kernel(rows, span, pitch, x_hbm, w_hbm, k_hbm, b_hbm, filt_hbm, gain_hbm, wout_hbm,
                 out_ref, x_ref, w_ref, k_ref, b_ref, filt_ref, gain_ref, wout_ref, load_sem, pext,
                 shifted, kb, bb, send_col, recv_col, recv_row, stage, send_row,
                 send_cor, recv_cor, ext, fb, qf, gated, edge_acc, halo_only, send_sem,
                 recv_sem):
    width = out_ref.shape[1]
    wide = w_ref.shape[1]
    count = rows * span
    r = lax.axis_index("row")
    c = lax.axis_index("col")
    ncol = lax.axis_size("col")
    partner = 1 - r
    edge = partner * (rows - 1)
    mesh_id = pl.DeviceIdType.MESH
    right = lax.rem(c + 1, ncol)
    left = lax.rem(c + ncol - 1, ncol)
    peers = ((r, right), (r, left), (partner, right), (partner, left), (partner, c), (partner, c))

    recv_col[...] = jnp.zeros_like(recv_col)
    recv_cor[...] = jnp.zeros_like(recv_cor)
    barrier = pltpu.get_barrier_semaphore()
    conds = (c < ncol - 1, c > 0, c < ncol - 1, c > 0)
    for dev, cond in zip(peers[:4], conds):
        @pl.when(cond)
        def _():
            pl.semaphore_signal(barrier, 1, device_id=dev, device_id_type=mesh_id)
    pl.semaphore_signal(barrier, 1, device_id=peers[4], device_id_type=mesh_id)
    has_left = (c + ncol - 1) // ncol
    has_right = (2 * ncol - 3 - c) // (ncol - 1)

    loads = [
        pltpu.make_async_copy(src, dst, load_sem.at[i])
        for i, (src, dst) in enumerate((
            (x_hbm, x_ref), (w_hbm, w_ref), (k_hbm, k_ref), (b_hbm, b_ref),
            (filt_hbm, filt_ref), (gain_hbm, gain_ref), (wout_hbm, wout_ref)))
    ]
    for cp in loads:
        cp.start()
    for cp in loads[:4]:
        cp.wait()
    proj = jnp.dot(x_ref[...], w_ref[...], preferred_element_type=jnp.float32)
    proj = proj.astype(jnp.bfloat16).astype(jnp.float32)
    for i in range(rows):
        pext[pl.ds((1 + i) * pitch + 8, span), :] = proj[i * span : (i + 1) * span]
    other_row = r * (rows + 1)
    pext[pl.ds(pl.multiple_of(other_row * pitch, 8), pitch), :] = jnp.zeros((pitch, wide),
                                                                            jnp.float32)
    for i in range(rows):
        stage[0, i : i + 1, :] = pext[pl.ds((1 + i) * pitch + 8 + span - 1, 1), :]
        stage[1, i : i + 1, :] = pext[pl.ds((1 + i) * pitch + 8, 1), :]
    send_col[0] = stage[0].astype(jnp.bfloat16)
    send_col[1] = stage[1].astype(jnp.bfloat16)
    edge_base = pl.multiple_of((1 + edge) * pitch, 8)
    send_row[...] = pext[pl.ds(edge_base + 8, span), :].astype(jnp.bfloat16)
    corner_rows = send_cor.shape[1]
    send_cor[0] = jnp.broadcast_to(pext[pl.ds(edge_base + 8 + span - 1, 1), :],
                                   (corner_rows, wide)).astype(jnp.bfloat16)
    send_cor[1] = jnp.broadcast_to(pext[pl.ds(edge_base + 8, 1), :],
                                   (corner_rows, wide)).astype(jnp.bfloat16)

    pl.semaphore_wait(barrier, 1 + 2 * has_left + 2 * has_right)
    pairs = ((send_col.at[0], recv_col.at[0]), (send_col.at[1], recv_col.at[1]),
             (send_cor.at[0], recv_cor.at[0]), (send_cor.at[1], recv_cor.at[1]),
             (send_row, recv_row))
    copies = [
        pltpu.make_async_remote_copy(src_ref, dst_ref, send_sem.at[slot], recv_sem.at[slot],
                                     device_id=peers[slot], device_id_type=mesh_id)
        for slot, (src_ref, dst_ref) in enumerate(pairs)
    ]
    spans = ((8, span - 16), (0, 8), (span - 8, 8))
    product_copies = [
        pltpu.make_async_remote_copy(
            ext.at[pl.ds(rows, rows), pl.ds(w0, size), :],
            ext.at[pl.ds(0, rows), pl.ds(w0, size), :],
            send_sem.at[5 + k], recv_sem.at[5 + k], device_id=peers[5], device_id_type=mesh_id)
        for k, (w0, size) in enumerate(spans)
    ]
    send_when = (c < ncol - 1, c > 0, c < ncol - 1, c > 0, None)
    recv_when = (c > 0, c < ncol - 1, c > 0, c < ncol - 1, None)

    def guarded(cond, fn):
        if cond is None:
            fn()
        else:
            pl.when(cond)(fn)

    for cp, cond in zip(copies, send_when):
        guarded(cond, cp.start)
    for i in range(9):
        kb[i] = jnp.broadcast_to(
            k_ref[i // 3, i % 3 : i % 3 + 1, :].astype(jnp.float32), (span, wide))
    bb[...] = jnp.broadcast_to(b_ref[...].reshape(1, wide), (span, wide))
    for cp in loads[4:]:
        cp.wait()
    for lag in range(2 * rows):
        fb[lag] = jnp.broadcast_to(filt_ref[lag : lag + 1, :].astype(jnp.float32), (8, width))
    copies[4].wait_send()
    copies[4].wait_recv()
    halo_base = pl.multiple_of(partner * (rows + 1) * pitch, 8)
    pext[pl.ds(halo_base + 8, span), :] = recv_row[...].astype(jnp.float32)

    def shift_body(i, carry):
        window = pext[pl.ds(pl.multiple_of(i * pitch, 8), pitch), :]
        dst = pl.ds(pl.multiple_of(i * span, 8), span)
        shifted[0, dst, :] = window[7 : 7 + span]
        shifted[1, dst, :] = window[8 : 8 + span]
        shifted[2, dst, :] = window[9 : 9 + span]
        return carry

    def depthwise(i, w0, size):
        res = []
        for grp in range(3):
            lanes = pl.ds(grp * width, width)
            acc = bb[0:size, lanes]
            for a in range(3):
                src = pl.ds(pl.multiple_of((i + a) * span, 8) + w0, size)
                for b in range(3):
                    acc = acc + shifted[b, src, lanes] * kb[a * 3 + b, 0:size, lanes]
            res.append(acc.astype(jnp.bfloat16).astype(jnp.float32))
        qf[pl.ds(pl.multiple_of(i * span, 8) + w0, size), :] = res[0]
        ext[rows + i, pl.ds(w0, size), :] = (
            (res[1] * res[2]).astype(jnp.bfloat16).astype(jnp.float32))

    def inner_body(i, carry):
        depthwise(i, 8, span - 16)
        return carry

    def outer_body(i, carry):
        depthwise(i, 0, 8)
        depthwise(i, span - 8, 8)
        return carry

    lane_groups = width // 128
    chunks = (span // 8) * lane_groups

    def own_pass(i, carry):
        lanes = pl.ds(pl.multiple_of((i % lane_groups) * 128, 128), 128)
        w0 = pl.multiple_of((i // lane_groups) * 8, 8)
        acc = [None] * rows
        for src in range(rows, 2 * rows):
            x = ext[src, pl.ds(w0, 8), lanes]
            for a in range(src - rows, rows):
                term = fb[rows + a - src, :, lanes] * x
                acc[a] = term if acc[a] is None else acc[a] + term
        for a in range(rows):
            gated[pl.ds(a * span + w0, 8), lanes] = acc[a]
        return carry

    def prev_pass(i, carry):
        lanes = pl.ds(pl.multiple_of((i % lane_groups) * 128, 128), 128)
        w0 = pl.multiple_of((i // lane_groups) * 8, 8)
        acc = [gated[pl.ds(a * span + w0, 8), lanes] for a in range(rows)]
        for src in range(rows):
            x = ext[src, pl.ds(w0, 8), lanes]
            for a in range(rows):
                acc[a] = acc[a] + fb[rows + a - src, :, lanes] * x
        gain = jnp.broadcast_to(gain_ref[lanes].reshape(1, 128), (8, 128))
        for a in range(rows):
            own = ext[rows + a, pl.ds(w0, 8), lanes]
            q = qf[pl.ds(a * span + w0, 8), lanes]
            gated[pl.ds(a * span + w0, 8), lanes] = q * (acc[a] + gain * own)
        return carry

    @pl.when(r == 0)
    def _():
        ext[0:rows] = jnp.zeros((rows, span, width), jnp.float32)

    lax.fori_loop(0, rows + 2, shift_body, 0)
    lax.fori_loop(0, rows, inner_body, 0)

    @pl.when(r == 0)
    def _():
        product_copies[0].start()

    lax.fori_loop(lane_groups, chunks - lane_groups, own_pass, 0)

    @pl.when(r == 1)
    def _():
        product_copies[0].wait_recv()

    lax.fori_loop(lane_groups, chunks - lane_groups, prev_pass, 0)

    @pl.when(r == 0)
    def _():
        product_copies[0].wait_send()

    zero_row = jnp.zeros((1, wide), jnp.float32)
    for i in range(rows + 2):
        shifted[0, pl.ds(i * span, 1), :] = zero_row
        shifted[2, pl.ds(i * span + span - 1, 1), :] = zero_row
    halo_only[...] = jnp.zeros_like(halo_only)
    sides = ((0, 0, 0), (span - 8, 1, 2))

    def edge_partial(i, carry):
        for k, (w0, side, tap) in enumerate(sides):
            for grp in range(3):
                lanes = pl.ds(grp * width, width)
                acc = bb[0:8, lanes]
                for a in range(3):
                    src = pl.ds(pl.multiple_of((i + a) * span, 8) + w0, 8)
                    for b in range(3):
                        acc = acc + shifted[b, src, lanes] * kb[a * 3 + b, 0:8, lanes]
                edge_acc[i, pl.ds(8 * k, 8), lanes] = acc
        return carry

    lax.fori_loop(0, rows, edge_partial, 0)

    for cp, cond in zip(copies[:4], send_when[:4]):
        guarded(cond, cp.wait_send)
    for cp, cond in zip(copies[:4], recv_when[:4]):
        guarded(cond, cp.wait_recv)
    stage[0] = recv_col[0].astype(jnp.float32)
    stage[1] = recv_col[1].astype(jnp.float32)
    for i in range(rows):
        halo_only[0, 1 + i, 0:1, :] = stage[0, i : i + 1, :]
        halo_only[1, 1 + i, 7:8, :] = stage[1, i : i + 1, :]
    halo_row = partner * (rows + 1)
    halo_only[0, halo_row, 0:1, :] = recv_cor[0, 0:1, :].astype(jnp.float32)
    halo_only[1, halo_row, 7:8, :] = recv_cor[1, 0:1, :].astype(jnp.float32)

    def edge_final(i, carry):
        for k, (w0, side, tap) in enumerate(sides):
            res = []
            for grp in range(3):
                lanes = pl.ds(grp * width, width)
                acc = edge_acc[i, pl.ds(8 * k, 8), lanes]
                for a in range(3):
                    acc = acc + halo_only[side, i + a, :, lanes] * kb[a * 3 + tap, 0:8, lanes]
                res.append(acc.astype(jnp.bfloat16).astype(jnp.float32))
            qf[pl.ds(pl.multiple_of(i * span, 8) + w0, 8), :] = res[0]
            ext[rows + i, pl.ds(w0, 8), :] = (
                (res[1] * res[2]).astype(jnp.bfloat16).astype(jnp.float32))
        return carry

    lax.fori_loop(0, rows, edge_final, 0)

    @pl.when(r == 0)
    def _():
        product_copies[1].start()
        product_copies[2].start()

    lax.fori_loop(0, lane_groups, own_pass, 0)
    lax.fori_loop(chunks - lane_groups, chunks, own_pass, 0)

    @pl.when(r == 1)
    def _():
        product_copies[1].wait_recv()
        product_copies[2].wait_recv()

    lax.fori_loop(0, lane_groups, prev_pass, 0)
    lax.fori_loop(chunks - lane_groups, chunks, prev_pass, 0)

    @pl.when(r == 0)
    def _():
        for cp in product_copies[1:]:
            cp.wait_send()
    out_ref[...] = gated[...].astype(out_ref.dtype)


def on_device(image_tokens, w_in, conv_kernel, conv_bias, long_filter, skip_gain, w_out):
    row_count, col_count, width = image_tokens.shape
    pitch = 48
    flat = row_count * col_count
    wide = w_in.shape[1]
    vmem = pl.BlockSpec(memory_space=pltpu.VMEM)
    out = pl.pallas_call(
        functools.partial(layer_kernel, row_count, col_count, pitch),
        out_shape=jax.ShapeDtypeStruct((flat, width), jnp.bfloat16),
        in_specs=[pl.BlockSpec(memory_space=pl.ANY)] * 7,
        out_specs=vmem,
        scratch_shapes=[
            pltpu.VMEM((flat, width), jnp.bfloat16),
            pltpu.VMEM(w_in.shape, jnp.bfloat16),
            pltpu.VMEM(conv_kernel.shape, jnp.bfloat16),
            pltpu.VMEM(conv_bias.shape, jnp.float32),
            pltpu.VMEM(long_filter.shape, jnp.bfloat16),
            pltpu.VMEM(skip_gain.shape, jnp.float32),
            pltpu.VMEM(w_out.shape, jnp.bfloat16),
            pltpu.SemaphoreType.DMA((7,)),
            pltpu.VMEM(((row_count + 2) * pitch, wide), jnp.float32),
            pltpu.VMEM((3, (row_count + 2) * col_count, wide), jnp.float32),
            pltpu.VMEM((9, col_count, wide), jnp.float32),
            pltpu.VMEM((col_count, wide), jnp.float32),
            pltpu.VMEM((2, row_count, wide), jnp.bfloat16),
            pltpu.VMEM((2, row_count, wide), jnp.bfloat16),
            pltpu.VMEM((col_count, wide), jnp.bfloat16),
            pltpu.VMEM((2, row_count, wide), jnp.float32),
            pltpu.VMEM((col_count, wide), jnp.bfloat16),
            pltpu.VMEM((2, 16, wide), jnp.bfloat16),
            pltpu.VMEM((2, 16, wide), jnp.bfloat16),
            pltpu.VMEM((2 * row_count, col_count, width), jnp.float32),
            pltpu.VMEM((2 * row_count, 8, width), jnp.float32),
            pltpu.VMEM((flat, width), jnp.float32),
            pltpu.VMEM((flat, width), jnp.float32),
            pltpu.VMEM((row_count, 16, wide), jnp.float32),
            pltpu.VMEM((2, row_count + 2, 8, wide), jnp.float32),
            pltpu.SemaphoreType.DMA((8,)),
            pltpu.SemaphoreType.DMA((8,)),
        ],
        compiler_params=pltpu.CompilerParams(
            collective_id=0, has_side_effects=True, vmem_limit_bytes=67043328
        ),
    )(
        image_tokens.reshape(flat, width),
        w_in,
        conv_kernel,
        conv_bias,
        long_filter,
        skip_gain,
        w_out,
    )
    out = jnp.dot(out, w_out, preferred_element_type=jnp.float32).astype(jnp.bfloat16)
    return out.reshape(row_count, col_count, width)


def solution(mesh):
    in_specs = (P("row", "col", None), P(), P(), P(), P(), P(), P())
    out_specs = P("row", "col", None)
    return jax.shard_map(
        on_device, mesh=mesh, in_specs=in_specs, out_specs=out_specs, check_vma=False
    )
```
